128 devices in a mesh: lon: 32 (over x_lo, y, z), lat: 4 (over x_hi, core).
Axes of the slice: x: 4 (x_hi: 2, x_lo: 2; x = x_hi * 2 + x_lo), y: 4, z: 4, core: 2. Of those that a mesh axis runs over, the one named last changes fastest.
Arguments:
- ocean_state: bfloat16 [320, 1024, 128], P('lat', 'lon'), may hold values from -6 to 6
- land_sea: int32 [320, 1024], P('lat', 'lon'), may hold values 0 or 1
- kernel: bfloat16 [7, 7, 128], replicated, may hold values from -0.875 to 0.875
- conv_bias: float32 [128], replicated, may hold values from -3 to 3
- norm_gain: float32 [128], replicated, may hold values from 0.5 to 1.5
- norm_bias: float32 [128], replicated, may hold values from -3 to 3
- w_expand: bfloat16 [128, 512], replicated, may hold values from -0.5 to 0.5
- b_expand: float32 [512], replicated, may hold values from -3 to 3
- w_reduce: bfloat16 [512, 128], replicated, may hold values from -0.25 to 0.25
- b_reduce: float32 [128], replicated, may hold values from -3 to 3
- layer_scale: float32 [128], replicated, may hold values from 0.3 to 1
- cotangent: bfloat16 [320, 1024, 128], P('lat', 'lon'), may hold values from -6 to 6
Outputs:
- result: bfloat16 [320, 1024, 128], P('lat', 'lon')
- state_grad: bfloat16 [320, 1024, 128], P('lat', 'lon')
The draws below stay inside these ranges and needn't reach their ends.
All inputs are finite; a program needn't handle non-finite values. No bound on the sum of `land_sea` on one device may be relied on, other than what follows from the above.
Results may differ from the reference program's by a relative error of at most 0.0037.
Values may be sent and summed in bfloat16 or wider, within the bound.
A program may use at most 192 MiB of HBM per device.

```python
import math
import jax
import jax.numpy as jnp
from jax import lax

CHANS = 128
HIDDEN_SIZE = 512
NLAT = 320
NLON = 1024


def with_ends(values, rng, low, largest):
    dims = values.shape
    index_at = [jax.random.randint(jax.random.fold_in(rng, axis), (), 0, dims[axis]) for axis in range(len(dims))]
    values = values.at[tuple(index_at)].set(low)
    longest = dims.index(max(dims))
    index_at[longest] = (index_at[longest] + 1) % dims[longest]
    return values.at[tuple(index_at)].set(largest)


def level_of(own_key, dims, pieces, low, largest):
    def one(position, shards_of):
        draws = jax.random.uniform(jax.random.fold_in(jax.random.fold_in(own_key, 6), position), (shards_of,), jnp.float32, low / len(pieces), largest / len(pieces))
        return jnp.repeat(jnp.exp(draws), dims[position] // shards_of).reshape((-1,) + (1,) * (len(dims) - position - 1))

    level = one(*pieces[0])
    for cut in pieces[1:]:
        level = level * one(*cut)
    return level


def bell_draw(key, dims, scale, bound, split=(), held_as=jnp.bfloat16):
    entries = jax.random.normal(key, dims, jnp.float32) * scale
    if len(split) > 0:
        entries = level_of(key, dims, split, -0.22, 0.18) * entries
    return jnp.clip(entries, min=-bound, max=bound).astype(held_as)


def setup_inputs(seed: int = 0) -> dict:
    arg_keys = jax.random.split(jax.random.key(seed), 13)
    return {
        "ocean_state": bell_draw(arg_keys[0], (NLAT, NLON, CHANS), 1.0, 6.0, ((0, 4), (1, 32))),
        "land_sea": with_ends((jax.random.randint(arg_keys[1], (NLAT, NLON), 0, 4) < 3).astype(jnp.int32), jax.random.fold_in(arg_keys[1], 1), 0, 1),
        "kernel": bell_draw(arg_keys[2], (7, 7, CHANS), 49 ** -0.5, 0.875),
        "conv_bias": bell_draw(arg_keys[3], (CHANS,), 0.5, 3.0, (), jnp.float32),
        "norm_gain": jnp.clip(jax.random.uniform(arg_keys[4], (CHANS,), jnp.float32, 0.5, 1.5), 0.5, 1.5),
        "norm_bias": bell_draw(arg_keys[5], (CHANS,), 0.5, 3.0, (), jnp.float32),
        "w_expand": bell_draw(arg_keys[6], (CHANS, HIDDEN_SIZE), CHANS ** -0.5, 0.5),
        "b_expand": bell_draw(arg_keys[7], (HIDDEN_SIZE,), 0.5, 3.0, (), jnp.float32),
        "w_reduce": bell_draw(arg_keys[8], (HIDDEN_SIZE, CHANS), HIDDEN_SIZE ** -0.5, 0.25),
        "b_reduce": bell_draw(arg_keys[9], (CHANS,), 0.5, 3.0, (), jnp.float32),
        "layer_scale": jnp.clip(jnp.exp(jax.random.uniform(arg_keys[10], (CHANS,), jnp.float32, math.log(0.3), math.log(1.0))), 0.3, 1.0),
        "cotangent": bell_draw(arg_keys[11], (NLAT, NLON, CHANS), 1.0, 6.0, ((0, 4), (1, 32))),
    }


def gelu_value(values):
    return 0.5 * values * (1.0 + lax.erf(values * 0.7071067811865476))

def gelu_slope(values):
    cumulative = 0.5 * (1.0 + lax.erf(values * 0.7071067811865476))
    return cumulative + values * jnp.exp(-0.5 * values * values) * 0.3989422804014327

def fold_pad(plane_in):
    upper_rows = plane_in[::-1][:3][:, ::-1]
    lower_rows = jnp.zeros_like(plane_in[:3])
    stacked = jnp.concatenate([lower_rows, plane_in, upper_rows], 0)
    return jnp.concatenate([stacked[:, -3:], stacked, stacked[:, :3]], 1)

def depthwise(padded, kernel, conv_bias):
    out_rows = padded.shape[0] - 6
    out_cols = padded.shape[1] - 6
    summed = jnp.zeros((out_rows, out_cols, padded.shape[2]), jnp.float32) + conv_bias
    for row_tap in range(7):
        for col_tap in range(7):
            window = padded[row_tap:row_tap + out_rows, col_tap:col_tap + out_cols].astype(jnp.float32)
            summed = summed + kernel[row_tap, col_tap].astype(jnp.float32) * window
    return summed

def pointwise(conv_out, ocean_state, keep_mask, cotangent, norm_gain, norm_bias, w_expand, b_expand, w_reduce, b_reduce, layer_scale):
    row_mean = lax.optimization_barrier(jnp.mean(conv_out, axis=-1, keepdims=True))
    centered = conv_out - row_mean
    inv_std = lax.rsqrt(lax.optimization_barrier(jnp.mean(centered * centered, axis=-1, keepdims=True)) + 1e-06)
    normal_hat = centered * inv_std
    normed = (normal_hat * norm_gain + norm_bias).astype(jnp.bfloat16)
    hidden = jnp.dot(normed, w_expand, preferred_element_type=jnp.float32) + b_expand
    activated = gelu_value(hidden).astype(jnp.bfloat16)
    projected = jnp.dot(activated, w_reduce, preferred_element_type=jnp.float32) + b_reduce
    result = (keep_mask * (ocean_state.astype(jnp.float32) + layer_scale * projected)).astype(jnp.bfloat16)
    grad_out = (keep_mask * layer_scale * cotangent.astype(jnp.float32)).astype(jnp.bfloat16)
    grad_act = jnp.dot(grad_out, w_reduce.T, preferred_element_type=jnp.float32)
    grad_hidden = (grad_act * gelu_slope(hidden)).astype(jnp.bfloat16)
    grad_normed = jnp.dot(grad_hidden, w_expand.T, preferred_element_type=jnp.float32)
    grad_scaled = grad_normed * norm_gain
    conv_grad = inv_std * (grad_scaled - lax.optimization_barrier(jnp.mean(grad_scaled, axis=-1, keepdims=True)) - normal_hat * lax.optimization_barrier(jnp.mean(grad_scaled * normal_hat, axis=-1, keepdims=True)))
    return (result, conv_grad)

def reference(ocean_state, land_sea, kernel, conv_bias, norm_gain, norm_bias, w_expand, b_expand, w_reduce, b_reduce, layer_scale, cotangent):
    keep_mask = land_sea.astype(jnp.float32)[:, :, None]
    masked = (ocean_state.astype(jnp.float32) * keep_mask).astype(jnp.bfloat16)

    def convolve(plane_in):
        return depthwise(fold_pad(plane_in), kernel, conv_bias)
    conv_out, pullback = jax.vjp(convolve, masked.astype(jnp.float32))

    def per_row(row_items):
        return pointwise(row_items[0], row_items[1], row_items[2], row_items[3], norm_gain, norm_bias, w_expand, b_expand, w_reduce, b_reduce, layer_scale)
    result, conv_grad = lax.map(per_row, (conv_out, ocean_state, keep_mask, cotangent))
    masked_grad = pullback(conv_grad)[0]
    state_grad = (keep_mask * (cotangent.astype(jnp.float32) + masked_grad)).astype(jnp.bfloat16)
    return (result, state_grad)
```

```python
import jax
import jax.numpy as jnp
from jax import lax
from jax.sharding import PartitionSpec as P


def shifted(block, axis, distance):
    devices = range(lax.axis_size(axis))
    route = [((i - distance) % len(devices), i) for i in devices]
    return lax.ppermute(block, axis, route)


def from_behind(value, axis, steps):
    count = lax.axis_size(axis)
    leading, last = (max(0, -steps), min(count, count - steps))
    return lax.ppermute(value, axis, [(source, source + steps) for source in range(leading, last)])


def mirrored(value, axis):
    count = lax.axis_size(axis)
    return lax.ppermute(value[::-1, ::-1], axis, [(i, count - 1 - i) for i in range(count)])


def with_col_halo(block, width):
    left = shifted(block[:, block.shape[1] - width :], "lon", 1)
    right = shifted(block[:, :width], "lon", -1)
    return jnp.concatenate([left, block, right], axis=1)


def gelu_value(values):
    return 0.5 * values * (1.0 + lax.erf(values * 0.7071067811865476))


def gelu_slope(values):
    cumulative = 0.5 * (1.0 + lax.erf(values * 0.7071067811865476))
    return cumulative + values * jnp.exp(-0.5 * values * values) * 0.3989422804014327


def correlate(padded, kernel, start):
    out_rows = padded.shape[0] - 6
    out_cols = padded.shape[1] - 6
    summed = start
    for row_tap in range(7):
        for col_tap in range(7):
            window = padded[row_tap : row_tap + out_rows, col_tap : col_tap + out_cols]
            summed = summed + kernel[row_tap, col_tap].astype(jnp.float32) * window
    return summed


def pointwise(
    conv_out,
    ocean_state,
    keep_mask,
    cotangent,
    norm_gain,
    norm_bias,
    w_expand,
    b_expand,
    w_reduce,
    b_reduce,
    layer_scale,
):
    row_mean = jnp.mean(conv_out, axis=-1, keepdims=True)
    centered = conv_out - row_mean
    inv_std = lax.rsqrt(jnp.mean(centered * centered, axis=-1, keepdims=True) + 1e-06)
    normal_hat = centered * inv_std
    normed = (normal_hat * norm_gain + norm_bias).astype(jnp.bfloat16)
    hidden = jnp.dot(normed, w_expand, preferred_element_type=jnp.float32) + b_expand
    activated = gelu_value(hidden).astype(jnp.bfloat16)
    projected = jnp.dot(activated, w_reduce, preferred_element_type=jnp.float32) + b_reduce
    result = (keep_mask * (ocean_state.astype(jnp.float32) + layer_scale * projected)).astype(
        jnp.bfloat16
    )
    grad_out = (keep_mask * layer_scale * cotangent.astype(jnp.float32)).astype(jnp.bfloat16)
    grad_act = jnp.dot(grad_out, w_reduce.T, preferred_element_type=jnp.float32)
    grad_hidden = (grad_act * gelu_slope(hidden)).astype(jnp.bfloat16)
    grad_normed = jnp.dot(grad_hidden, w_expand.T, preferred_element_type=jnp.float32)
    grad_scaled = grad_normed * norm_gain
    conv_grad = inv_std * (
        grad_scaled
        - jnp.mean(grad_scaled, axis=-1, keepdims=True)
        - normal_hat * jnp.mean(grad_scaled * normal_hat, axis=-1, keepdims=True)
    )
    return (result, conv_grad)


def body(
    ocean_state,
    land_sea,
    kernel,
    conv_bias,
    norm_gain,
    norm_bias,
    w_expand,
    b_expand,
    w_reduce,
    b_reduce,
    layer_scale,
    cotangent,
):
    band_rows, band_cols, channels = ocean_state.shape
    top_band = lax.axis_index("lat") == lax.axis_size("lat") - 1
    keep_mask = land_sea.astype(jnp.float32)[:, :, None]
    masked = (ocean_state.astype(jnp.float32) * keep_mask).astype(jnp.bfloat16)

    below = from_behind(masked[band_rows - 3 :], "lat", 1)
    above = from_behind(masked[:3], "lat", -1)
    fold_rows = mirrored(masked[band_rows - 3 :], "lon")
    upper = jnp.where(top_band, fold_rows, above)
    tall = jnp.concatenate([below, masked, upper], axis=0)
    padded = with_col_halo(tall, 3).astype(jnp.float32)

    start = jnp.zeros((band_rows, band_cols, channels), jnp.float32) + conv_bias
    conv_out = correlate(padded, kernel, start)
    cell_count = band_rows * band_cols
    result, conv_grad = pointwise(
        conv_out.reshape(cell_count, channels),
        ocean_state.reshape(cell_count, channels),
        keep_mask.reshape(cell_count, 1),
        cotangent.reshape(cell_count, channels),
        norm_gain,
        norm_bias,
        w_expand,
        b_expand,
        w_reduce,
        b_reduce,
        layer_scale,
    )
    conv_grad = conv_grad.reshape(band_rows, band_cols, channels)

    grad_below = from_behind(conv_grad[band_rows - 3 :], "lat", 1)
    grad_above = from_behind(conv_grad[:3], "lat", -1)
    grad_tall = jnp.concatenate(
        [grad_below, conv_grad, grad_above, jnp.zeros_like(grad_above)], axis=0
    )
    grad_wide = with_col_halo(grad_tall, 3)
    flipped = kernel[::-1, ::-1]
    spread = correlate(
        grad_wide, flipped, jnp.zeros((band_rows + 3, band_cols, channels), jnp.float32)
    )
    fold_grad = mirrored(spread[band_rows:], "lon")
    fold_term = jnp.where(top_band, fold_grad, jnp.zeros_like(fold_grad))
    masked_grad = spread[:band_rows] + jnp.pad(fold_term, ((band_rows - 3, 0), (0, 0), (0, 0)))
    state_grad = (keep_mask * (cotangent.astype(jnp.float32) + masked_grad)).astype(jnp.bfloat16)
    return (result.reshape(band_rows, band_cols, channels), state_grad)


def solution(mesh):
    placed = (
        P("lat", "lon", None),
        P("lat", "lon"),
        P(),
        P(),
        P(),
        P(),
        P(),
        P(),
        P(),
        P(),
        P(),
        P("lat", "lon", None),
    )
    return jax.shard_map(
        body,
        mesh=mesh,
        in_specs=placed,
        out_specs=(P("lat", "lon", None), P("lat", "lon", None)),
        check_vma=False,
    )
```

```python
import jax
import jax.numpy as jnp
from jax import lax
from jax.sharding import PartitionSpec as P
from jax.experimental import pallas as pl
from jax.experimental.pallas import tpu as pltpu


def shifted(block, axis, distance):
    devices = range(lax.axis_size(axis))
    route = [((i - distance) % len(devices), i) for i in devices]
    return lax.ppermute(block, axis, route)


def from_behind(value, axis, steps):
    count = lax.axis_size(axis)
    leading, last = (max(0, -steps), min(count, count - steps))
    return lax.ppermute(value, axis, [(source, source + steps) for source in range(leading, last)])


def mirrored(value, axis):
    count = lax.axis_size(axis)
    return lax.ppermute(value[::-1, ::-1], axis, [(i, count - 1 - i) for i in range(count)])


def with_col_halo(block, width):
    left = shifted(block[:, block.shape[1] - width :], "lon", 1)
    right = shifted(block[:, :width], "lon", -1)
    return jnp.concatenate([left, block, right], axis=1)


def gelu_value(values):
    return 0.5 * values * (1.0 + lax.erf(values * 0.7071067811865476))


def gelu_slope(values):
    cumulative = 0.5 * (1.0 + lax.erf(values * 0.7071067811865476))
    return cumulative + values * jnp.exp(-0.5 * values * values) * 0.3989422804014327


def correlate(padded, kernel, start, block=4):
    in_rows, in_cols, chans = padded.shape
    out_rows, out_cols = in_rows - 6, in_cols - 6
    steps = -(-out_rows // block)
    taps = kernel.astype(jnp.float32).reshape(49, 1, chans)

    def run(x_ref, k_ref, s_ref, o_ref):
        def step(i, carry):
            r0 = jnp.minimum(i * block, out_rows - block)
            acc = jnp.broadcast_to(s_ref[...], (block, out_cols, chans))
            for row_tap in range(7):
                for col_tap in range(7):
                    window = x_ref[pl.ds(r0 + row_tap, block), pl.ds(col_tap, out_cols), :]
                    acc = acc + k_ref[row_tap * 7 + col_tap] * window
            o_ref[pl.ds(r0, block)] = acc
            return carry

        lax.fori_loop(0, steps, step, 0)

    return pl.pallas_call(
        run,
        out_shape=jax.ShapeDtypeStruct((out_rows, out_cols, chans), jnp.float32),
        in_specs=[pl.BlockSpec(memory_space=pltpu.VMEM)] * 3,
        out_specs=pl.BlockSpec(memory_space=pltpu.VMEM),
    )(padded, taps, start.reshape(1, chans))


def pointwise(
    conv_out,
    ocean_state,
    keep_mask,
    cotangent,
    norm_gain,
    norm_bias,
    w_expand,
    b_expand,
    w_reduce,
    b_reduce,
    layer_scale,
):
    row_mean = jnp.mean(conv_out, axis=-1, keepdims=True)
    centered = conv_out - row_mean
    inv_std = lax.rsqrt(jnp.mean(centered * centered, axis=-1, keepdims=True) + 1e-06)
    normal_hat = centered * inv_std
    normed = (normal_hat * norm_gain + norm_bias).astype(jnp.bfloat16)
    hidden = jnp.dot(normed, w_expand, preferred_element_type=jnp.float32) + b_expand
    activated = gelu_value(hidden).astype(jnp.bfloat16)
    projected = jnp.dot(activated, w_reduce, preferred_element_type=jnp.float32) + b_reduce
    result = (keep_mask * (ocean_state.astype(jnp.float32) + layer_scale * projected)).astype(
        jnp.bfloat16
    )
    grad_out = (keep_mask * layer_scale * cotangent.astype(jnp.float32)).astype(jnp.bfloat16)
    grad_act = jnp.dot(grad_out, w_reduce.T, preferred_element_type=jnp.float32)
    grad_hidden = (grad_act * gelu_slope(hidden)).astype(jnp.bfloat16)
    grad_normed = jnp.dot(grad_hidden, w_expand.T, preferred_element_type=jnp.float32)
    grad_scaled = grad_normed * norm_gain
    conv_grad = inv_std * (
        grad_scaled
        - jnp.mean(grad_scaled, axis=-1, keepdims=True)
        - normal_hat * jnp.mean(grad_scaled * normal_hat, axis=-1, keepdims=True)
    )
    return (result, conv_grad)


def body(
    ocean_state,
    land_sea,
    kernel,
    conv_bias,
    norm_gain,
    norm_bias,
    w_expand,
    b_expand,
    w_reduce,
    b_reduce,
    layer_scale,
    cotangent,
):
    band_rows, band_cols, channels = ocean_state.shape
    top_band = lax.axis_index("lat") == lax.axis_size("lat") - 1
    keep_mask = land_sea.astype(jnp.float32)[:, :, None]
    masked = (ocean_state.astype(jnp.float32) * keep_mask).astype(jnp.bfloat16)

    below = from_behind(masked[band_rows - 3 :], "lat", 1)
    above = from_behind(masked[:3], "lat", -1)
    fold_rows = mirrored(masked[band_rows - 3 :], "lon")
    upper = jnp.where(top_band, fold_rows, above)
    tall = jnp.concatenate([below, masked, upper], axis=0)
    padded = with_col_halo(tall, 3).astype(jnp.float32)

    conv_out = correlate(padded, kernel, conv_bias)
    cell_count = band_rows * band_cols
    result, conv_grad = pointwise(
        conv_out.reshape(cell_count, channels),
        ocean_state.reshape(cell_count, channels),
        keep_mask.reshape(cell_count, 1),
        cotangent.reshape(cell_count, channels),
        norm_gain,
        norm_bias,
        w_expand,
        b_expand,
        w_reduce,
        b_reduce,
        layer_scale,
    )
    conv_grad = conv_grad.reshape(band_rows, band_cols, channels)

    grad_below = from_behind(conv_grad[band_rows - 3 :], "lat", 1)
    grad_above = from_behind(conv_grad[:3], "lat", -1)
    grad_tall = jnp.concatenate(
        [grad_below, conv_grad, grad_above, jnp.zeros_like(grad_above)], axis=0
    )
    grad_wide = with_col_halo(grad_tall, 3)
    flipped = kernel[::-1, ::-1]
    spread = correlate(grad_wide, flipped, jnp.zeros((channels,), jnp.float32))
    fold_grad = mirrored(spread[band_rows:], "lon")
    fold_term = jnp.where(top_band, fold_grad, jnp.zeros_like(fold_grad))
    masked_grad = spread[:band_rows] + jnp.pad(fold_term, ((band_rows - 3, 0), (0, 0), (0, 0)))
    state_grad = (keep_mask * (cotangent.astype(jnp.float32) + masked_grad)).astype(jnp.bfloat16)
    return (result.reshape(band_rows, band_cols, channels), state_grad)


def solution(mesh):
    placed = (
        P("lat", "lon", None),
        P("lat", "lon"),
        P(),
        P(),
        P(),
        P(),
        P(),
        P(),
        P(),
        P(),
        P(),
        P("lat", "lon", None),
    )
    return jax.shard_map(
        body,
        mesh=mesh,
        in_specs=placed,
        out_specs=(P("lat", "lon", None), P("lat", "lon", None)),
        check_vma=False,
    )
```

```python
import jax
import jax.numpy as jnp
from jax import lax
from jax.sharding import PartitionSpec as P
from jax.experimental import pallas as pl
from jax.experimental.pallas import tpu as pltpu


def take(piece, dlat, dlon):
    nlat, nlon = lax.axis_size("lat"), lax.axis_size("lon")
    if dlat == 0:
        return lax.ppermute(piece, "lon", [((j - dlon) % nlon, j) for j in range(nlon)])
    sources = [i for i in range(nlat) if 0 <= i - dlat < nlat]
    if dlon == 0:
        return lax.ppermute(piece, "lat", [(i - dlat, i) for i in sources])
    pairs = [
        (((j - dlon) % nlon) * nlat + i - dlat, j * nlat + i) for i in sources for j in range(nlon)
    ]
    return lax.ppermute(piece, ("lon", "lat"), pairs)


def mirror(piece, offset):
    nlat, nlon = lax.axis_size("lat"), lax.axis_size("lon")
    top = nlat - 1
    pairs = [(q * nlat + top, ((nlon - 1 - q + offset) % nlon) * nlat + top) for q in range(nlon)]
    return lax.ppermute(piece, ("lon", "lat"), pairs)


def fold_pieces(rows):
    flipped = rows[::-1, ::-1]
    cols = rows.shape[1]
    return (mirror(flipped[:, cols - 3 :], 1), mirror(flipped, 0), mirror(flipped[:, :3], -1))


def haloed(block, north):
    rows, cols = block.shape[:2]
    low, high = block[:3], block[rows - 3 :]
    south = (take(high[:, cols - 3 :], 1, 1), take(high, 1, 0), take(high[:, :3], 1, -1))
    above = (take(low[:, cols - 3 :], -1, 1), take(low, -1, 0), take(low[:, :3], -1, -1))
    if north is not None:
        above = tuple(x + y for x, y in zip(above, north))
    middle = (take(block[:, cols - 3 :], 0, 1), block, take(block[:, :3], 0, -1))
    return jnp.concatenate(
        [jnp.concatenate(part, axis=1) for part in (south, middle, above)], axis=0
    )


def gelu_value(values):
    return 0.5 * values * (1.0 + lax.erf(values * 0.7071067811865476))


def gelu_slope(values):
    cumulative = 0.5 * (1.0 + lax.erf(values * 0.7071067811865476))
    return cumulative + values * jnp.exp(-0.5 * values * values) * 0.3989422804014327


def correlate(padded, kernel, start, block=4):
    in_rows, in_cols, chans = padded.shape
    out_rows, out_cols = in_rows - 6, in_cols - 6
    block = min(block, out_rows)
    steps = -(-out_rows // block)
    taps = kernel.astype(jnp.float32).reshape(49, 1, chans)

    def run(x_ref, k_ref, s_ref, o_ref):
        def step(i, carry):
            r0 = jnp.minimum(i * block, out_rows - block)
            acc = jnp.broadcast_to(s_ref[...], (block, out_cols, chans))
            for row_tap in range(7):
                for col_tap in range(7):
                    window = x_ref[pl.ds(r0 + row_tap, block), pl.ds(col_tap, out_cols), :]
                    acc = acc + k_ref[row_tap * 7 + col_tap] * window
            o_ref[pl.ds(r0, block)] = acc
            return carry

        lax.fori_loop(0, steps, step, 0)

    return pl.pallas_call(
        run,
        out_shape=jax.ShapeDtypeStruct((out_rows, out_cols, chans), jnp.float32),
        in_specs=[pl.BlockSpec(memory_space=pltpu.VMEM)] * 3,
        out_specs=pl.BlockSpec(memory_space=pltpu.VMEM),
    )(padded, taps, start.reshape(1, chans))


def pointwise(
    conv_out,
    ocean_state,
    keep_mask,
    cotangent,
    norm_gain,
    norm_bias,
    w_expand,
    b_expand,
    w_reduce,
    b_reduce,
    layer_scale,
):
    row_mean = jnp.mean(conv_out, axis=-1, keepdims=True)
    centered = conv_out - row_mean
    inv_std = lax.rsqrt(jnp.mean(centered * centered, axis=-1, keepdims=True) + 1e-06)
    normal_hat = centered * inv_std
    normed = (normal_hat * norm_gain + norm_bias).astype(jnp.bfloat16)
    hidden = jnp.dot(normed, w_expand, preferred_element_type=jnp.float32) + b_expand
    activated = gelu_value(hidden).astype(jnp.bfloat16)
    projected = jnp.dot(activated, w_reduce, preferred_element_type=jnp.float32) + b_reduce
    result = (keep_mask * (ocean_state.astype(jnp.float32) + layer_scale * projected)).astype(
        jnp.bfloat16
    )
    grad_out = (keep_mask * layer_scale * cotangent.astype(jnp.float32)).astype(jnp.bfloat16)
    grad_act = jnp.dot(grad_out, w_reduce.T, preferred_element_type=jnp.float32)
    grad_hidden = (grad_act * gelu_slope(hidden)).astype(jnp.bfloat16)
    grad_normed = jnp.dot(grad_hidden, w_expand.T, preferred_element_type=jnp.float32)
    grad_scaled = grad_normed * norm_gain
    conv_grad = inv_std * (
        grad_scaled
        - jnp.mean(grad_scaled, axis=-1, keepdims=True)
        - normal_hat * jnp.mean(grad_scaled * normal_hat, axis=-1, keepdims=True)
    )
    return (result, conv_grad)


def body(
    ocean_state,
    land_sea,
    kernel,
    conv_bias,
    norm_gain,
    norm_bias,
    w_expand,
    b_expand,
    w_reduce,
    b_reduce,
    layer_scale,
    cotangent,
):
    band_rows, band_cols, channels = ocean_state.shape
    keep_mask = land_sea.astype(jnp.float32)[:, :, None]
    masked = (ocean_state.astype(jnp.float32) * keep_mask).astype(jnp.bfloat16)

    padded = haloed(masked, fold_pieces(masked[band_rows - 3 :])).astype(jnp.float32)
    conv_out = correlate(padded, kernel, conv_bias)
    cell_count = band_rows * band_cols
    result, conv_grad = pointwise(
        conv_out.reshape(cell_count, channels),
        ocean_state.reshape(cell_count, channels),
        keep_mask.reshape(cell_count, 1),
        cotangent.reshape(cell_count, channels),
        norm_gain,
        norm_bias,
        w_expand,
        b_expand,
        w_reduce,
        b_reduce,
        layer_scale,
    )
    conv_grad = conv_grad.reshape(band_rows, band_cols, channels)

    grad_wide = haloed(conv_grad, None)
    zero_bias = jnp.zeros((channels,), jnp.float32)
    masked_grad = correlate(grad_wide, kernel[::-1, ::-1], zero_bias)
    fold_grad = jnp.concatenate(fold_pieces(conv_grad[band_rows - 3 :]), axis=1)
    fold_grad = jnp.concatenate([jnp.zeros((6,) + fold_grad.shape[1:], jnp.float32), fold_grad], 0)
    fold_term = correlate(fold_grad, kernel, zero_bias)
    masked_grad = masked_grad + jnp.pad(fold_term, ((band_rows - 3, 0), (0, 0), (0, 0)))
    state_grad = (keep_mask * (cotangent.astype(jnp.float32) + masked_grad)).astype(jnp.bfloat16)
    return (result.reshape(band_rows, band_cols, channels), state_grad)


def solution(mesh):
    placed = (
        P("lat", "lon", None),
        P("lat", "lon"),
        P(),
        P(),
        P(),
        P(),
        P(),
        P(),
        P(),
        P(),
        P(),
        P("lat", "lon", None),
    )
    return jax.shard_map(
        body,
        mesh=mesh,
        in_specs=placed,
        out_specs=(P("lat", "lon", None), P("lat", "lon", None)),
        check_vma=False,
    )
```

```python
import jax
import jax.numpy as jnp
from jax import lax
from jax.sharding import PartitionSpec as P
from jax.experimental import pallas as pl
from jax.experimental.pallas import tpu as pltpu


MESH = pl.DeviceIdType.MESH


def correlate_into(src, taps, bias, o_ref, out_rows, out_cols, chans, block=4):
    block = min(block, out_rows)
    steps = -(-out_rows // block)

    def step(i, carry):
        r0 = jnp.minimum(i * block, out_rows - block)
        acc = jnp.broadcast_to(bias, (block, out_cols, chans))
        for row_tap in range(7):
            for col_tap in range(7):
                window = src[pl.ds(r0 + row_tap, block), pl.ds(col_tap, out_cols), :]
                acc = acc + taps[row_tap * 7 + col_tap] * window
        o_ref[pl.ds(r0, block)] = acc
        return carry

    lax.fori_loop(0, steps, step, 0)


def halo_correlate(block, fold_src, taps, fold_taps, bias, north_fold, collective):
    rows, cols, chans = block.shape
    nlat, nlon = lax.axis_size("lat"), lax.axis_size("lon")
    fold_back = fold_taps is not None

    def run(x_ref, f_ref, k_ref, kf_ref, b_ref, o_ref, pad, gf, send, recv, local, folds):
        band = lax.axis_index("lat")
        lon = lax.axis_index("lon")
        has_south = band > 0
        has_north = band < nlat - 1
        top = band == nlat - 1
        west = lax.rem(lon + nlon - 1, nlon)
        east = lax.rem(lon + 1, nlon)
        fold_dst = gf if fold_back else pad
        fold_row = 6 if fold_back else rows + 3
        hi = pl.ds(rows - 3, 3)
        lo = pl.ds(0, 3)
        allr = pl.ds(0, rows)
        c_lo, c_hi, c_all = pl.ds(0, 3), pl.ds(cols - 3, 3), pl.ds(0, cols)
        d_w, d_mid, d_e = pl.ds(0, 3), pl.ds(3, cols), pl.ds(cols + 3, 3)
        messages = [
            (x_ref.at[hi, c_all], pad.at[pl.ds(0, 3), d_mid], (lon, band + 1), has_north, has_south),
            (x_ref.at[hi, c_hi], pad.at[pl.ds(0, 3), d_w], (east, band + 1), has_north, has_south),
            (x_ref.at[hi, c_lo], pad.at[pl.ds(0, 3), d_e], (west, band + 1), has_north, has_south),
            (x_ref.at[lo, c_all], pad.at[pl.ds(rows + 3, 3), d_mid], (lon, band - 1), has_south, has_north),
            (x_ref.at[lo, c_hi], pad.at[pl.ds(rows + 3, 3), d_w], (east, band - 1), has_south, has_north),
            (x_ref.at[lo, c_lo], pad.at[pl.ds(rows + 3, 3), d_e], (west, band - 1), has_south, has_north),
            (x_ref.at[allr, c_hi], pad.at[pl.ds(3, rows), d_w], (east, band), None, None),
            (x_ref.at[allr, c_lo], pad.at[pl.ds(3, rows), d_e], (west, band), None, None),
            (f_ref.at[:, c_all], fold_dst.at[pl.ds(fold_row, 3), d_mid], (nlon - 1 - lon, band), top, top),
            (f_ref.at[:, c_hi], fold_dst.at[pl.ds(fold_row, 3), d_w], (lax.rem(2 * nlon - lon, nlon), band), top, top),
            (f_ref.at[:, c_lo], fold_dst.at[pl.ds(fold_row, 3), d_e], (lax.rem(2 * nlon - 2 - lon, nlon), band), top, top),
        ]
        sources = [
            (lon, band - 1), (west, band - 1), (east, band - 1),
            (lon, band + 1), (west, band + 1), (east, band + 1),
            (west, band), (east, band),
        ]
        for i in (9, 10):
            src, dst, target, _, _ = messages[i]
            apart = jnp.logical_and(top, target[0] != lon)
            messages[i] = (src, dst, target, apart, apart)
        sources += [messages[8][2], messages[9][2], messages[10][2]]
        own = [
            (pltpu.make_async_copy(messages[i][0], messages[i][1], folds.at[j]),
             jnp.logical_and(top, messages[i][2][0] == lon))
            for j, i in enumerate((9, 10))
        ]
        for copy, cond in own:
            pl.when(cond)(copy.start)

        interior = pltpu.make_async_copy(x_ref, pad.at[pl.ds(3, rows), pl.ds(3, cols)], local)
        interior.start()

        @pl.when(band == 0)
        def _():
            pad[pl.ds(0, 3)] = jnp.zeros((3, cols + 6, chans), jnp.float32)

        if not north_fold:
            @pl.when(top)
            def _():
                pad[pl.ds(rows + 3, 3)] = jnp.zeros((3, cols + 6, chans), jnp.float32)

        if fold_back:
            gf[pl.ds(0, 6)] = jnp.zeros((6, cols + 6, chans), jnp.float32)

            @pl.when(jnp.logical_not(top))
            def _():
                gf[pl.ds(6, 3)] = jnp.zeros((3, cols + 6, chans), jnp.float32)

        barrier = pltpu.get_barrier_semaphore()

        def when(cond, fn):
            if cond is None:
                fn()
            else:
                pl.when(cond)(fn)

        for (src, dst, target, s_cond, r_cond), source in zip(messages, sources):
            def greet_target(target=target):
                pl.semaphore_signal(barrier, 1, device_id=target, device_id_type=MESH)

            def greet_source(source=source):
                pl.semaphore_signal(barrier, 1, device_id=source, device_id_type=MESH)

            when(s_cond, greet_target)
            when(r_cond, greet_source)
        edge = has_north.astype(jnp.int32) + has_south.astype(jnp.int32)
        folded = top.astype(jnp.int32) + sum(messages[i][3].astype(jnp.int32) for i in (9, 10))
        expected = 2 * (3 * edge + 2 + folded)
        pl.semaphore_wait(barrier, expected)

        copies = []
        for i, (src, dst, target, s_cond, r_cond) in enumerate(messages):
            copy = pltpu.make_async_remote_copy(
                src_ref=src,
                dst_ref=dst,
                send_sem=send.at[i],
                recv_sem=recv.at[i],
                device_id=target,
                device_id_type=MESH,
            )
            copies.append(copy)
            when(s_cond, copy.start)
        for copy, (src, dst, target, s_cond, r_cond) in zip(copies, messages):
            when(s_cond, copy.wait_send)
            when(r_cond, copy.wait_recv)
        interior.wait()
        for copy, cond in own:
            pl.when(cond)(copy.wait)

        correlate_into(pad, k_ref, b_ref[...], o_ref, rows, cols, chans)
        if fold_back:
            extra = jnp.zeros((3, cols, chans), jnp.float32)
            for row_tap in range(7):
                for col_tap in range(7):
                    window = gf[pl.ds(row_tap, 3), pl.ds(col_tap, cols), :]
                    extra = extra + kf_ref[row_tap * 7 + col_tap] * window
            o_ref[pl.ds(rows - 3, 3)] = o_ref[pl.ds(rows - 3, 3)] + extra

    taps = taps.astype(jnp.float32).reshape(49, 1, chans)
    if fold_taps is None:
        fold_taps = taps
    else:
        fold_taps = fold_taps.astype(jnp.float32).reshape(49, 1, chans)
    return pl.pallas_call(
        run,
        out_shape=jax.ShapeDtypeStruct((rows, cols, chans), jnp.float32),
        in_specs=[pl.BlockSpec(memory_space=pltpu.VMEM)] * 5,
        out_specs=pl.BlockSpec(memory_space=pltpu.VMEM),
        scratch_shapes=[
            pltpu.VMEM((rows + 6, cols + 6, chans), jnp.float32),
            pltpu.VMEM((9, cols + 6, chans), jnp.float32),
            pltpu.SemaphoreType.DMA((11,)),
            pltpu.SemaphoreType.DMA((11,)),
            pltpu.SemaphoreType.DMA,
            pltpu.SemaphoreType.DMA((2,)),
        ],
        compiler_params=pltpu.CompilerParams(collective_id=collective, has_side_effects=True),
    )(block, fold_src, taps, fold_taps, bias.reshape(1, chans))


def gelu_value(values):
    return 0.5 * values * (1.0 + lax.erf(values * 0.7071067811865476))


def gelu_slope(values):
    cumulative = 0.5 * (1.0 + lax.erf(values * 0.7071067811865476))
    return cumulative + values * jnp.exp(-0.5 * values * values) * 0.3989422804014327


def pointwise(
    conv_out,
    ocean_state,
    keep_mask,
    cotangent,
    norm_gain,
    norm_bias,
    w_expand,
    b_expand,
    w_reduce,
    b_reduce,
    layer_scale,
):
    row_mean = jnp.mean(conv_out, axis=-1, keepdims=True)
    centered = conv_out - row_mean
    inv_std = lax.rsqrt(jnp.mean(centered * centered, axis=-1, keepdims=True) + 1e-06)
    normal_hat = centered * inv_std
    normed = (normal_hat * norm_gain + norm_bias).astype(jnp.bfloat16)
    hidden = jnp.dot(normed, w_expand, preferred_element_type=jnp.float32) + b_expand
    activated = gelu_value(hidden).astype(jnp.bfloat16)
    projected = jnp.dot(activated, w_reduce, preferred_element_type=jnp.float32) + b_reduce
    result = (keep_mask * (ocean_state.astype(jnp.float32) + layer_scale * projected)).astype(
        jnp.bfloat16
    )
    grad_out = (keep_mask * layer_scale * cotangent.astype(jnp.float32)).astype(jnp.bfloat16)
    grad_act = jnp.dot(grad_out, w_reduce.T, preferred_element_type=jnp.float32)
    grad_hidden = (grad_act * gelu_slope(hidden)).astype(jnp.bfloat16)
    grad_normed = jnp.dot(grad_hidden, w_expand.T, preferred_element_type=jnp.float32)
    grad_scaled = grad_normed * norm_gain
    conv_grad = inv_std * (
        grad_scaled
        - jnp.mean(grad_scaled, axis=-1, keepdims=True)
        - normal_hat * jnp.mean(grad_scaled * normal_hat, axis=-1, keepdims=True)
    )
    return (result, conv_grad)


def body(
    ocean_state,
    land_sea,
    kernel,
    conv_bias,
    norm_gain,
    norm_bias,
    w_expand,
    b_expand,
    w_reduce,
    b_reduce,
    layer_scale,
    cotangent,
):
    band_rows, band_cols, channels = ocean_state.shape
    keep_mask = land_sea.astype(jnp.float32)[:, :, None]
    masked = (ocean_state.astype(jnp.float32) * keep_mask).astype(jnp.bfloat16)

    masked32 = masked.astype(jnp.float32)
    top_rows = masked32[band_rows - 3 :][::-1, ::-1]
    conv_out = halo_correlate(masked32, top_rows, kernel, None, conv_bias, True, 0)
    cell_count = band_rows * band_cols
    result, conv_grad = pointwise(
        conv_out.reshape(cell_count, channels),
        ocean_state.reshape(cell_count, channels),
        keep_mask.reshape(cell_count, 1),
        cotangent.reshape(cell_count, channels),
        norm_gain,
        norm_bias,
        w_expand,
        b_expand,
        w_reduce,
        b_reduce,
        layer_scale,
    )
    conv_grad = conv_grad.reshape(band_rows, band_cols, channels)

    grad_top = conv_grad[band_rows - 3 :][::-1, ::-1]
    zero_bias = jnp.zeros((channels,), jnp.float32)
    masked_grad = halo_correlate(
        conv_grad, grad_top, kernel[::-1, ::-1], kernel, zero_bias, False, 1
    )
    state_grad = (keep_mask * (cotangent.astype(jnp.float32) + masked_grad)).astype(jnp.bfloat16)
    return (result.reshape(band_rows, band_cols, channels), state_grad)


def solution(mesh):
    placed = (
        P("lat", "lon", None),
        P("lat", "lon"),
        P(),
        P(),
        P(),
        P(),
        P(),
        P(),
        P(),
        P(),
        P(),
        P("lat", "lon", None),
    )
    return jax.shard_map(
        body,
        mesh=mesh,
        in_specs=placed,
        out_specs=(P("lat", "lon", None), P("lat", "lon", None)),
        check_vma=False,
    )
```

```python
import jax
import jax.numpy as jnp
from jax import lax
from jax.sharding import PartitionSpec as P
from jax.experimental import pallas as pl
from jax.experimental.pallas import tpu as pltpu


MESH = pl.DeviceIdType.MESH


def correlate_into(src, taps, bias, o_ref, out_rows, out_cols, chans, block=4):
    block = min(block, out_rows)
    steps = -(-out_rows // block)

    def step(i, carry):
        r0 = jnp.minimum(i * block, out_rows - block)
        acc = jnp.broadcast_to(bias, (block, out_cols, chans))
        for row_tap in range(7):
            for col_tap in range(7):
                window = src[pl.ds(r0 + row_tap, block), pl.ds(col_tap, out_cols), :]
                acc = acc + taps[row_tap * 7 + col_tap] * window
        o_ref[pl.ds(r0, block)] = acc
        return carry

    lax.fori_loop(0, steps, step, 0)


def halo_correlate(block, fold_src, taps, fold_taps, bias, north_fold, collective):
    rows, cols, chans = block.shape
    nlat, nlon = lax.axis_size("lat"), lax.axis_size("lon")
    fold_back = fold_taps is not None

    def run(x_ref, f_ref, k_ref, kf_ref, b_ref, o_ref, pad, gf, send, recv, local, folds):
        band = lax.axis_index("lat")
        lon = lax.axis_index("lon")
        has_south = band > 0
        has_north = band < nlat - 1
        top = band == nlat - 1
        west = lax.rem(lon + nlon - 1, nlon)
        east = lax.rem(lon + 1, nlon)
        fold_dst = gf if fold_back else pad
        fold_row = 6 if fold_back else rows + 3
        hi = pl.ds(rows - 3, 3)
        lo = pl.ds(0, 3)
        allr = pl.ds(0, rows)
        c_lo, c_hi, c_all = pl.ds(0, 3), pl.ds(cols - 3, 3), pl.ds(0, cols)
        d_w, d_mid, d_e = pl.ds(0, 3), pl.ds(3, cols), pl.ds(cols + 3, 3)
        messages = [
            (x_ref.at[hi, c_all], pad.at[pl.ds(0, 3), d_mid], (lon, band + 1), has_north, has_south),
            (x_ref.at[hi, c_hi], pad.at[pl.ds(0, 3), d_w], (east, band + 1), has_north, has_south),
            (x_ref.at[hi, c_lo], pad.at[pl.ds(0, 3), d_e], (west, band + 1), has_north, has_south),
            (x_ref.at[lo, c_all], pad.at[pl.ds(rows + 3, 3), d_mid], (lon, band - 1), has_south, has_north),
            (x_ref.at[lo, c_hi], pad.at[pl.ds(rows + 3, 3), d_w], (east, band - 1), has_south, has_north),
            (x_ref.at[lo, c_lo], pad.at[pl.ds(rows + 3, 3), d_e], (west, band - 1), has_south, has_north),
            (x_ref.at[allr, c_hi], pad.at[pl.ds(3, rows), d_w], (east, band), None, None),
            (x_ref.at[allr, c_lo], pad.at[pl.ds(3, rows), d_e], (west, band), None, None),
            (f_ref.at[:, c_all], fold_dst.at[pl.ds(fold_row, 3), d_mid], (nlon - 1 - lon, band), top, top),
            (f_ref.at[:, c_hi], fold_dst.at[pl.ds(fold_row, 3), d_w], (lax.rem(2 * nlon - lon, nlon), band), top, top),
            (f_ref.at[:, c_lo], fold_dst.at[pl.ds(fold_row, 3), d_e], (lax.rem(2 * nlon - 2 - lon, nlon), band), top, top),
        ]
        sources = [
            (lon, band - 1), (west, band - 1), (east, band - 1),
            (lon, band + 1), (west, band + 1), (east, band + 1),
            (west, band), (east, band),
        ]
        for i in (9, 10):
            src, dst, target, _, _ = messages[i]
            apart = jnp.logical_and(top, target[0] != lon)
            messages[i] = (src, dst, target, apart, apart)
        sources += [messages[8][2], messages[9][2], messages[10][2]]
        own = [
            (pltpu.make_async_copy(messages[i][0], messages[i][1], folds.at[j]),
             jnp.logical_and(top, messages[i][2][0] == lon))
            for j, i in enumerate((9, 10))
        ]
        for copy, cond in own:
            pl.when(cond)(copy.start)

        interior = pltpu.make_async_copy(x_ref, pad.at[pl.ds(3, rows), pl.ds(3, cols)], local)
        interior.start()

        @pl.when(band == 0)
        def _():
            pad[pl.ds(0, 3)] = jnp.zeros((3, cols + 6, chans), jnp.float32)

        if not north_fold:
            @pl.when(top)
            def _():
                pad[pl.ds(rows + 3, 3)] = jnp.zeros((3, cols + 6, chans), jnp.float32)

        if fold_back:
            gf[pl.ds(0, 6)] = jnp.zeros((6, cols + 6, chans), jnp.float32)

            @pl.when(jnp.logical_not(top))
            def _():
                gf[pl.ds(6, 3)] = jnp.zeros((3, cols + 6, chans), jnp.float32)

        barrier = pltpu.get_barrier_semaphore()

        def when(cond, fn):
            if cond is None:
                fn()
            else:
                pl.when(cond)(fn)

        for (src, dst, target, s_cond, r_cond), source in zip(messages, sources):
            def greet_target(target=target):
                pl.semaphore_signal(barrier, 1, device_id=target, device_id_type=MESH)

            def greet_source(source=source):
                pl.semaphore_signal(barrier, 1, device_id=source, device_id_type=MESH)

            when(s_cond, greet_target)
            when(r_cond, greet_source)
        edge = has_north.astype(jnp.int32) + has_south.astype(jnp.int32)
        folded = top.astype(jnp.int32) + sum(messages[i][3].astype(jnp.int32) for i in (9, 10))
        expected = 2 * (3 * edge + 2 + folded)
        pl.semaphore_wait(barrier, expected)

        copies = []
        for i, (src, dst, target, s_cond, r_cond) in enumerate(messages):
            copy = pltpu.make_async_remote_copy(
                src_ref=src,
                dst_ref=dst,
                send_sem=send.at[i],
                recv_sem=recv.at[i],
                device_id=target,
                device_id_type=MESH,
            )
            copies.append(copy)
            when(s_cond, copy.start)
        for copy, (src, dst, target, s_cond, r_cond) in zip(copies, messages):
            when(s_cond, copy.wait_send)
            when(r_cond, copy.wait_recv)
        interior.wait()
        for copy, cond in own:
            pl.when(cond)(copy.wait)

        correlate_into(pad, k_ref, b_ref[...], o_ref, rows, cols, chans)
        if fold_back:
            extra = jnp.zeros((3, cols, chans), jnp.float32)
            for row_tap in range(7):
                for col_tap in range(7):
                    window = gf[pl.ds(row_tap, 3), pl.ds(col_tap, cols), :]
                    extra = extra + kf_ref[row_tap * 7 + col_tap] * window
            o_ref[pl.ds(rows - 3, 3)] = o_ref[pl.ds(rows - 3, 3)] + extra

    taps = taps.astype(jnp.float32).reshape(49, 1, chans)
    if fold_taps is None:
        fold_taps = taps
    else:
        fold_taps = fold_taps.astype(jnp.float32).reshape(49, 1, chans)
    return pl.pallas_call(
        run,
        out_shape=jax.ShapeDtypeStruct((rows, cols, chans), jnp.float32),
        in_specs=[pl.BlockSpec(memory_space=pltpu.VMEM)] * 5,
        out_specs=pl.BlockSpec(memory_space=pltpu.VMEM),
        scratch_shapes=[
            pltpu.VMEM((rows + 6, cols + 6, chans), jnp.float32),
            pltpu.VMEM((9, cols + 6, chans), jnp.float32),
            pltpu.SemaphoreType.DMA((11,)),
            pltpu.SemaphoreType.DMA((11,)),
            pltpu.SemaphoreType.DMA,
            pltpu.SemaphoreType.DMA((2,)),
        ],
        compiler_params=pltpu.CompilerParams(collective_id=collective, has_side_effects=True),
    )(block, fold_src, taps, fold_taps, bias.reshape(1, chans))


def gelu_value(values):
    return 0.5 * values * (1.0 + lax.erf(values * 0.7071067811865476))


def gelu_slope(values):
    cumulative = 0.5 * (1.0 + lax.erf(values * 0.7071067811865476))
    return cumulative + values * jnp.exp(-0.5 * values * values) * 0.3989422804014327


def pointwise(
    conv_out,
    ocean_state,
    keep_mask,
    cotangent,
    norm_gain,
    norm_bias,
    w_expand,
    b_expand,
    w_reduce,
    b_reduce,
    layer_scale,
    tile=512,
):
    cells, chans = conv_out.shape
    hidden_size = w_expand.shape[1]
    tile = min(tile, cells)
    contract_last = (((1,), (1,)), ((), ()))

    def run(c_ref, s_ref, m_ref, t_ref, g_ref, nb_ref, we_ref, be_ref, wr_ref, br_ref, ls_ref, r_ref, o_ref):
        conv = c_ref[...]
        keep = m_ref[...]
        gain = g_ref[...]
        scale = ls_ref[...]
        row_mean = jnp.mean(conv, axis=-1, keepdims=True)
        centered = conv - row_mean
        inv_std = lax.rsqrt(jnp.mean(centered * centered, axis=-1, keepdims=True) + 1e-06)
        normal_hat = centered * inv_std
        normed = (normal_hat * gain + nb_ref[...]).astype(jnp.bfloat16)
        hidden = jnp.dot(normed, we_ref[...], preferred_element_type=jnp.float32) + be_ref[...]
        erf_term = lax.erf(hidden * 0.7071067811865476)
        activated = (0.5 * hidden * (1.0 + erf_term)).astype(jnp.bfloat16)
        projected = jnp.dot(activated, wr_ref[...], preferred_element_type=jnp.float32) + br_ref[...]
        r_ref[...] = (keep * (s_ref[...].astype(jnp.float32) + scale * projected)).astype(r_ref.dtype)
        grad_out = (keep * scale * t_ref[...].astype(jnp.float32)).astype(jnp.bfloat16)
        grad_act = lax.dot_general(
            grad_out, wr_ref[...], contract_last, preferred_element_type=jnp.float32
        )
        slope = 0.5 * (1.0 + erf_term) + hidden * jnp.exp(-0.5 * hidden * hidden) * 0.3989422804014327
        grad_hidden = (grad_act * slope).astype(jnp.bfloat16)
        grad_normed = lax.dot_general(
            grad_hidden, we_ref[...], contract_last, preferred_element_type=jnp.float32
        )
        grad_scaled = grad_normed * gain
        o_ref[...] = inv_std * (
            grad_scaled
            - jnp.mean(grad_scaled, axis=-1, keepdims=True)
            - normal_hat * jnp.mean(grad_scaled * normal_hat, axis=-1, keepdims=True)
        )

    rows = lambda width: pl.BlockSpec((tile, width), lambda i: (i, 0))
    whole = lambda shape: pl.BlockSpec(shape, lambda i: (0, 0))
    vec = lambda v: v.reshape(1, -1)
    return pl.pallas_call(
        run,
        grid=(cells // tile,),
        out_shape=(
            jax.ShapeDtypeStruct((cells, chans), jnp.bfloat16),
            jax.ShapeDtypeStruct((cells, chans), jnp.float32),
        ),
        in_specs=[
            rows(chans), rows(chans), rows(1), rows(chans),
            whole((1, chans)), whole((1, chans)),
            whole((chans, hidden_size)), whole((1, hidden_size)),
            whole((hidden_size, chans)), whole((1, chans)), whole((1, chans)),
        ],
        out_specs=(rows(chans), rows(chans)),
    )(
        conv_out, ocean_state, keep_mask, cotangent, vec(norm_gain), vec(norm_bias),
        w_expand, vec(b_expand), w_reduce, vec(b_reduce), vec(layer_scale),
    )


def body(
    ocean_state,
    land_sea,
    kernel,
    conv_bias,
    norm_gain,
    norm_bias,
    w_expand,
    b_expand,
    w_reduce,
    b_reduce,
    layer_scale,
    cotangent,
):
    band_rows, band_cols, channels = ocean_state.shape
    keep_mask = land_sea.astype(jnp.float32)[:, :, None]
    masked = (ocean_state.astype(jnp.float32) * keep_mask).astype(jnp.bfloat16)

    masked32 = masked.astype(jnp.float32)
    top_rows = masked32[band_rows - 3 :][::-1, ::-1]
    conv_out = halo_correlate(masked32, top_rows, kernel, None, conv_bias, True, 0)
    cell_count = band_rows * band_cols
    result, conv_grad = pointwise(
        conv_out.reshape(cell_count, channels),
        ocean_state.reshape(cell_count, channels),
        keep_mask.reshape(cell_count, 1),
        cotangent.reshape(cell_count, channels),
        norm_gain,
        norm_bias,
        w_expand,
        b_expand,
        w_reduce,
        b_reduce,
        layer_scale,
    )
    conv_grad = conv_grad.reshape(band_rows, band_cols, channels)

    grad_top = conv_grad[band_rows - 3 :][::-1, ::-1]
    zero_bias = jnp.zeros((channels,), jnp.float32)
    masked_grad = halo_correlate(
        conv_grad, grad_top, kernel[::-1, ::-1], kernel, zero_bias, False, 1
    )
    state_grad = (keep_mask * (cotangent.astype(jnp.float32) + masked_grad)).astype(jnp.bfloat16)
    return (result.reshape(band_rows, band_cols, channels), state_grad)


def solution(mesh):
    placed = (
        P("lat", "lon", None),
        P("lat", "lon"),
        P(),
        P(),
        P(),
        P(),
        P(),
        P(),
        P(),
        P(),
        P(),
        P("lat", "lon", None),
    )
    return jax.shard_map(
        body,
        mesh=mesh,
        in_specs=placed,
        out_specs=(P("lat", "lon", None), P("lat", "lon", None)),
        check_vma=False,
    )
```

```python
import jax
import jax.numpy as jnp
from jax import lax
from jax.sharding import PartitionSpec as P
from jax.experimental import pallas as pl
from jax.experimental.pallas import tpu as pltpu


MESH = pl.DeviceIdType.MESH


def correlate_into(src, taps, bias, o_ref, first_row, count, col_tiles, block=8):
    block = min(block, count)
    steps = -(-count // block)
    chans = o_ref.shape[-1]

    def step(i, carry):
        r0 = first_row + jnp.minimum(i * block, count - block)
        for c0 in col_tiles:
            acc = jnp.broadcast_to(bias, (block, 8, chans))
            for col_tap in range(7):
                window = src[pl.ds(r0, block + 6), pl.ds(c0 + col_tap, 8), :]
                for row_tap in range(7):
                    acc = acc + taps[row_tap * 7 + col_tap] * window[row_tap : row_tap + block]
            o_ref[pl.ds(r0, block), pl.ds(c0, 8), :] = acc
        return carry

    lax.fori_loop(0, steps, step, 0)


def halo_correlate(block, fold_src, taps, fold_taps, bias, north_fold, collective):
    rows, cols, chans = block.shape
    nlat, nlon = lax.axis_size("lat"), lax.axis_size("lon")
    fold_back = fold_taps is not None

    def run(x_ref, f_ref, k_ref, kf_ref, b_ref, o_ref, pad, gf, send, recv, local, folds):
        band = lax.axis_index("lat")
        lon = lax.axis_index("lon")
        has_south = band > 0
        has_north = band < nlat - 1
        top = band == nlat - 1
        west = lax.rem(lon + nlon - 1, nlon)
        east = lax.rem(lon + 1, nlon)
        fold_dst = gf if fold_back else pad
        fold_row = 6 if fold_back else rows + 3
        hi = pl.ds(rows - 3, 3)
        lo = pl.ds(0, 3)
        allr = pl.ds(0, rows)
        c_lo, c_hi, c_all = pl.ds(0, 3), pl.ds(cols - 3, 3), pl.ds(0, cols)
        d_w, d_mid, d_e = pl.ds(0, 3), pl.ds(3, cols), pl.ds(cols + 3, 3)
        messages = [
            (x_ref.at[hi, c_all], pad.at[pl.ds(0, 3), d_mid], (lon, band + 1), has_north, has_south),
            (x_ref.at[hi, c_hi], pad.at[pl.ds(0, 3), d_w], (east, band + 1), has_north, has_south),
            (x_ref.at[hi, c_lo], pad.at[pl.ds(0, 3), d_e], (west, band + 1), has_north, has_south),
            (x_ref.at[lo, c_all], pad.at[pl.ds(rows + 3, 3), d_mid], (lon, band - 1), has_south, has_north),
            (x_ref.at[lo, c_hi], pad.at[pl.ds(rows + 3, 3), d_w], (east, band - 1), has_south, has_north),
            (x_ref.at[lo, c_lo], pad.at[pl.ds(rows + 3, 3), d_e], (west, band - 1), has_south, has_north),
            (x_ref.at[allr, c_hi], pad.at[pl.ds(3, rows), d_w], (east, band), None, None),
            (x_ref.at[allr, c_lo], pad.at[pl.ds(3, rows), d_e], (west, band), None, None),
            (f_ref.at[:, c_all], fold_dst.at[pl.ds(fold_row, 3), d_mid], (nlon - 1 - lon, band), top, top),
            (f_ref.at[:, c_hi], fold_dst.at[pl.ds(fold_row, 3), d_w], (lax.rem(2 * nlon - lon, nlon), band), top, top),
            (f_ref.at[:, c_lo], fold_dst.at[pl.ds(fold_row, 3), d_e], (lax.rem(2 * nlon - 2 - lon, nlon), band), top, top),
        ]
        sources = [
            (lon, band - 1), (west, band - 1), (east, band - 1),
            (lon, band + 1), (west, band + 1), (east, band + 1),
            (west, band), (east, band),
        ]
        for i in (9, 10):
            src, dst, target, _, _ = messages[i]
            apart = jnp.logical_and(top, target[0] != lon)
            messages[i] = (src, dst, target, apart, apart)
        sources += [messages[8][2], messages[9][2], messages[10][2]]
        own = [
            (pltpu.make_async_copy(messages[i][0], messages[i][1], folds.at[j]),
             jnp.logical_and(top, messages[i][2][0] == lon))
            for j, i in enumerate((9, 10))
        ]
        for copy, cond in own:
            pl.when(cond)(copy.start)

        interior = pltpu.make_async_copy(x_ref, pad.at[pl.ds(3, rows), pl.ds(3, cols)], local)
        interior.start()

        @pl.when(band == 0)
        def _():
            pad[pl.ds(0, 3)] = jnp.zeros((3, cols + 6, chans), jnp.float32)

        if not north_fold:
            @pl.when(top)
            def _():
                pad[pl.ds(rows + 3, 3)] = jnp.zeros((3, cols + 6, chans), jnp.float32)

        if fold_back:
            gf[pl.ds(0, 6)] = jnp.zeros((6, cols + 6, chans), jnp.float32)

            @pl.when(jnp.logical_not(top))
            def _():
                gf[pl.ds(6, 3)] = jnp.zeros((3, cols + 6, chans), jnp.float32)

        barrier = pltpu.get_barrier_semaphore()

        def when(cond, fn):
            if cond is None:
                fn()
            else:
                pl.when(cond)(fn)

        for (src, dst, target, s_cond, r_cond), source in zip(messages, sources):
            def greet_target(target=target):
                pl.semaphore_signal(barrier, 1, device_id=target, device_id_type=MESH)

            def greet_source(source=source):
                pl.semaphore_signal(barrier, 1, device_id=source, device_id_type=MESH)

            when(s_cond, greet_target)
            when(r_cond, greet_source)
        interior.wait()
        inner_tiles = tuple(range(8, cols - 8, 8))
        bias_row = b_ref[...]
        correlate_into(pad, k_ref, bias_row, o_ref, 3, rows - 6, inner_tiles)

        edge = has_north.astype(jnp.int32) + has_south.astype(jnp.int32)
        folded = top.astype(jnp.int32) + sum(messages[i][3].astype(jnp.int32) for i in (9, 10))
        expected = 2 * (3 * edge + 2 + folded)
        pl.semaphore_wait(barrier, expected)

        copies = []
        for i, (src, dst, target, s_cond, r_cond) in enumerate(messages):
            copy = pltpu.make_async_remote_copy(
                src_ref=src,
                dst_ref=dst,
                send_sem=send.at[i],
                recv_sem=recv.at[i],
                device_id=target,
                device_id_type=MESH,
            )
            copies.append(copy)
            when(s_cond, copy.start)
        for copy, (src, dst, target, s_cond, r_cond) in zip(copies, messages):
            when(s_cond, copy.wait_send)
            when(r_cond, copy.wait_recv)
        for copy, cond in own:
            pl.when(cond)(copy.wait)

        outer_tiles = (0, cols - 8)
        correlate_into(pad, k_ref, bias_row, o_ref, 0, rows, outer_tiles)
        correlate_into(pad, k_ref, bias_row, o_ref, 0, 3, inner_tiles)
        correlate_into(pad, k_ref, bias_row, o_ref, rows - 3, 3, inner_tiles)
        if fold_back:
            extra = jnp.zeros((3, cols, chans), jnp.float32)
            for row_tap in range(7):
                for col_tap in range(7):
                    window = gf[pl.ds(row_tap, 3), pl.ds(col_tap, cols), :]
                    extra = extra + kf_ref[row_tap * 7 + col_tap] * window
            o_ref[pl.ds(rows - 3, 3)] = o_ref[pl.ds(rows - 3, 3)] + extra

    taps = taps.astype(jnp.float32).reshape(49, 1, chans)
    if fold_taps is None:
        fold_taps = taps
    else:
        fold_taps = fold_taps.astype(jnp.float32).reshape(49, 1, chans)
    return pl.pallas_call(
        run,
        out_shape=jax.ShapeDtypeStruct((rows, cols, chans), jnp.float32),
        in_specs=[pl.BlockSpec(memory_space=pltpu.VMEM)] * 5,
        out_specs=pl.BlockSpec(memory_space=pltpu.VMEM),
        scratch_shapes=[
            pltpu.VMEM((rows + 6, cols + 6, chans), jnp.float32),
            pltpu.VMEM((9, cols + 6, chans), jnp.float32),
            pltpu.SemaphoreType.DMA((11,)),
            pltpu.SemaphoreType.DMA((11,)),
            pltpu.SemaphoreType.DMA,
            pltpu.SemaphoreType.DMA((2,)),
        ],
        compiler_params=pltpu.CompilerParams(collective_id=collective, has_side_effects=True),
    )(block, fold_src, taps, fold_taps, bias.reshape(1, chans))


def gelu_value(values):
    return 0.5 * values * (1.0 + lax.erf(values * 0.7071067811865476))


def gelu_slope(values):
    cumulative = 0.5 * (1.0 + lax.erf(values * 0.7071067811865476))
    return cumulative + values * jnp.exp(-0.5 * values * values) * 0.3989422804014327


def pointwise(
    conv_out,
    ocean_state,
    keep_mask,
    cotangent,
    norm_gain,
    norm_bias,
    w_expand,
    b_expand,
    w_reduce,
    b_reduce,
    layer_scale,
    tile=512,
):
    cells, chans = conv_out.shape
    hidden_size = w_expand.shape[1]
    tile = min(tile, cells)
    contract_last = (((1,), (1,)), ((), ()))

    def run(c_ref, s_ref, m_ref, t_ref, g_ref, nb_ref, we_ref, be_ref, wr_ref, br_ref, ls_ref, r_ref, o_ref):
        conv = c_ref[...]
        keep = m_ref[...]
        gain = g_ref[...]
        scale = ls_ref[...]
        row_mean = jnp.mean(conv, axis=-1, keepdims=True)
        centered = conv - row_mean
        inv_std = lax.rsqrt(jnp.mean(centered * centered, axis=-1, keepdims=True) + 1e-06)
        normal_hat = centered * inv_std
        normed = (normal_hat * gain + nb_ref[...]).astype(jnp.bfloat16)
        hidden = jnp.dot(normed, we_ref[...], preferred_element_type=jnp.float32) + be_ref[...]
        erf_term = lax.erf(hidden * 0.7071067811865476)
        activated = (0.5 * hidden * (1.0 + erf_term)).astype(jnp.bfloat16)
        projected = jnp.dot(activated, wr_ref[...], preferred_element_type=jnp.float32) + br_ref[...]
        r_ref[...] = (keep * (s_ref[...].astype(jnp.float32) + scale * projected)).astype(r_ref.dtype)
        grad_out = (keep * scale * t_ref[...].astype(jnp.float32)).astype(jnp.bfloat16)
        grad_act = lax.dot_general(
            grad_out, wr_ref[...], contract_last, preferred_element_type=jnp.float32
        )
        slope = 0.5 * (1.0 + erf_term) + hidden * jnp.exp(-0.5 * hidden * hidden) * 0.3989422804014327
        grad_hidden = (grad_act * slope).astype(jnp.bfloat16)
        grad_normed = lax.dot_general(
            grad_hidden, we_ref[...], contract_last, preferred_element_type=jnp.float32
        )
        grad_scaled = grad_normed * gain
        o_ref[...] = inv_std * (
            grad_scaled
            - jnp.mean(grad_scaled, axis=-1, keepdims=True)
            - normal_hat * jnp.mean(grad_scaled * normal_hat, axis=-1, keepdims=True)
        )

    rows = lambda width: pl.BlockSpec((tile, width), lambda i: (i, 0))
    whole = lambda shape: pl.BlockSpec(shape, lambda i: (0, 0))
    vec = lambda v: v.reshape(1, -1)
    return pl.pallas_call(
        run,
        grid=(cells // tile,),
        out_shape=(
            jax.ShapeDtypeStruct((cells, chans), jnp.bfloat16),
            jax.ShapeDtypeStruct((cells, chans), jnp.float32),
        ),
        in_specs=[
            rows(chans), rows(chans), rows(1), rows(chans),
            whole((1, chans)), whole((1, chans)),
            whole((chans, hidden_size)), whole((1, hidden_size)),
            whole((hidden_size, chans)), whole((1, chans)), whole((1, chans)),
        ],
        out_specs=(rows(chans), rows(chans)),
    )(
        conv_out, ocean_state, keep_mask, cotangent, vec(norm_gain), vec(norm_bias),
        w_expand, vec(b_expand), w_reduce, vec(b_reduce), vec(layer_scale),
    )


def body(
    ocean_state,
    land_sea,
    kernel,
    conv_bias,
    norm_gain,
    norm_bias,
    w_expand,
    b_expand,
    w_reduce,
    b_reduce,
    layer_scale,
    cotangent,
):
    band_rows, band_cols, channels = ocean_state.shape
    keep_mask = land_sea.astype(jnp.float32)[:, :, None]
    masked = (ocean_state.astype(jnp.float32) * keep_mask).astype(jnp.bfloat16)

    masked32 = masked.astype(jnp.float32)
    top_rows = masked32[band_rows - 3 :][::-1, ::-1]
    conv_out = halo_correlate(masked32, top_rows, kernel, None, conv_bias, True, 0)
    cell_count = band_rows * band_cols
    result, conv_grad = pointwise(
        conv_out.reshape(cell_count, channels),
        ocean_state.reshape(cell_count, channels),
        keep_mask.reshape(cell_count, 1),
        cotangent.reshape(cell_count, channels),
        norm_gain,
        norm_bias,
        w_expand,
        b_expand,
        w_reduce,
        b_reduce,
        layer_scale,
    )
    conv_grad = conv_grad.reshape(band_rows, band_cols, channels)

    grad_top = conv_grad[band_rows - 3 :][::-1, ::-1]
    zero_bias = jnp.zeros((channels,), jnp.float32)
    masked_grad = halo_correlate(
        conv_grad, grad_top, kernel[::-1, ::-1], kernel, zero_bias, False, 1
    )
    state_grad = (keep_mask * (cotangent.astype(jnp.float32) + masked_grad)).astype(jnp.bfloat16)
    return (result.reshape(band_rows, band_cols, channels), state_grad)


def solution(mesh):
    placed = (
        P("lat", "lon", None),
        P("lat", "lon"),
        P(),
        P(),
        P(),
        P(),
        P(),
        P(),
        P(),
        P(),
        P(),
        P("lat", "lon", None),
    )
    return jax.shard_map(
        body,
        mesh=mesh,
        in_specs=placed,
        out_specs=(P("lat", "lon", None), P("lat", "lon", None)),
        check_vma=False,
    )
```

```python
import jax
import jax.numpy as jnp
from jax import lax
from jax.sharding import PartitionSpec as P
from jax.experimental import pallas as pl
from jax.experimental.pallas import tpu as pltpu


MESH = pl.DeviceIdType.MESH


def correlate_into(src, taps, bias, o_ref, first_row, count, col_tiles, block=8):
    block = min(block, count)
    steps = -(-count // block)
    chans = o_ref.shape[-1]

    def step(i, carry):
        r0 = first_row + jnp.minimum(i * block, count - block)
        for c0 in col_tiles:
            acc = jnp.broadcast_to(bias, (block, 8, chans))
            for col_tap in range(7):
                window = src[pl.ds(r0, block + 6), pl.ds(c0 + col_tap, 8), :]
                for row_tap in range(7):
                    acc = acc + taps[row_tap * 7 + col_tap] * window[row_tap : row_tap + block]
            o_ref[pl.ds(r0, block), pl.ds(c0, 8), :] = acc
        return carry

    lax.fori_loop(0, steps, step, 0)


def halo_correlate(block, fold_src, kernel, bias, north_fold, collective, tail=None):
    rows, cols, chans = block.shape
    nlat, nlon = lax.axis_size("lat"), lax.axis_size("lon")
    fold_back = tail is not None

    def run(*refs):
        if fold_back:
            x_ref, f_ref, kw_ref, t_ref, m_ref, o_ref, pad, gf, k_ref, acc_ref, send, recv, local, folds = refs
        else:
            x_ref, f_ref, kw_ref, b_ref, o_ref, pad, gf, k_ref, acc_ref, send, recv, local, folds = refs
            acc_ref = o_ref
        band = lax.axis_index("lat")
        lon = lax.axis_index("lon")
        has_south = band > 0
        has_north = band < nlat - 1
        top = band == nlat - 1
        west = lax.rem(lon + nlon - 1, nlon)
        east = lax.rem(lon + 1, nlon)
        fold_dst = gf if fold_back else pad
        fold_row = 6 if fold_back else rows + 3
        hi = pl.ds(rows - 3, 3)
        lo = pl.ds(0, 3)
        allr = pl.ds(0, rows)
        c_lo, c_hi, c_all = pl.ds(0, 3), pl.ds(cols - 3, 3), pl.ds(0, cols)
        d_w, d_mid, d_e = pl.ds(0, 3), pl.ds(3, cols), pl.ds(cols + 3, 3)
        messages = [
            (x_ref.at[hi, c_all], pad.at[pl.ds(0, 3), d_mid], (lon, band + 1), has_north, has_south),
            (x_ref.at[hi, c_hi], pad.at[pl.ds(0, 3), d_w], (east, band + 1), has_north, has_south),
            (x_ref.at[hi, c_lo], pad.at[pl.ds(0, 3), d_e], (west, band + 1), has_north, has_south),
            (x_ref.at[lo, c_all], pad.at[pl.ds(rows + 3, 3), d_mid], (lon, band - 1), has_south, has_north),
            (x_ref.at[lo, c_hi], pad.at[pl.ds(rows + 3, 3), d_w], (east, band - 1), has_south, has_north),
            (x_ref.at[lo, c_lo], pad.at[pl.ds(rows + 3, 3), d_e], (west, band - 1), has_south, has_north),
            (x_ref.at[allr, c_hi], pad.at[pl.ds(3, rows), d_w], (east, band), None, None),
            (x_ref.at[allr, c_lo], pad.at[pl.ds(3, rows), d_e], (west, band), None, None),
            (f_ref.at[:, c_all], fold_dst.at[pl.ds(fold_row, 3), d_mid], (nlon - 1 - lon, band), top, top),
            (f_ref.at[:, c_hi], fold_dst.at[pl.ds(fold_row, 3), d_w], (lax.rem(2 * nlon - lon, nlon), band), top, top),
            (f_ref.at[:, c_lo], fold_dst.at[pl.ds(fold_row, 3), d_e], (lax.rem(2 * nlon - 2 - lon, nlon), band), top, top),
        ]
        sources = [
            (lon, band - 1), (west, band - 1), (east, band - 1),
            (lon, band + 1), (west, band + 1), (east, band + 1),
            (west, band), (east, band),
        ]
        for i in (9, 10):
            src, dst, target, _, _ = messages[i]
            apart = jnp.logical_and(top, target[0] != lon)
            messages[i] = (src, dst, target, apart, apart)
        sources += [messages[8][2], messages[9][2], messages[10][2]]
        own = [
            (pltpu.make_async_copy(messages[i][0], messages[i][1], folds.at[j]),
             jnp.logical_and(top, messages[i][2][0] == lon))
            for j, i in enumerate((9, 10))
        ]
        for copy, cond in own:
            pl.when(cond)(copy.start)

        interior = pltpu.make_async_copy(x_ref, pad.at[pl.ds(3, rows), pl.ds(3, cols)], local)
        interior.start()

        @pl.when(band == 0)
        def _():
            pad[pl.ds(0, 3)] = jnp.zeros((3, cols + 6, chans), jnp.float32)

        if not north_fold:
            @pl.when(top)
            def _():
                pad[pl.ds(rows + 3, 3)] = jnp.zeros((3, cols + 6, chans), jnp.float32)

        if fold_back:
            gf[pl.ds(0, 6)] = jnp.zeros((6, cols + 6, chans), jnp.float32)

            @pl.when(jnp.logical_not(top))
            def _():
                gf[pl.ds(6, 3)] = jnp.zeros((3, cols + 6, chans), jnp.float32)

        barrier = pltpu.get_barrier_semaphore()

        def when(cond, fn):
            if cond is None:
                fn()
            else:
                pl.when(cond)(fn)

        for (src, dst, target, s_cond, r_cond), source in zip(messages, sources):
            def greet_target(target=target):
                pl.semaphore_signal(barrier, 1, device_id=target, device_id_type=MESH)

            def greet_source(source=source):
                pl.semaphore_signal(barrier, 1, device_id=source, device_id_type=MESH)

            when(s_cond, greet_target)
            when(r_cond, greet_source)
        for row_tap in range(7):
            for col_tap in range(7):
                a, b = (6 - row_tap, 6 - col_tap) if fold_back else (row_tap, col_tap)
                k_ref[row_tap * 7 + col_tap] = kw_ref[a, pl.ds(b, 1), :].astype(jnp.float32)
        if fold_back:
            bias_row = jnp.zeros((1, chans), jnp.float32)
        else:
            bias_row = b_ref[...]

        interior.wait()
        inner_tiles = tuple(range(8, cols - 8, 8))
        correlate_into(pad, k_ref, bias_row, acc_ref, 3, rows - 6, inner_tiles)

        edge = has_north.astype(jnp.int32) + has_south.astype(jnp.int32)
        folded = top.astype(jnp.int32) + sum(messages[i][3].astype(jnp.int32) for i in (9, 10))
        expected = 2 * (3 * edge + 2 + folded)
        pl.semaphore_wait(barrier, expected)

        copies = []
        for i, (src, dst, target, s_cond, r_cond) in enumerate(messages):
            copy = pltpu.make_async_remote_copy(
                src_ref=src,
                dst_ref=dst,
                send_sem=send.at[i],
                recv_sem=recv.at[i],
                device_id=target,
                device_id_type=MESH,
            )
            copies.append(copy)
            when(s_cond, copy.start)
        for copy, (src, dst, target, s_cond, r_cond) in zip(copies, messages):
            when(s_cond, copy.wait_send)
            when(r_cond, copy.wait_recv)
        for copy, cond in own:
            pl.when(cond)(copy.wait)

        outer_tiles = (0, cols - 8)
        correlate_into(pad, k_ref, bias_row, acc_ref, 0, rows, outer_tiles)
        correlate_into(pad, k_ref, bias_row, acc_ref, 0, 3, inner_tiles)
        correlate_into(pad, k_ref, bias_row, acc_ref, rows - 3, 3, inner_tiles)
        if fold_back:
            extra = jnp.zeros((3, cols, chans), jnp.float32)
            for row_tap in range(7):
                for col_tap in range(7):
                    window = gf[pl.ds(row_tap, 3), pl.ds(col_tap, cols), :]
                    tap = kw_ref[row_tap, pl.ds(col_tap, 1), :].astype(jnp.float32)
                    extra = extra + tap * window
            acc_ref[pl.ds(rows - 3, 3)] = acc_ref[pl.ds(rows - 3, 3)] + extra
            step = 8 if rows % 8 == 0 else rows

            def finish(i, carry):
                at = pl.ds(i * step, step)
                total = t_ref[at].astype(jnp.float32) + acc_ref[at]
                o_ref[at] = (m_ref[at].astype(jnp.float32) * total).astype(o_ref.dtype)
                return carry

            lax.fori_loop(0, rows // step, finish, 0)

    if fold_back:
        cotangent, keep = tail
        operands = (block, fold_src, kernel, cotangent, keep)
    else:
        operands = (block, fold_src, kernel, bias.reshape(1, chans))
    return pl.pallas_call(
        run,
        out_shape=jax.ShapeDtypeStruct(
            (rows, cols, chans), jnp.bfloat16 if fold_back else jnp.float32
        ),
        in_specs=[pl.BlockSpec(memory_space=pltpu.VMEM)] * len(operands),
        out_specs=pl.BlockSpec(memory_space=pltpu.VMEM),
        scratch_shapes=[
            pltpu.VMEM((rows + 6, cols + 6, chans), jnp.float32),
            pltpu.VMEM((9, cols + 6, chans), jnp.float32),
            pltpu.VMEM((49, 1, chans), jnp.float32),
            pltpu.VMEM((rows, cols, chans) if fold_back else (8, 128), jnp.float32),
            pltpu.SemaphoreType.DMA((11,)),
            pltpu.SemaphoreType.DMA((11,)),
            pltpu.SemaphoreType.DMA,
            pltpu.SemaphoreType.DMA((2,)),
        ],
        compiler_params=pltpu.CompilerParams(collective_id=collective, has_side_effects=True),
    )(*operands)


def gelu_value(values):
    return 0.5 * values * (1.0 + lax.erf(values * 0.7071067811865476))


def gelu_slope(values):
    cumulative = 0.5 * (1.0 + lax.erf(values * 0.7071067811865476))
    return cumulative + values * jnp.exp(-0.5 * values * values) * 0.3989422804014327


def pointwise(
    conv_out,
    ocean_state,
    keep_mask,
    cotangent,
    norm_gain,
    norm_bias,
    w_expand,
    b_expand,
    w_reduce,
    b_reduce,
    layer_scale,
    tile=512,
):
    cells, chans = conv_out.shape
    hidden_size = w_expand.shape[1]
    tile = min(tile, cells)
    contract_last = (((1,), (1,)), ((), ()))

    def run(c_ref, s_ref, m_ref, t_ref, g_ref, nb_ref, we_ref, be_ref, wr_ref, br_ref, ls_ref, r_ref, o_ref):
        conv = c_ref[...]
        keep = m_ref[...].astype(jnp.float32)
        gain = g_ref[...]
        scale = ls_ref[...]
        row_mean = jnp.mean(conv, axis=-1, keepdims=True)
        centered = conv - row_mean
        inv_std = lax.rsqrt(jnp.mean(centered * centered, axis=-1, keepdims=True) + 1e-06)
        normal_hat = centered * inv_std
        normed = (normal_hat * gain + nb_ref[...]).astype(jnp.bfloat16)
        hidden = jnp.dot(normed, we_ref[...], preferred_element_type=jnp.float32) + be_ref[...]
        erf_term = lax.erf(hidden * 0.7071067811865476)
        activated = (0.5 * hidden * (1.0 + erf_term)).astype(jnp.bfloat16)
        projected = jnp.dot(activated, wr_ref[...], preferred_element_type=jnp.float32) + br_ref[...]
        r_ref[...] = (keep * (s_ref[...].astype(jnp.float32) + scale * projected)).astype(r_ref.dtype)
        grad_out = (keep * scale * t_ref[...].astype(jnp.float32)).astype(jnp.bfloat16)
        grad_act = lax.dot_general(
            grad_out, wr_ref[...], contract_last, preferred_element_type=jnp.float32
        )
        slope = 0.5 * (1.0 + erf_term) + hidden * jnp.exp(-0.5 * hidden * hidden) * 0.3989422804014327
        grad_hidden = (grad_act * slope).astype(jnp.bfloat16)
        grad_normed = lax.dot_general(
            grad_hidden, we_ref[...], contract_last, preferred_element_type=jnp.float32
        )
        grad_scaled = grad_normed * gain
        o_ref[...] = inv_std * (
            grad_scaled
            - jnp.mean(grad_scaled, axis=-1, keepdims=True)
            - normal_hat * jnp.mean(grad_scaled * normal_hat, axis=-1, keepdims=True)
        )

    rows = lambda width: pl.BlockSpec((tile, width), lambda i: (i, 0))
    whole = lambda shape: pl.BlockSpec(shape, lambda i: (0, 0))
    vec = lambda v: v.reshape(1, -1)
    return pl.pallas_call(
        run,
        grid=(cells // tile,),
        out_shape=(
            jax.ShapeDtypeStruct((cells, chans), jnp.bfloat16),
            jax.ShapeDtypeStruct((cells, chans), jnp.float32),
        ),
        in_specs=[
            rows(chans), rows(chans), rows(chans), rows(chans),
            whole((1, chans)), whole((1, chans)),
            whole((chans, hidden_size)), whole((1, hidden_size)),
            whole((hidden_size, chans)), whole((1, chans)), whole((1, chans)),
        ],
        out_specs=(rows(chans), rows(chans)),
    )(
        conv_out, ocean_state, keep_mask, cotangent, vec(norm_gain), vec(norm_bias),
        w_expand, vec(b_expand), w_reduce, vec(b_reduce), vec(layer_scale),
    )


def body(
    ocean_state,
    land_sea,
    kernel,
    conv_bias,
    norm_gain,
    norm_bias,
    w_expand,
    b_expand,
    w_reduce,
    b_reduce,
    layer_scale,
    cotangent,
):
    band_rows, band_cols, channels = ocean_state.shape
    keep_mask = land_sea.astype(jnp.float32)[:, :, None]
    masked32 = ocean_state.astype(jnp.float32) * keep_mask
    keep_wide = jnp.broadcast_to(keep_mask, ocean_state.shape).astype(jnp.bfloat16)
    top_rows = masked32[band_rows - 3 :][::-1, ::-1]
    conv_out = halo_correlate(masked32, top_rows, kernel, conv_bias, True, 0)
    cell_count = band_rows * band_cols
    result, conv_grad = pointwise(
        conv_out.reshape(cell_count, channels),
        ocean_state.reshape(cell_count, channels),
        keep_wide.reshape(cell_count, channels),
        cotangent.reshape(cell_count, channels),
        norm_gain,
        norm_bias,
        w_expand,
        b_expand,
        w_reduce,
        b_reduce,
        layer_scale,
    )
    conv_grad = conv_grad.reshape(band_rows, band_cols, channels)

    grad_top = conv_grad[band_rows - 3 :][::-1, ::-1]
    state_grad = halo_correlate(
        conv_grad, grad_top, kernel, None, False, 1, (cotangent, keep_wide)
    )
    return (result.reshape(band_rows, band_cols, channels), state_grad)


def solution(mesh):
    placed = (
        P("lat", "lon", None),
        P("lat", "lon"),
        P(),
        P(),
        P(),
        P(),
        P(),
        P(),
        P(),
        P(),
        P(),
        P("lat", "lon", None),
    )
    return jax.shard_map(
        body,
        mesh=mesh,
        in_specs=placed,
        out_specs=(P("lat", "lon", None), P("lat", "lon", None)),
        check_vma=False,
    )
```

```python
import jax
import jax.numpy as jnp
from jax import lax
from jax.sharding import PartitionSpec as P
from jax.experimental import pallas as pl
from jax.experimental.pallas import tpu as pltpu


MESH = pl.DeviceIdType.MESH


def correlate_into(src, taps, bias, o_ref, first_row, count, col_tiles, block=8):
    block = min(block, count)
    steps = -(-count // block)
    chans = o_ref.shape[-1]

    def step(i, carry):
        r0 = first_row + jnp.minimum(i * block, count - block)
        for c0 in col_tiles:
            acc = jnp.broadcast_to(bias, (block, 8, chans))
            for col_tap in range(7):
                window = src[pl.ds(r0, block + 6), pl.ds(c0 + col_tap, 8), :]
                for row_tap in range(7):
                    acc = acc + taps[row_tap * 7 + col_tap] * window[row_tap : row_tap + block]
            o_ref[pl.ds(r0, block), pl.ds(c0, 8), :] = acc
        return carry

    lax.fori_loop(0, steps, step, 0)


def halo_correlate(block, fold_src, kernel, bias, north_fold, collective, tail=None):
    rows, cols, chans = block.shape
    nlat, nlon = lax.axis_size("lat"), lax.axis_size("lon")
    fold_back = tail is not None

    def run(*refs):
        if fold_back:
            x_ref, f_ref, kw_ref, t_ref, m_ref, o_ref, pad, gf, k_ref, acc_ref, send, recv, local, folds = refs
        else:
            x_ref, f_ref, kw_ref, b_ref, o_ref, pad, gf, k_ref, acc_ref, send, recv, local, folds = refs
            acc_ref = o_ref
        band = lax.axis_index("lat")
        lon = lax.axis_index("lon")
        has_south = band > 0
        has_north = band < nlat - 1
        top = band == nlat - 1
        west = lax.rem(lon + nlon - 1, nlon)
        east = lax.rem(lon + 1, nlon)
        fold_dst = gf if fold_back else pad
        fold_row = 6 if fold_back else rows + 3
        hi = pl.ds(rows - 3, 3)
        lo = pl.ds(0, 3)
        allr = pl.ds(0, rows)
        c_lo, c_hi, c_all = pl.ds(0, 3), pl.ds(cols - 3, 3), pl.ds(0, cols)
        d_w, d_mid, d_e = pl.ds(0, 3), pl.ds(3, cols), pl.ds(cols + 3, 3)
        messages = [
            (x_ref.at[hi, c_all], pad.at[pl.ds(0, 3), d_mid], (lon, band + 1), has_north, has_south),
            (x_ref.at[hi, c_hi], pad.at[pl.ds(0, 3), d_w], (east, band + 1), has_north, has_south),
            (x_ref.at[hi, c_lo], pad.at[pl.ds(0, 3), d_e], (west, band + 1), has_north, has_south),
            (x_ref.at[lo, c_all], pad.at[pl.ds(rows + 3, 3), d_mid], (lon, band - 1), has_south, has_north),
            (x_ref.at[lo, c_hi], pad.at[pl.ds(rows + 3, 3), d_w], (east, band - 1), has_south, has_north),
            (x_ref.at[lo, c_lo], pad.at[pl.ds(rows + 3, 3), d_e], (west, band - 1), has_south, has_north),
            (x_ref.at[allr, c_hi], pad.at[pl.ds(3, rows), d_w], (east, band), None, None),
            (x_ref.at[allr, c_lo], pad.at[pl.ds(3, rows), d_e], (west, band), None, None),
            (f_ref.at[:, c_all], fold_dst.at[pl.ds(fold_row, 3), d_mid], (nlon - 1 - lon, band), top, top),
            (f_ref.at[:, c_hi], fold_dst.at[pl.ds(fold_row, 3), d_w], (lax.rem(2 * nlon - lon, nlon), band), top, top),
            (f_ref.at[:, c_lo], fold_dst.at[pl.ds(fold_row, 3), d_e], (lax.rem(2 * nlon - 2 - lon, nlon), band), top, top),
        ]
        sources = [
            (lon, band - 1), (west, band - 1), (east, band - 1),
            (lon, band + 1), (west, band + 1), (east, band + 1),
            (west, band), (east, band),
        ]
        for i in (9, 10):
            src, dst, target, _, _ = messages[i]
            apart = jnp.logical_and(top, target[0] != lon)
            messages[i] = (src, dst, target, apart, apart)
        sources += [messages[8][2], messages[9][2], messages[10][2]]
        own = [
            (pltpu.make_async_copy(messages[i][0], messages[i][1], folds.at[j]),
             jnp.logical_and(top, messages[i][2][0] == lon))
            for j, i in enumerate((9, 10))
        ]
        for copy, cond in own:
            pl.when(cond)(copy.start)

        interior = pltpu.make_async_copy(x_ref, pad.at[pl.ds(3, rows), pl.ds(3, cols)], local)
        interior.start()

        @pl.when(band == 0)
        def _():
            pad[pl.ds(0, 3)] = jnp.zeros((3, cols + 6, chans), jnp.float32)

        if not north_fold:
            @pl.when(top)
            def _():
                pad[pl.ds(rows + 3, 3)] = jnp.zeros((3, cols + 6, chans), jnp.float32)

        if fold_back:
            gf[pl.ds(0, 6)] = jnp.zeros((6, cols + 6, chans), jnp.float32)

            @pl.when(jnp.logical_not(top))
            def _():
                gf[pl.ds(6, 3)] = jnp.zeros((3, cols + 6, chans), jnp.float32)

        barrier = pltpu.get_barrier_semaphore()

        def when(cond, fn):
            if cond is None:
                fn()
            else:
                pl.when(cond)(fn)

        for (src, dst, target, s_cond, r_cond), source in zip(messages, sources):
            def greet_target(target=target):
                pl.semaphore_signal(barrier, 1, device_id=target, device_id_type=MESH)

            def greet_source(source=source):
                pl.semaphore_signal(barrier, 1, device_id=source, device_id_type=MESH)

            when(s_cond, greet_target)
            when(r_cond, greet_source)
        for row_tap in range(7):
            for col_tap in range(7):
                a, b = (6 - row_tap, 6 - col_tap) if fold_back else (row_tap, col_tap)
                k_ref[row_tap * 7 + col_tap] = kw_ref[a, pl.ds(b, 1), :].astype(jnp.float32)
        if fold_back:
            bias_row = jnp.zeros((1, chans), jnp.float32)
        else:
            bias_row = b_ref[...]

        interior.wait()
        inner_tiles = tuple(range(8, cols - 8, 8))
        correlate_into(pad, k_ref, bias_row, acc_ref, 3, rows - 6, inner_tiles)

        edge = has_north.astype(jnp.int32) + has_south.astype(jnp.int32)
        folded = top.astype(jnp.int32) + sum(messages[i][3].astype(jnp.int32) for i in (9, 10))
        expected = 2 * (3 * edge + 2 + folded)
        pl.semaphore_wait(barrier, expected)

        copies = []
        for i, (src, dst, target, s_cond, r_cond) in enumerate(messages):
            copy = pltpu.make_async_remote_copy(
                src_ref=src,
                dst_ref=dst,
                send_sem=send.at[i],
                recv_sem=recv.at[i],
                device_id=target,
                device_id_type=MESH,
            )
            copies.append(copy)
            when(s_cond, copy.start)
        for copy, (src, dst, target, s_cond, r_cond) in zip(copies, messages):
            when(s_cond, copy.wait_send)
            when(r_cond, copy.wait_recv)
        for copy, cond in own:
            pl.when(cond)(copy.wait)

        outer_tiles = (0, cols - 8)
        correlate_into(pad, k_ref, bias_row, acc_ref, 0, rows, outer_tiles)
        correlate_into(pad, k_ref, bias_row, acc_ref, 0, 3, inner_tiles)
        correlate_into(pad, k_ref, bias_row, acc_ref, rows - 3, 3, inner_tiles)
        if fold_back:
            extra = jnp.zeros((3, cols, chans), jnp.float32)
            for row_tap in range(7):
                for col_tap in range(7):
                    window = gf[pl.ds(row_tap, 3), pl.ds(col_tap, cols), :]
                    tap = kw_ref[row_tap, pl.ds(col_tap, 1), :].astype(jnp.float32)
                    extra = extra + tap * window
            acc_ref[pl.ds(rows - 3, 3)] = acc_ref[pl.ds(rows - 3, 3)] + extra
            step = 8 if rows % 8 == 0 else rows

            def finish(i, carry):
                at = pl.ds(i * step, step)
                total = t_ref[at].astype(jnp.float32) + acc_ref[at]
                o_ref[at] = (m_ref[at].astype(jnp.float32) * total).astype(o_ref.dtype)
                return carry

            lax.fori_loop(0, rows // step, finish, 0)

    if fold_back:
        cotangent, keep = tail
        operands = (block, fold_src, kernel, cotangent, keep)
    else:
        operands = (block, fold_src, kernel, bias.reshape(1, chans))
    return pl.pallas_call(
        run,
        out_shape=jax.ShapeDtypeStruct(
            (rows, cols, chans), jnp.bfloat16 if fold_back else jnp.float32
        ),
        in_specs=[pl.BlockSpec(memory_space=pltpu.VMEM)] * len(operands),
        out_specs=pl.BlockSpec(memory_space=pltpu.VMEM),
        scratch_shapes=[
            pltpu.VMEM((rows + 6, cols + 6, chans), jnp.float32),
            pltpu.VMEM((9, cols + 6, chans), jnp.float32),
            pltpu.VMEM((49, 1, chans), jnp.float32),
            pltpu.VMEM((rows, cols, chans) if fold_back else (8, 128), jnp.float32),
            pltpu.SemaphoreType.DMA((11,)),
            pltpu.SemaphoreType.DMA((11,)),
            pltpu.SemaphoreType.DMA,
            pltpu.SemaphoreType.DMA((2,)),
        ],
        compiler_params=pltpu.CompilerParams(collective_id=collective, has_side_effects=True),
    )(*operands)


def gelu_value(values):
    return 0.5 * values * (1.0 + lax.erf(values * 0.7071067811865476))


def gelu_slope(values):
    cumulative = 0.5 * (1.0 + lax.erf(values * 0.7071067811865476))
    return cumulative + values * jnp.exp(-0.5 * values * values) * 0.3989422804014327


def pointwise(
    conv_out,
    ocean_state,
    keep_mask,
    cotangent,
    norm_gain,
    norm_bias,
    w_expand,
    b_expand,
    w_reduce,
    b_reduce,
    layer_scale,
    tile=16,
):
    band_rows, band_cols, chans = conv_out.shape
    cells = tile * band_cols
    hidden_size = w_expand.shape[1]
    tile = tile if band_rows % tile == 0 else band_rows
    cells = tile * band_cols
    contract_last = (((1,), (1,)), ((), ()))

    def run(c_ref, s_ref, m_ref, t_ref, g_ref, nb_ref, we_ref, be_ref, wr_ref, br_ref, ls_ref, r_ref, o_ref):
        flat = lambda ref: ref[...].reshape(cells, chans)
        conv = flat(c_ref)
        keep = flat(m_ref).astype(jnp.float32)
        gain = g_ref[...]
        scale = ls_ref[...]
        row_mean = jnp.mean(conv, axis=-1, keepdims=True)
        centered = conv - row_mean
        inv_std = lax.rsqrt(jnp.mean(centered * centered, axis=-1, keepdims=True) + 1e-06)
        normal_hat = centered * inv_std
        normed = (normal_hat * gain + nb_ref[...]).astype(jnp.bfloat16)
        hidden = jnp.dot(normed, we_ref[...], preferred_element_type=jnp.float32) + be_ref[...]
        erf_term = lax.erf(hidden * 0.7071067811865476)
        activated = (0.5 * hidden * (1.0 + erf_term)).astype(jnp.bfloat16)
        projected = jnp.dot(activated, wr_ref[...], preferred_element_type=jnp.float32) + br_ref[...]
        result = keep * (flat(s_ref).astype(jnp.float32) + scale * projected)
        r_ref[...] = result.astype(r_ref.dtype).reshape(tile, band_cols, chans)
        grad_out = (keep * scale * flat(t_ref).astype(jnp.float32)).astype(jnp.bfloat16)
        grad_act = lax.dot_general(
            grad_out, wr_ref[...], contract_last, preferred_element_type=jnp.float32
        )
        slope = 0.5 * (1.0 + erf_term) + hidden * jnp.exp(-0.5 * hidden * hidden) * 0.3989422804014327
        grad_hidden = (grad_act * slope).astype(jnp.bfloat16)
        grad_normed = lax.dot_general(
            grad_hidden, we_ref[...], contract_last, preferred_element_type=jnp.float32
        )
        grad_scaled = grad_normed * gain
        conv_grad = inv_std * (
            grad_scaled
            - jnp.mean(grad_scaled, axis=-1, keepdims=True)
            - normal_hat * jnp.mean(grad_scaled * normal_hat, axis=-1, keepdims=True)
        )
        o_ref[...] = conv_grad.reshape(tile, band_cols, chans)

    rows = lambda width: pl.BlockSpec((tile, band_cols, width), lambda i: (i, 0, 0))
    whole = lambda shape: pl.BlockSpec(shape, lambda i: (0, 0))
    vec = lambda v: v.reshape(1, -1)
    return pl.pallas_call(
        run,
        grid=(band_rows // tile,),
        out_shape=(
            jax.ShapeDtypeStruct(conv_out.shape, jnp.bfloat16),
            jax.ShapeDtypeStruct(conv_out.shape, jnp.float32),
        ),
        in_specs=[
            rows(chans), rows(chans), rows(chans), rows(chans),
            whole((1, chans)), whole((1, chans)),
            whole((chans, hidden_size)), whole((1, hidden_size)),
            whole((hidden_size, chans)), whole((1, chans)), whole((1, chans)),
        ],
        out_specs=(rows(chans), rows(chans)),
    )(
        conv_out, ocean_state, keep_mask, cotangent, vec(norm_gain), vec(norm_bias),
        w_expand, vec(b_expand), w_reduce, vec(b_reduce), vec(layer_scale),
    )


def body(
    ocean_state,
    land_sea,
    kernel,
    conv_bias,
    norm_gain,
    norm_bias,
    w_expand,
    b_expand,
    w_reduce,
    b_reduce,
    layer_scale,
    cotangent,
):
    band_rows, band_cols, channels = ocean_state.shape
    keep_mask = land_sea.astype(jnp.float32)[:, :, None]
    masked32 = ocean_state.astype(jnp.float32) * keep_mask
    keep_wide = jnp.broadcast_to(keep_mask, ocean_state.shape).astype(jnp.bfloat16)
    top_rows = masked32[band_rows - 3 :][::-1, ::-1]
    conv_out = halo_correlate(masked32, top_rows, kernel, conv_bias, True, 0)
    result, conv_grad = pointwise(
        conv_out,
        ocean_state,
        keep_wide,
        cotangent,
        norm_gain,
        norm_bias,
        w_expand,
        b_expand,
        w_reduce,
        b_reduce,
        layer_scale,
    )

    grad_top = conv_grad[band_rows - 3 :][::-1, ::-1]
    state_grad = halo_correlate(
        conv_grad, grad_top, kernel, None, False, 1, (cotangent, keep_wide)
    )
    return (result, state_grad)


def solution(mesh):
    placed = (
        P("lat", "lon", None),
        P("lat", "lon"),
        P(),
        P(),
        P(),
        P(),
        P(),
        P(),
        P(),
        P(),
        P(),
        P("lat", "lon", None),
    )
    return jax.shard_map(
        body,
        mesh=mesh,
        in_specs=placed,
        out_specs=(P("lat", "lon", None), P("lat", "lon", None)),
        check_vma=False,
    )
```

```python
import jax
import jax.numpy as jnp
from jax import lax
from jax.sharding import PartitionSpec as P
from jax.experimental import pallas as pl
from jax.experimental.pallas import tpu as pltpu


MESH = pl.DeviceIdType.MESH


def correlate_into(src, taps, bias, o_ref, first_row, count, col_tiles, block=8):
    block = min(block, count)
    steps = -(-count // block)
    chans = o_ref.shape[-1]

    def step(i, carry):
        r0 = first_row + jnp.minimum(i * block, count - block)
        for c0 in col_tiles:
            acc = jnp.broadcast_to(bias, (block, 8, chans))
            for col_tap in range(7):
                window = src[pl.ds(r0, block + 6), pl.ds(c0 + col_tap, 8), :]
                for row_tap in range(7):
                    acc = acc + taps[row_tap * 7 + col_tap] * window[row_tap : row_tap + block]
            o_ref[pl.ds(r0, block), pl.ds(c0, 8), :] = acc
        return carry

    lax.fori_loop(0, steps, step, 0)


def halo_correlate(block, kernel, bias, north_fold, collective, tail=None):
    rows, cols, chans = block.shape
    nlat, nlon = lax.axis_size("lat"), lax.axis_size("lon")
    fold_back = tail is not None

    def run(*refs):
        if fold_back:
            x_ref, kw_ref, t_ref, m_ref, o_ref, pad, gf, k_ref, acc_ref, stage, send, recv, local, folds = refs
        else:
            x_ref, kw_ref, b_ref, o_ref, pad, gf, k_ref, acc_ref, stage, send, recv, local, folds = refs
            acc_ref = o_ref
        band = lax.axis_index("lat")
        lon = lax.axis_index("lon")
        has_south = band > 0
        has_north = band < nlat - 1
        top = band == nlat - 1
        west = lax.rem(lon + nlon - 1, nlon)
        east = lax.rem(lon + 1, nlon)
        fold_dst = gf if fold_back else pad
        fold_row = 6 if fold_back else rows + 3
        hi = pl.ds(rows - 3, 3)
        lo = pl.ds(0, 3)
        allr = pl.ds(0, rows)
        c_lo, c_hi, c_all = pl.ds(0, 3), pl.ds(cols - 3, 3), pl.ds(0, cols)
        d_w, d_mid, d_e = pl.ds(0, 3), pl.ds(3, cols), pl.ds(cols + 3, 3)
        messages = [
            (x_ref.at[hi, c_all], pad.at[pl.ds(0, 3), d_mid], (lon, band + 1), has_north, has_south),
            (x_ref.at[hi, c_hi], pad.at[pl.ds(0, 3), d_w], (east, band + 1), has_north, has_south),
            (x_ref.at[hi, c_lo], pad.at[pl.ds(0, 3), d_e], (west, band + 1), has_north, has_south),
            (x_ref.at[lo, c_all], pad.at[pl.ds(rows + 3, 3), d_mid], (lon, band - 1), has_south, has_north),
            (x_ref.at[lo, c_hi], pad.at[pl.ds(rows + 3, 3), d_w], (east, band - 1), has_south, has_north),
            (x_ref.at[lo, c_lo], pad.at[pl.ds(rows + 3, 3), d_e], (west, band - 1), has_south, has_north),
            (x_ref.at[allr, c_hi], pad.at[pl.ds(3, rows), d_w], (east, band), None, None),
            (x_ref.at[allr, c_lo], pad.at[pl.ds(3, rows), d_e], (west, band), None, None),
            (x_ref.at[hi, c_all], stage.at[:, d_mid], (nlon - 1 - lon, band), top, top),
            (x_ref.at[hi, c_lo], stage.at[:, d_e], (lax.rem(2 * nlon - lon, nlon), band), top, top),
            (x_ref.at[hi, c_hi], stage.at[:, d_w], (lax.rem(2 * nlon - 2 - lon, nlon), band), top, top),
        ]
        sources = [
            (lon, band - 1), (west, band - 1), (east, band - 1),
            (lon, band + 1), (west, band + 1), (east, band + 1),
            (west, band), (east, band),
        ]
        for i in (9, 10):
            src, dst, target, _, _ = messages[i]
            apart = jnp.logical_and(top, target[0] != lon)
            messages[i] = (src, dst, target, apart, apart)
        sources += [messages[8][2], messages[9][2], messages[10][2]]
        own = [
            (pltpu.make_async_copy(messages[i][0], messages[i][1], folds.at[j]),
             jnp.logical_and(top, messages[i][2][0] == lon))
            for j, i in enumerate((9, 10))
        ]
        for copy, cond in own:
            pl.when(cond)(copy.start)

        interior = pltpu.make_async_copy(x_ref, pad.at[pl.ds(3, rows), pl.ds(3, cols)], local)
        interior.start()

        @pl.when(band == 0)
        def _():
            pad[pl.ds(0, 3)] = jnp.zeros((3, cols + 6, chans), jnp.float32)

        if not north_fold:
            @pl.when(top)
            def _():
                pad[pl.ds(rows + 3, 3)] = jnp.zeros((3, cols + 6, chans), jnp.float32)

        if fold_back:
            gf[pl.ds(0, 6)] = jnp.zeros((6, cols + 6, chans), jnp.float32)

            @pl.when(jnp.logical_not(top))
            def _():
                gf[pl.ds(6, 3)] = jnp.zeros((3, cols + 6, chans), jnp.float32)

        barrier = pltpu.get_barrier_semaphore()

        def when(cond, fn):
            if cond is None:
                fn()
            else:
                pl.when(cond)(fn)

        for (src, dst, target, s_cond, r_cond), source in zip(messages, sources):
            def greet_target(target=target):
                pl.semaphore_signal(barrier, 1, device_id=target, device_id_type=MESH)

            def greet_source(source=source):
                pl.semaphore_signal(barrier, 1, device_id=source, device_id_type=MESH)

            when(s_cond, greet_target)
            when(r_cond, greet_source)
        for row_tap in range(7):
            for col_tap in range(7):
                a, b = (6 - row_tap, 6 - col_tap) if fold_back else (row_tap, col_tap)
                k_ref[row_tap * 7 + col_tap] = kw_ref[a, pl.ds(b, 1), :].astype(jnp.float32)
        if fold_back:
            bias_row = jnp.zeros((1, chans), jnp.float32)
        else:
            bias_row = b_ref[...]

        interior.wait()
        inner_tiles = tuple(range(8, cols - 8, 8))
        correlate_into(pad, k_ref, bias_row, acc_ref, 3, rows - 6, inner_tiles)

        edge = has_north.astype(jnp.int32) + has_south.astype(jnp.int32)
        folded = top.astype(jnp.int32) + sum(messages[i][3].astype(jnp.int32) for i in (9, 10))
        expected = 2 * (3 * edge + 2 + folded)
        pl.semaphore_wait(barrier, expected)

        copies = []
        for i, (src, dst, target, s_cond, r_cond) in enumerate(messages):
            copy = pltpu.make_async_remote_copy(
                src_ref=src,
                dst_ref=dst,
                send_sem=send.at[i],
                recv_sem=recv.at[i],
                device_id=target,
                device_id_type=MESH,
            )
            copies.append(copy)
            when(s_cond, copy.start)
        for copy, (src, dst, target, s_cond, r_cond) in zip(copies, messages):
            when(s_cond, copy.wait_send)
            when(r_cond, copy.wait_recv)
        for copy, cond in own:
            pl.when(cond)(copy.wait)

        @pl.when(top)
        def _():
            for t in range(3):
                for j in range(cols + 6):
                    fold_dst[fold_row + t, pl.ds(j, 1), :] = stage[2 - t, pl.ds(cols + 5 - j, 1), :]

        outer_tiles = (0, cols - 8)
        correlate_into(pad, k_ref, bias_row, acc_ref, 0, rows, outer_tiles)
        correlate_into(pad, k_ref, bias_row, acc_ref, 0, 3, inner_tiles)
        correlate_into(pad, k_ref, bias_row, acc_ref, rows - 3, 3, inner_tiles)
        if fold_back:
            extra = jnp.zeros((3, cols, chans), jnp.float32)
            for row_tap in range(7):
                for col_tap in range(7):
                    window = gf[pl.ds(row_tap, 3), pl.ds(col_tap, cols), :]
                    tap = kw_ref[row_tap, pl.ds(col_tap, 1), :].astype(jnp.float32)
                    extra = extra + tap * window
            acc_ref[pl.ds(rows - 3, 3)] = acc_ref[pl.ds(rows - 3, 3)] + extra
            step = 8 if rows % 8 == 0 else rows

            def finish(i, carry):
                at = pl.ds(i * step, step)
                total = t_ref[at].astype(jnp.float32) + acc_ref[at]
                o_ref[at] = (m_ref[at].astype(jnp.float32) * total).astype(o_ref.dtype)
                return carry

            lax.fori_loop(0, rows // step, finish, 0)

    if fold_back:
        cotangent, keep = tail
        operands = (block, kernel, cotangent, keep)
    else:
        operands = (block, kernel, bias.reshape(1, chans))
    return pl.pallas_call(
        run,
        out_shape=jax.ShapeDtypeStruct(
            (rows, cols, chans), jnp.bfloat16 if fold_back else jnp.float32
        ),
        in_specs=[pl.BlockSpec(memory_space=pltpu.VMEM)] * len(operands),
        out_specs=pl.BlockSpec(memory_space=pltpu.VMEM),
        scratch_shapes=[
            pltpu.VMEM((rows + 6, cols + 6, chans), jnp.float32),
            pltpu.VMEM((9, cols + 6, chans), jnp.float32),
            pltpu.VMEM((49, 1, chans), jnp.float32),
            pltpu.VMEM((rows, cols, chans) if fold_back else (8, 128), jnp.float32),
            pltpu.VMEM((3, cols + 6, chans), jnp.float32),
            pltpu.SemaphoreType.DMA((11,)),
            pltpu.SemaphoreType.DMA((11,)),
            pltpu.SemaphoreType.DMA,
            pltpu.SemaphoreType.DMA((2,)),
        ],
        compiler_params=pltpu.CompilerParams(collective_id=collective, has_side_effects=True),
    )(*operands)


def gelu_value(values):
    return 0.5 * values * (1.0 + lax.erf(values * 0.7071067811865476))


def gelu_slope(values):
    cumulative = 0.5 * (1.0 + lax.erf(values * 0.7071067811865476))
    return cumulative + values * jnp.exp(-0.5 * values * values) * 0.3989422804014327


def pointwise(
    conv_out,
    ocean_state,
    keep_mask,
    cotangent,
    norm_gain,
    norm_bias,
    w_expand,
    b_expand,
    w_reduce,
    b_reduce,
    layer_scale,
    tile=16,
):
    band_rows, band_cols, chans = conv_out.shape
    cells = tile * band_cols
    hidden_size = w_expand.shape[1]
    tile = tile if band_rows % tile == 0 else band_rows
    cells = tile * band_cols
    contract_last = (((1,), (1,)), ((), ()))

    def run(c_ref, s_ref, m_ref, t_ref, g_ref, nb_ref, we_ref, be_ref, wr_ref, br_ref, ls_ref, r_ref, o_ref):
        flat = lambda ref: ref[...].reshape(cells, chans)
        conv = flat(c_ref)
        keep = flat(m_ref).astype(jnp.float32)
        gain = g_ref[...]
        scale = ls_ref[...]
        row_mean = jnp.mean(conv, axis=-1, keepdims=True)
        centered = conv - row_mean
        inv_std = lax.rsqrt(jnp.mean(centered * centered, axis=-1, keepdims=True) + 1e-06)
        normal_hat = centered * inv_std
        normed = (normal_hat * gain + nb_ref[...]).astype(jnp.bfloat16)
        hidden = jnp.dot(normed, we_ref[...], preferred_element_type=jnp.float32) + be_ref[...]
        erf_term = lax.erf(hidden * 0.7071067811865476)
        activated = (0.5 * hidden * (1.0 + erf_term)).astype(jnp.bfloat16)
        projected = jnp.dot(activated, wr_ref[...], preferred_element_type=jnp.float32) + br_ref[...]
        result = keep * (flat(s_ref).astype(jnp.float32) + scale * projected)
        r_ref[...] = result.astype(r_ref.dtype).reshape(tile, band_cols, chans)
        grad_out = (keep * scale * flat(t_ref).astype(jnp.float32)).astype(jnp.bfloat16)
        grad_act = lax.dot_general(
            grad_out, wr_ref[...], contract_last, preferred_element_type=jnp.float32
        )
        slope = 0.5 * (1.0 + erf_term) + hidden * jnp.exp(-0.5 * hidden * hidden) * 0.3989422804014327
        grad_hidden = (grad_act * slope).astype(jnp.bfloat16)
        grad_normed = lax.dot_general(
            grad_hidden, we_ref[...], contract_last, preferred_element_type=jnp.float32
        )
        grad_scaled = grad_normed * gain
        conv_grad = inv_std * (
            grad_scaled
            - jnp.mean(grad_scaled, axis=-1, keepdims=True)
            - normal_hat * jnp.mean(grad_scaled * normal_hat, axis=-1, keepdims=True)
        )
        o_ref[...] = conv_grad.reshape(tile, band_cols, chans)

    rows = lambda width: pl.BlockSpec((tile, band_cols, width), lambda i: (i, 0, 0))
    whole = lambda shape: pl.BlockSpec(shape, lambda i: (0, 0))
    vec = lambda v: v.reshape(1, -1)
    return pl.pallas_call(
        run,
        grid=(band_rows // tile,),
        out_shape=(
            jax.ShapeDtypeStruct(conv_out.shape, jnp.bfloat16),
            jax.ShapeDtypeStruct(conv_out.shape, jnp.float32),
        ),
        in_specs=[
            rows(chans), rows(chans), rows(chans), rows(chans),
            whole((1, chans)), whole((1, chans)),
            whole((chans, hidden_size)), whole((1, hidden_size)),
            whole((hidden_size, chans)), whole((1, chans)), whole((1, chans)),
        ],
        out_specs=(rows(chans), rows(chans)),
    )(
        conv_out, ocean_state, keep_mask, cotangent, vec(norm_gain), vec(norm_bias),
        w_expand, vec(b_expand), w_reduce, vec(b_reduce), vec(layer_scale),
    )


def body(
    ocean_state,
    land_sea,
    kernel,
    conv_bias,
    norm_gain,
    norm_bias,
    w_expand,
    b_expand,
    w_reduce,
    b_reduce,
    layer_scale,
    cotangent,
):
    band_rows, band_cols, channels = ocean_state.shape
    keep_mask = land_sea.astype(jnp.float32)[:, :, None]
    masked32 = ocean_state.astype(jnp.float32) * keep_mask
    keep_wide = jnp.broadcast_to(keep_mask, ocean_state.shape).astype(jnp.bfloat16)
    conv_out = halo_correlate(masked32, kernel, conv_bias, True, 0)
    result, conv_grad = pointwise(
        conv_out,
        ocean_state,
        keep_wide,
        cotangent,
        norm_gain,
        norm_bias,
        w_expand,
        b_expand,
        w_reduce,
        b_reduce,
        layer_scale,
    )

    state_grad = halo_correlate(
        conv_grad, kernel, None, False, 1, (cotangent, keep_wide)
    )
    return (result, state_grad)


def solution(mesh):
    placed = (
        P("lat", "lon", None),
        P("lat", "lon"),
        P(),
        P(),
        P(),
        P(),
        P(),
        P(),
        P(),
        P(),
        P(),
        P("lat", "lon", None),
    )
    return jax.shard_map(
        body,
        mesh=mesh,
        in_specs=placed,
        out_specs=(P("lat", "lon", None), P("lat", "lon", None)),
        check_vma=False,
    )
```

```python
import jax
import jax.numpy as jnp
from jax import lax
from jax.sharding import PartitionSpec as P
from jax.experimental import pallas as pl
from jax.experimental.pallas import tpu as pltpu


MESH = pl.DeviceIdType.MESH


def correlate_into(src, taps, bias, o_ref, first_row, count, col_tiles, block=16):
    block = min(block, count)
    steps = -(-count // block)
    chans = o_ref.shape[-1]

    def step(i, carry):
        r0 = first_row + jnp.minimum(i * block, count - block)
        for c0 in col_tiles:
            acc = jnp.broadcast_to(bias, (block, 8, chans))
            for col_tap in range(7):
                window = src[pl.ds(r0, block + 6), pl.ds(c0 + col_tap, 8), :]
                for row_tap in range(7):
                    acc = acc + taps[row_tap * 7 + col_tap] * window[row_tap : row_tap + block]
            o_ref[pl.ds(r0, block), pl.ds(c0, 8), :] = acc
        return carry

    lax.fori_loop(0, steps, step, 0)


def halo_correlate(block, kernel, bias, north_fold, collective, tail=None):
    rows, cols, chans = block.shape
    nlat, nlon = lax.axis_size("lat"), lax.axis_size("lon")
    fold_back = tail is not None

    def run(*refs):
        if fold_back:
            x_ref, kw_ref, t_ref, m_ref, o_ref, pad, gf, k_ref, acc_ref, stage, send, recv, local, folds = refs
        else:
            x_ref, kw_ref, b_ref, o_ref, pad, gf, k_ref, acc_ref, stage, send, recv, local, folds = refs
            acc_ref = o_ref
        band = lax.axis_index("lat")
        lon = lax.axis_index("lon")
        has_south = band > 0
        has_north = band < nlat - 1
        top = band == nlat - 1
        west = lax.rem(lon + nlon - 1, nlon)
        east = lax.rem(lon + 1, nlon)
        fold_dst = gf if fold_back else pad
        fold_row = 6 if fold_back else rows + 3
        hi = pl.ds(rows - 3, 3)
        lo = pl.ds(0, 3)
        allr = pl.ds(0, rows)
        c_lo, c_hi, c_all = pl.ds(0, 3), pl.ds(cols - 3, 3), pl.ds(0, cols)
        d_w, d_mid, d_e = pl.ds(0, 3), pl.ds(3, cols), pl.ds(cols + 3, 3)
        messages = [
            (x_ref.at[hi, c_all], pad.at[pl.ds(0, 3), d_mid], (lon, band + 1), has_north, has_south),
            (x_ref.at[hi, c_hi], pad.at[pl.ds(0, 3), d_w], (east, band + 1), has_north, has_south),
            (x_ref.at[hi, c_lo], pad.at[pl.ds(0, 3), d_e], (west, band + 1), has_north, has_south),
            (x_ref.at[lo, c_all], pad.at[pl.ds(rows + 3, 3), d_mid], (lon, band - 1), has_south, has_north),
            (x_ref.at[lo, c_hi], pad.at[pl.ds(rows + 3, 3), d_w], (east, band - 1), has_south, has_north),
            (x_ref.at[lo, c_lo], pad.at[pl.ds(rows + 3, 3), d_e], (west, band - 1), has_south, has_north),
            (x_ref.at[allr, c_hi], pad.at[pl.ds(3, rows), d_w], (east, band), None, None),
            (x_ref.at[allr, c_lo], pad.at[pl.ds(3, rows), d_e], (west, band), None, None),
            (x_ref.at[hi, c_all], stage.at[:, d_mid], (nlon - 1 - lon, band), top, top),
            (x_ref.at[hi, c_lo], stage.at[:, d_e], (lax.rem(2 * nlon - lon, nlon), band), top, top),
            (x_ref.at[hi, c_hi], stage.at[:, d_w], (lax.rem(2 * nlon - 2 - lon, nlon), band), top, top),
        ]
        sources = [
            (lon, band - 1), (west, band - 1), (east, band - 1),
            (lon, band + 1), (west, band + 1), (east, band + 1),
            (west, band), (east, band),
        ]
        for i in (9, 10):
            src, dst, target, _, _ = messages[i]
            apart = jnp.logical_and(top, target[0] != lon)
            messages[i] = (src, dst, target, apart, apart)
        sources += [messages[8][2], messages[9][2], messages[10][2]]
        own = [
            (pltpu.make_async_copy(messages[i][0], messages[i][1], folds.at[j]),
             jnp.logical_and(top, messages[i][2][0] == lon))
            for j, i in enumerate((9, 10))
        ]
        for copy, cond in own:
            pl.when(cond)(copy.start)

        interior = pltpu.make_async_copy(x_ref, pad.at[pl.ds(3, rows), pl.ds(3, cols)], local)
        interior.start()

        @pl.when(band == 0)
        def _():
            pad[pl.ds(0, 3)] = jnp.zeros((3, cols + 6, chans), jnp.float32)

        if not north_fold:
            @pl.when(top)
            def _():
                pad[pl.ds(rows + 3, 3)] = jnp.zeros((3, cols + 6, chans), jnp.float32)

        if fold_back:
            gf[pl.ds(0, 6)] = jnp.zeros((6, cols + 6, chans), jnp.float32)

            @pl.when(jnp.logical_not(top))
            def _():
                gf[pl.ds(6, 3)] = jnp.zeros((3, cols + 6, chans), jnp.float32)

        barrier = pltpu.get_barrier_semaphore()

        def when(cond, fn):
            if cond is None:
                fn()
            else:
                pl.when(cond)(fn)

        for (src, dst, target, s_cond, r_cond), source in zip(messages, sources):
            def greet_target(target=target):
                pl.semaphore_signal(barrier, 1, device_id=target, device_id_type=MESH)

            def greet_source(source=source):
                pl.semaphore_signal(barrier, 1, device_id=source, device_id_type=MESH)

            when(s_cond, greet_target)
            when(r_cond, greet_source)
        for row_tap in range(7):
            for col_tap in range(7):
                a, b = (6 - row_tap, 6 - col_tap) if fold_back else (row_tap, col_tap)
                k_ref[row_tap * 7 + col_tap] = kw_ref[a, pl.ds(b, 1), :].astype(jnp.float32)
        if fold_back:
            bias_row = jnp.zeros((1, chans), jnp.float32)
        else:
            bias_row = b_ref[...]

        interior.wait()
        inner_tiles = tuple(range(8, cols - 8, 8))
        correlate_into(pad, k_ref, bias_row, acc_ref, 3, rows - 6, inner_tiles)

        edge = has_north.astype(jnp.int32) + has_south.astype(jnp.int32)
        folded = top.astype(jnp.int32) + sum(messages[i][3].astype(jnp.int32) for i in (9, 10))
        expected = 2 * (3 * edge + 2 + folded)
        pl.semaphore_wait(barrier, expected)

        copies = []
        for i, (src, dst, target, s_cond, r_cond) in enumerate(messages):
            copy = pltpu.make_async_remote_copy(
                src_ref=src,
                dst_ref=dst,
                send_sem=send.at[i],
                recv_sem=recv.at[i],
                device_id=target,
                device_id_type=MESH,
            )
            copies.append(copy)
            when(s_cond, copy.start)
        for copy, (src, dst, target, s_cond, r_cond) in zip(copies, messages):
            when(s_cond, copy.wait_send)
            when(r_cond, copy.wait_recv)
        for copy, cond in own:
            pl.when(cond)(copy.wait)

        @pl.when(top)
        def _():
            for t in range(3):
                for j in range(cols + 6):
                    fold_dst[fold_row + t, pl.ds(j, 1), :] = stage[2 - t, pl.ds(cols + 5 - j, 1), :]

        outer_tiles = (0, cols - 8)
        correlate_into(pad, k_ref, bias_row, acc_ref, 0, rows, outer_tiles)
        correlate_into(pad, k_ref, bias_row, acc_ref, 0, 3, inner_tiles)
        correlate_into(pad, k_ref, bias_row, acc_ref, rows - 3, 3, inner_tiles)
        if fold_back:
            extra = jnp.zeros((3, cols, chans), jnp.float32)
            for row_tap in range(7):
                for col_tap in range(7):
                    window = gf[pl.ds(row_tap, 3), pl.ds(col_tap, cols), :]
                    tap = kw_ref[row_tap, pl.ds(col_tap, 1), :].astype(jnp.float32)
                    extra = extra + tap * window
            acc_ref[pl.ds(rows - 3, 3)] = acc_ref[pl.ds(rows - 3, 3)] + extra
            step = 8 if rows % 8 == 0 else rows

            def finish(i, carry):
                at = pl.ds(i * step, step)
                total = t_ref[at].astype(jnp.float32) + acc_ref[at]
                o_ref[at] = (m_ref[at].astype(jnp.float32) * total).astype(o_ref.dtype)
                return carry

            lax.fori_loop(0, rows // step, finish, 0)

    if fold_back:
        cotangent, keep = tail
        operands = (block, kernel, cotangent, keep)
    else:
        operands = (block, kernel, bias.reshape(1, chans))
    return pl.pallas_call(
        run,
        out_shape=jax.ShapeDtypeStruct(
            (rows, cols, chans), jnp.bfloat16 if fold_back else jnp.float32
        ),
        in_specs=[pl.BlockSpec(memory_space=pltpu.VMEM)] * len(operands),
        out_specs=pl.BlockSpec(memory_space=pltpu.VMEM),
        scratch_shapes=[
            pltpu.VMEM((rows + 6, cols + 6, chans), jnp.float32),
            pltpu.VMEM((9, cols + 6, chans), jnp.float32),
            pltpu.VMEM((49, 1, chans), jnp.float32),
            pltpu.VMEM((rows, cols, chans) if fold_back else (8, 128), jnp.float32),
            pltpu.VMEM((3, cols + 6, chans), jnp.float32),
            pltpu.SemaphoreType.DMA((11,)),
            pltpu.SemaphoreType.DMA((11,)),
            pltpu.SemaphoreType.DMA,
            pltpu.SemaphoreType.DMA((2,)),
        ],
        compiler_params=pltpu.CompilerParams(collective_id=collective, has_side_effects=True),
    )(*operands)


def gelu_value(values):
    return 0.5 * values * (1.0 + lax.erf(values * 0.7071067811865476))


def gelu_slope(values):
    cumulative = 0.5 * (1.0 + lax.erf(values * 0.7071067811865476))
    return cumulative + values * jnp.exp(-0.5 * values * values) * 0.3989422804014327


def pointwise(
    conv_out,
    ocean_state,
    keep_mask,
    cotangent,
    norm_gain,
    norm_bias,
    w_expand,
    b_expand,
    w_reduce,
    b_reduce,
    layer_scale,
    tile=16,
):
    band_rows, band_cols, chans = conv_out.shape
    cells = tile * band_cols
    hidden_size = w_expand.shape[1]
    tile = tile if band_rows % tile == 0 else band_rows
    cells = tile * band_cols
    contract_last = (((1,), (1,)), ((), ()))

    def run(c_ref, s_ref, m_ref, t_ref, g_ref, nb_ref, we_ref, be_ref, wr_ref, br_ref, ls_ref, r_ref, o_ref):
        flat = lambda ref: ref[...].reshape(cells, chans)
        conv = flat(c_ref)
        keep = flat(m_ref).astype(jnp.float32)
        gain = g_ref[...]
        scale = ls_ref[...]
        row_mean = jnp.mean(conv, axis=-1, keepdims=True)
        centered = conv - row_mean
        inv_std = lax.rsqrt(jnp.mean(centered * centered, axis=-1, keepdims=True) + 1e-06)
        normal_hat = centered * inv_std
        normed = (normal_hat * gain + nb_ref[...]).astype(jnp.bfloat16)
        hidden = jnp.dot(normed, we_ref[...], preferred_element_type=jnp.float32) + be_ref[...]
        erf_term = lax.erf(hidden * 0.7071067811865476)
        activated = (0.5 * hidden * (1.0 + erf_term)).astype(jnp.bfloat16)
        projected = jnp.dot(activated, wr_ref[...], preferred_element_type=jnp.float32) + br_ref[...]
        result = keep * (flat(s_ref).astype(jnp.float32) + scale * projected)
        r_ref[...] = result.astype(r_ref.dtype).reshape(tile, band_cols, chans)
        grad_out = (keep * scale * flat(t_ref).astype(jnp.float32)).astype(jnp.bfloat16)
        grad_act = lax.dot_general(
            grad_out, wr_ref[...], contract_last, preferred_element_type=jnp.float32
        )
        slope = 0.5 * (1.0 + erf_term) + hidden * jnp.exp(-0.5 * hidden * hidden) * 0.3989422804014327
        grad_hidden = (grad_act * slope).astype(jnp.bfloat16)
        grad_normed = lax.dot_general(
            grad_hidden, we_ref[...], contract_last, preferred_element_type=jnp.float32
        )
        grad_scaled = grad_normed * gain
        conv_grad = inv_std * (
            grad_scaled
            - jnp.mean(grad_scaled, axis=-1, keepdims=True)
            - normal_hat * jnp.mean(grad_scaled * normal_hat, axis=-1, keepdims=True)
        )
        o_ref[...] = conv_grad.reshape(tile, band_cols, chans)

    rows = lambda width: pl.BlockSpec((tile, band_cols, width), lambda i: (i, 0, 0))
    whole = lambda shape: pl.BlockSpec(shape, lambda i: (0, 0))
    vec = lambda v: v.reshape(1, -1)
    return pl.pallas_call(
        run,
        grid=(band_rows // tile,),
        out_shape=(
            jax.ShapeDtypeStruct(conv_out.shape, jnp.bfloat16),
            jax.ShapeDtypeStruct(conv_out.shape, jnp.float32),
        ),
        in_specs=[
            rows(chans), rows(chans), rows(chans), rows(chans),
            whole((1, chans)), whole((1, chans)),
            whole((chans, hidden_size)), whole((1, hidden_size)),
            whole((hidden_size, chans)), whole((1, chans)), whole((1, chans)),
        ],
        out_specs=(rows(chans), rows(chans)),
    )(
        conv_out, ocean_state, keep_mask, cotangent, vec(norm_gain), vec(norm_bias),
        w_expand, vec(b_expand), w_reduce, vec(b_reduce), vec(layer_scale),
    )


def body(
    ocean_state,
    land_sea,
    kernel,
    conv_bias,
    norm_gain,
    norm_bias,
    w_expand,
    b_expand,
    w_reduce,
    b_reduce,
    layer_scale,
    cotangent,
):
    band_rows, band_cols, channels = ocean_state.shape
    keep_mask = land_sea.astype(jnp.float32)[:, :, None]
    masked32 = ocean_state.astype(jnp.float32) * keep_mask
    keep_wide = jnp.broadcast_to(keep_mask, ocean_state.shape).astype(jnp.bfloat16)
    conv_out = halo_correlate(masked32, kernel, conv_bias, True, 0)
    result, conv_grad = pointwise(
        conv_out,
        ocean_state,
        keep_wide,
        cotangent,
        norm_gain,
        norm_bias,
        w_expand,
        b_expand,
        w_reduce,
        b_reduce,
        layer_scale,
    )

    state_grad = halo_correlate(
        conv_grad, kernel, None, False, 1, (cotangent, keep_wide)
    )
    return (result, state_grad)


def solution(mesh):
    placed = (
        P("lat", "lon", None),
        P("lat", "lon"),
        P(),
        P(),
        P(),
        P(),
        P(),
        P(),
        P(),
        P(),
        P(),
        P("lat", "lon", None),
    )
    return jax.shard_map(
        body,
        mesh=mesh,
        in_specs=placed,
        out_specs=(P("lat", "lon", None), P("lat", "lon", None)),
        check_vma=False,
    )
```

```python
import jax
import jax.numpy as jnp
from jax import lax
from jax.sharding import PartitionSpec as P
from jax.experimental import pallas as pl
from jax.experimental.pallas import tpu as pltpu


MESH = pl.DeviceIdType.MESH


def correlate_into(src, taps, bias, o_ref, first_row, count, col_tiles, block=16):
    block = min(block, count)
    steps = -(-count // block)
    chans = o_ref.shape[-1]

    def step(i, carry):
        r0 = first_row + jnp.minimum(i * block, count - block)
        for c0 in col_tiles:
            acc = jnp.broadcast_to(bias, (block, 8, chans))
            for col_tap in range(7):
                window = src[pl.ds(r0, block + 6), pl.ds(c0 + col_tap, 8), :]
                for row_tap in range(7):
                    acc = acc + taps[row_tap * 7 + col_tap] * window[row_tap : row_tap + block]
            o_ref[pl.ds(r0, block), pl.ds(c0, 8), :] = acc
        return carry

    lax.fori_loop(0, steps, step, 0)


def halo_correlate(block, kernel, bias, north_fold, collective, tail=None):
    rows, cols, chans = block.shape
    nlat, nlon = lax.axis_size("lat"), lax.axis_size("lon")
    fold_back = tail is not None

    def run(*refs):
        if fold_back:
            x_ref, kw_ref, t_ref, m_ref, o_ref, pad, gf, k_ref, acc_ref, stage, send, recv, local, folds = refs
        else:
            x_ref, kw_ref, b_ref, o_ref, pad, gf, k_ref, acc_ref, stage, send, recv, local, folds = refs
            acc_ref = o_ref
        band = lax.axis_index("lat")
        lon = lax.axis_index("lon")
        has_south = band > 0
        has_north = band < nlat - 1
        top = band == nlat - 1
        west = lax.rem(lon + nlon - 1, nlon)
        east = lax.rem(lon + 1, nlon)
        fold_dst = gf if fold_back else pad
        fold_row = 6 if fold_back else rows + 3
        hi = pl.ds(rows - 3, 3)
        lo = pl.ds(0, 3)
        allr = pl.ds(0, rows)
        c_lo, c_hi, c_all = pl.ds(0, 3), pl.ds(cols - 3, 3), pl.ds(0, cols)
        d_w, d_mid, d_e = pl.ds(0, 3), pl.ds(3, cols), pl.ds(cols + 3, 3)
        messages = [
            (x_ref.at[hi, c_all], pad.at[pl.ds(0, 3), d_mid], (lon, band + 1), has_north, has_south),
            (x_ref.at[hi, c_hi], pad.at[pl.ds(0, 3), d_w], (east, band + 1), has_north, has_south),
            (x_ref.at[hi, c_lo], pad.at[pl.ds(0, 3), d_e], (west, band + 1), has_north, has_south),
            (x_ref.at[lo, c_all], pad.at[pl.ds(rows + 3, 3), d_mid], (lon, band - 1), has_south, has_north),
            (x_ref.at[lo, c_hi], pad.at[pl.ds(rows + 3, 3), d_w], (east, band - 1), has_south, has_north),
            (x_ref.at[lo, c_lo], pad.at[pl.ds(rows + 3, 3), d_e], (west, band - 1), has_south, has_north),
            (x_ref.at[allr, c_hi], pad.at[pl.ds(3, rows), d_w], (east, band), None, None),
            (x_ref.at[allr, c_lo], pad.at[pl.ds(3, rows), d_e], (west, band), None, None),
            (x_ref.at[hi, c_all], stage.at[:, d_mid], (nlon - 1 - lon, band), top, top),
            (x_ref.at[hi, c_lo], stage.at[:, d_e], (lax.rem(2 * nlon - lon, nlon), band), top, top),
            (x_ref.at[hi, c_hi], stage.at[:, d_w], (lax.rem(2 * nlon - 2 - lon, nlon), band), top, top),
        ]
        sources = [
            (lon, band - 1), (west, band - 1), (east, band - 1),
            (lon, band + 1), (west, band + 1), (east, band + 1),
            (west, band), (east, band),
        ]
        for i in (9, 10):
            src, dst, target, _, _ = messages[i]
            apart = jnp.logical_and(top, target[0] != lon)
            messages[i] = (src, dst, target, apart, apart)
        sources += [messages[8][2], messages[9][2], messages[10][2]]
        own = [
            (pltpu.make_async_copy(messages[i][0], messages[i][1], folds.at[j]),
             jnp.logical_and(top, messages[i][2][0] == lon))
            for j, i in enumerate((9, 10))
        ]
        for copy, cond in own:
            pl.when(cond)(copy.start)

        interior = pltpu.make_async_copy(x_ref, pad.at[pl.ds(3, rows), pl.ds(3, cols)], local)
        interior.start()

        @pl.when(band == 0)
        def _():
            pad[pl.ds(0, 3)] = jnp.zeros((3, cols + 6, chans), jnp.float32)

        if not north_fold:
            @pl.when(top)
            def _():
                pad[pl.ds(rows + 3, 3)] = jnp.zeros((3, cols + 6, chans), jnp.float32)

        if fold_back:
            gf[pl.ds(0, 6)] = jnp.zeros((6, cols + 6, chans), jnp.float32)

            @pl.when(jnp.logical_not(top))
            def _():
                gf[pl.ds(6, 3)] = jnp.zeros((3, cols + 6, chans), jnp.float32)

        barrier = pltpu.get_barrier_semaphore()

        def when(cond, fn):
            if cond is None:
                fn()
            else:
                pl.when(cond)(fn)

        for (src, dst, target, s_cond, r_cond), source in zip(messages, sources):
            def greet_target(target=target):
                pl.semaphore_signal(barrier, 1, device_id=target, device_id_type=MESH)

            def greet_source(source=source):
                pl.semaphore_signal(barrier, 1, device_id=source, device_id_type=MESH)

            when(s_cond, greet_target)
            when(r_cond, greet_source)
        for row_tap in range(7):
            for col_tap in range(7):
                a, b = (6 - row_tap, 6 - col_tap) if fold_back else (row_tap, col_tap)
                k_ref[row_tap * 7 + col_tap] = kw_ref[a, pl.ds(b, 1), :].astype(jnp.float32)
        if fold_back:
            bias_row = jnp.zeros((1, chans), jnp.float32)
        else:
            bias_row = b_ref[...]

        interior.wait()
        inner_tiles = tuple(range(8, cols - 8, 8))
        correlate_into(pad, k_ref, bias_row, acc_ref, 3, rows - 6, inner_tiles)

        edge = has_north.astype(jnp.int32) + has_south.astype(jnp.int32)
        folded = top.astype(jnp.int32) + sum(messages[i][3].astype(jnp.int32) for i in (9, 10))
        expected = 2 * (3 * edge + 2 + folded)
        pl.semaphore_wait(barrier, expected)

        copies = []
        for i, (src, dst, target, s_cond, r_cond) in enumerate(messages):
            copy = pltpu.make_async_remote_copy(
                src_ref=src,
                dst_ref=dst,
                send_sem=send.at[i],
                recv_sem=recv.at[i],
                device_id=target,
                device_id_type=MESH,
            )
            copies.append(copy)
            when(s_cond, copy.start)
        for copy, (src, dst, target, s_cond, r_cond) in zip(copies, messages):
            when(s_cond, copy.wait_send)
            when(r_cond, copy.wait_recv)
        for copy, cond in own:
            pl.when(cond)(copy.wait)

        @pl.when(top)
        def _():
            for t in range(3):
                for j in range(cols + 6):
                    fold_dst[fold_row + t, pl.ds(j, 1), :] = stage[2 - t, pl.ds(cols + 5 - j, 1), :]

        outer_tiles = (0, cols - 8)
        correlate_into(pad, k_ref, bias_row, acc_ref, 0, rows, outer_tiles)
        correlate_into(pad, k_ref, bias_row, acc_ref, 0, 3, inner_tiles)
        correlate_into(pad, k_ref, bias_row, acc_ref, rows - 3, 3, inner_tiles)
        if fold_back:
            extra = jnp.zeros((3, cols, chans), jnp.float32)
            for row_tap in range(7):
                for col_tap in range(7):
                    window = gf[pl.ds(row_tap, 3), pl.ds(col_tap, cols), :]
                    tap = kw_ref[row_tap, pl.ds(col_tap, 1), :].astype(jnp.float32)
                    extra = extra + tap * window
            acc_ref[pl.ds(rows - 3, 3)] = acc_ref[pl.ds(rows - 3, 3)] + extra
            step = 8 if rows % 8 == 0 else rows

            def finish(i, carry):
                at = pl.ds(i * step, step)
                total = t_ref[at].astype(jnp.float32) + acc_ref[at]
                o_ref[at] = (m_ref[at].astype(jnp.float32) * total).astype(o_ref.dtype)
                return carry

            lax.fori_loop(0, rows // step, finish, 0)

    if fold_back:
        cotangent, keep = tail
        operands = (block, kernel, cotangent, keep)
    else:
        operands = (block, kernel, bias.reshape(1, chans))
    return pl.pallas_call(
        run,
        out_shape=jax.ShapeDtypeStruct(
            (rows, cols, chans), jnp.bfloat16 if fold_back else jnp.float32
        ),
        in_specs=[pl.BlockSpec(memory_space=pltpu.VMEM)] * len(operands),
        out_specs=pl.BlockSpec(memory_space=pltpu.VMEM),
        scratch_shapes=[
            pltpu.VMEM((rows + 6, cols + 6, chans), jnp.float32),
            pltpu.VMEM((9, cols + 6, chans), jnp.float32),
            pltpu.VMEM((49, 1, chans), jnp.float32),
            pltpu.VMEM((rows, cols, chans) if fold_back else (8, 128), jnp.float32),
            pltpu.VMEM((3, cols + 6, chans), jnp.float32),
            pltpu.SemaphoreType.DMA((11,)),
            pltpu.SemaphoreType.DMA((11,)),
            pltpu.SemaphoreType.DMA,
            pltpu.SemaphoreType.DMA((2,)),
        ],
        compiler_params=pltpu.CompilerParams(collective_id=collective, has_side_effects=True),
    )(*operands)


def gelu_value(values):
    return 0.5 * values * (1.0 + lax.erf(values * 0.7071067811865476))


def gelu_slope(values):
    cumulative = 0.5 * (1.0 + lax.erf(values * 0.7071067811865476))
    return cumulative + values * jnp.exp(-0.5 * values * values) * 0.3989422804014327


def pointwise(
    conv_out,
    ocean_state,
    keep_mask,
    cotangent,
    norm_gain,
    norm_bias,
    w_expand,
    b_expand,
    w_reduce,
    b_reduce,
    layer_scale,
    tile=40,
):
    band_rows, band_cols, chans = conv_out.shape
    cells = tile * band_cols
    hidden_size = w_expand.shape[1]
    tile = tile if band_rows % tile == 0 else band_rows
    cells = tile * band_cols
    contract_last = (((1,), (1,)), ((), ()))

    def run(c_ref, s_ref, m_ref, t_ref, g_ref, nb_ref, we_ref, be_ref, wr_ref, br_ref, ls_ref, r_ref, o_ref):
        flat = lambda ref: ref[...].reshape(cells, chans)
        conv = flat(c_ref)
        keep = flat(m_ref).astype(jnp.float32)
        gain = g_ref[...]
        scale = ls_ref[...]
        row_mean = jnp.mean(conv, axis=-1, keepdims=True)
        centered = conv - row_mean
        inv_std = lax.rsqrt(jnp.mean(centered * centered, axis=-1, keepdims=True) + 1e-06)
        normal_hat = centered * inv_std
        normed = (normal_hat * gain + nb_ref[...]).astype(jnp.bfloat16)
        hidden = jnp.dot(normed, we_ref[...], preferred_element_type=jnp.float32) + be_ref[...]
        erf_term = lax.erf(hidden * 0.7071067811865476)
        activated = (0.5 * hidden * (1.0 + erf_term)).astype(jnp.bfloat16)
        projected = jnp.dot(activated, wr_ref[...], preferred_element_type=jnp.float32) + br_ref[...]
        result = keep * (flat(s_ref).astype(jnp.float32) + scale * projected)
        r_ref[...] = result.astype(r_ref.dtype).reshape(tile, band_cols, chans)
        grad_out = (keep * scale * flat(t_ref).astype(jnp.float32)).astype(jnp.bfloat16)
        grad_act = lax.dot_general(
            grad_out, wr_ref[...], contract_last, preferred_element_type=jnp.float32
        )
        slope = 0.5 * (1.0 + erf_term) + hidden * jnp.exp(-0.5 * hidden * hidden) * 0.3989422804014327
        grad_hidden = (grad_act * slope).astype(jnp.bfloat16)
        grad_normed = lax.dot_general(
            grad_hidden, we_ref[...], contract_last, preferred_element_type=jnp.float32
        )
        grad_scaled = grad_normed * gain
        conv_grad = inv_std * (
            grad_scaled
            - jnp.mean(grad_scaled, axis=-1, keepdims=True)
            - normal_hat * jnp.mean(grad_scaled * normal_hat, axis=-1, keepdims=True)
        )
        o_ref[...] = conv_grad.reshape(tile, band_cols, chans)

    rows = lambda width: pl.BlockSpec((tile, band_cols, width), lambda i: (i, 0, 0))
    whole = lambda shape: pl.BlockSpec(shape, lambda i: (0, 0))
    vec = lambda v: v.reshape(1, -1)
    return pl.pallas_call(
        run,
        grid=(band_rows // tile,),
        out_shape=(
            jax.ShapeDtypeStruct(conv_out.shape, jnp.bfloat16),
            jax.ShapeDtypeStruct(conv_out.shape, jnp.float32),
        ),
        in_specs=[
            rows(chans), rows(chans), rows(chans), rows(chans),
            whole((1, chans)), whole((1, chans)),
            whole((chans, hidden_size)), whole((1, hidden_size)),
            whole((hidden_size, chans)), whole((1, chans)), whole((1, chans)),
        ],
        out_specs=(rows(chans), rows(chans)),
    )(
        conv_out, ocean_state, keep_mask, cotangent, vec(norm_gain), vec(norm_bias),
        w_expand, vec(b_expand), w_reduce, vec(b_reduce), vec(layer_scale),
    )


def body(
    ocean_state,
    land_sea,
    kernel,
    conv_bias,
    norm_gain,
    norm_bias,
    w_expand,
    b_expand,
    w_reduce,
    b_reduce,
    layer_scale,
    cotangent,
):
    band_rows, band_cols, channels = ocean_state.shape
    keep_mask = land_sea.astype(jnp.float32)[:, :, None]
    masked32 = ocean_state.astype(jnp.float32) * keep_mask
    keep_wide = jnp.broadcast_to(keep_mask, ocean_state.shape).astype(jnp.bfloat16)
    conv_out = halo_correlate(masked32, kernel, conv_bias, True, 0)
    result, conv_grad = pointwise(
        conv_out,
        ocean_state,
        keep_wide,
        cotangent,
        norm_gain,
        norm_bias,
        w_expand,
        b_expand,
        w_reduce,
        b_reduce,
        layer_scale,
    )

    state_grad = halo_correlate(
        conv_grad, kernel, None, False, 1, (cotangent, keep_wide)
    )
    return (result, state_grad)


def solution(mesh):
    placed = (
        P("lat", "lon", None),
        P("lat", "lon"),
        P(),
        P(),
        P(),
        P(),
        P(),
        P(),
        P(),
        P(),
        P(),
        P("lat", "lon", None),
    )
    return jax.shard_map(
        body,
        mesh=mesh,
        in_specs=placed,
        out_specs=(P("lat", "lon", None), P("lat", "lon", None)),
        check_vma=False,
    )
```

```python
import jax
import jax.numpy as jnp
from jax import lax
from jax.sharding import PartitionSpec as P
from jax.experimental import pallas as pl
from jax.experimental.pallas import tpu as pltpu


MESH = pl.DeviceIdType.MESH


def correlate_into(src, taps, bias, o_ref, first_row, count, col_tiles, block=16):
    block = min(block, count)
    steps = -(-count // block)
    chans = o_ref.shape[-1]

    def step(i, carry):
        r0 = first_row + jnp.minimum(i * block, count - block)
        for c0 in col_tiles:
            acc = jnp.broadcast_to(bias, (block, 8, chans))
            for col_tap in range(7):
                window = src[pl.ds(r0, block + 6), pl.ds(c0 + col_tap, 8), :]
                for row_tap in range(7):
                    acc = acc + taps[row_tap * 7 + col_tap] * window[row_tap : row_tap + block]
            o_ref[pl.ds(r0, block), pl.ds(c0, 8), :] = acc
        return carry

    lax.fori_loop(0, steps, step, 0)


def halo_correlate(block, kernel, bias, north_fold, collective, tail=None):
    rows, cols, chans = block.shape
    nlat, nlon = lax.axis_size("lat"), lax.axis_size("lon")
    fold_back = tail is not None

    def run(*refs):
        if fold_back:
            x_ref, kw_ref, t_ref, m_ref, o_ref, pad, gf, k_ref, acc_ref, stage, send, recv, local, folds = refs
        else:
            x_ref, kw_ref, b_ref, o_ref, pad, gf, k_ref, acc_ref, stage, send, recv, local, folds = refs
            acc_ref = o_ref
        band = lax.axis_index("lat")
        lon = lax.axis_index("lon")
        has_south = band > 0
        has_north = band < nlat - 1
        top = band == nlat - 1
        west = lax.rem(lon + nlon - 1, nlon)
        east = lax.rem(lon + 1, nlon)
        fold_dst = gf if fold_back else pad
        fold_row = 6 if fold_back else rows + 3
        hi = pl.ds(rows - 3, 3)
        lo = pl.ds(0, 3)
        allr = pl.ds(0, rows)
        c_lo, c_hi, c_all = pl.ds(0, 3), pl.ds(cols - 3, 3), pl.ds(0, cols)
        d_w, d_mid, d_e = pl.ds(0, 3), pl.ds(3, cols), pl.ds(cols + 3, 3)
        messages = [
            (x_ref.at[hi, c_all], pad.at[pl.ds(0, 3), d_mid], (lon, band + 1), has_north, has_south),
            (x_ref.at[hi, c_hi], pad.at[pl.ds(0, 3), d_w], (east, band + 1), has_north, has_south),
            (x_ref.at[hi, c_lo], pad.at[pl.ds(0, 3), d_e], (west, band + 1), has_north, has_south),
            (x_ref.at[lo, c_all], pad.at[pl.ds(rows + 3, 3), d_mid], (lon, band - 1), has_south, has_north),
            (x_ref.at[lo, c_hi], pad.at[pl.ds(rows + 3, 3), d_w], (east, band - 1), has_south, has_north),
            (x_ref.at[lo, c_lo], pad.at[pl.ds(rows + 3, 3), d_e], (west, band - 1), has_south, has_north),
            (x_ref.at[allr, c_hi], pad.at[pl.ds(3, rows), d_w], (east, band), None, None),
            (x_ref.at[allr, c_lo], pad.at[pl.ds(3, rows), d_e], (west, band), None, None),
            (x_ref.at[hi, c_all], stage.at[:, d_mid], (nlon - 1 - lon, band), top, top),
            (x_ref.at[hi, c_lo], stage.at[:, d_e], (lax.rem(2 * nlon - lon, nlon), band), top, top),
            (x_ref.at[hi, c_hi], stage.at[:, d_w], (lax.rem(2 * nlon - 2 - lon, nlon), band), top, top),
        ]
        sources = [
            (lon, band - 1), (west, band - 1), (east, band - 1),
            (lon, band + 1), (west, band + 1), (east, band + 1),
            (west, band), (east, band),
        ]
        for i in (9, 10):
            src, dst, target, _, _ = messages[i]
            apart = jnp.logical_and(top, target[0] != lon)
            messages[i] = (src, dst, target, apart, apart)
        sources += [messages[8][2], messages[9][2], messages[10][2]]
        own = [
            (pltpu.make_async_copy(messages[i][0], messages[i][1], folds.at[j]),
             jnp.logical_and(top, messages[i][2][0] == lon))
            for j, i in enumerate((9, 10))
        ]
        for copy, cond in own:
            pl.when(cond)(copy.start)

        interior = pltpu.make_async_copy(x_ref, pad.at[pl.ds(3, rows), pl.ds(3, cols)], local)
        interior.start()

        @pl.when(band == 0)
        def _():
            pad[pl.ds(0, 3)] = jnp.zeros((3, cols + 6, chans), jnp.float32)

        if not north_fold:
            @pl.when(top)
            def _():
                pad[pl.ds(rows + 3, 3)] = jnp.zeros((3, cols + 6, chans), jnp.float32)

        if fold_back:
            gf[pl.ds(0, 6)] = jnp.zeros((6, cols + 6, chans), jnp.float32)

            @pl.when(jnp.logical_not(top))
            def _():
                gf[pl.ds(6, 3)] = jnp.zeros((3, cols + 6, chans), jnp.float32)

        barrier = pltpu.get_barrier_semaphore()

        def when(cond, fn):
            if cond is None:
                fn()
            else:
                pl.when(cond)(fn)

        for (src, dst, target, s_cond, r_cond), source in zip(messages, sources):
            def greet_target(target=target):
                pl.semaphore_signal(barrier, 1, device_id=target, device_id_type=MESH)

            def greet_source(source=source):
                pl.semaphore_signal(barrier, 1, device_id=source, device_id_type=MESH)

            when(s_cond, greet_target)
            when(r_cond, greet_source)
        for row_tap in range(7):
            for col_tap in range(7):
                a, b = (6 - row_tap, 6 - col_tap) if fold_back else (row_tap, col_tap)
                k_ref[row_tap * 7 + col_tap] = kw_ref[a, pl.ds(b, 1), :].astype(jnp.float32)
        if fold_back:
            bias_row = jnp.zeros((1, chans), jnp.float32)
        else:
            bias_row = b_ref[...]

        interior.wait()
        inner_tiles = tuple(range(8, cols - 8, 8))
        correlate_into(pad, k_ref, bias_row, acc_ref, 3, rows - 6, inner_tiles)

        edge = has_north.astype(jnp.int32) + has_south.astype(jnp.int32)
        folded = top.astype(jnp.int32) + sum(messages[i][3].astype(jnp.int32) for i in (9, 10))
        expected = 2 * (3 * edge + 2 + folded)
        pl.semaphore_wait(barrier, expected)

        copies = []
        for i, (src, dst, target, s_cond, r_cond) in enumerate(messages):
            copy = pltpu.make_async_remote_copy(
                src_ref=src,
                dst_ref=dst,
                send_sem=send.at[i],
                recv_sem=recv.at[i],
                device_id=target,
                device_id_type=MESH,
            )
            copies.append(copy)
            when(s_cond, copy.start)
        for copy, (src, dst, target, s_cond, r_cond) in zip(copies, messages):
            when(s_cond, copy.wait_send)
            when(r_cond, copy.wait_recv)
        for copy, cond in own:
            pl.when(cond)(copy.wait)

        @pl.when(top)
        def _():
            for t in range(3):
                for j in range(cols + 6):
                    fold_dst[fold_row + t, pl.ds(j, 1), :] = stage[2 - t, pl.ds(cols + 5 - j, 1), :]

        outer_tiles = (0, cols - 8)
        correlate_into(pad, k_ref, bias_row, acc_ref, 0, rows, outer_tiles)
        correlate_into(pad, k_ref, bias_row, acc_ref, 0, 3, inner_tiles)
        correlate_into(pad, k_ref, bias_row, acc_ref, rows - 3, 3, inner_tiles)
        if fold_back:
            extra = jnp.zeros((3, cols, chans), jnp.float32)
            for row_tap in range(7):
                for col_tap in range(7):
                    window = gf[pl.ds(row_tap, 3), pl.ds(col_tap, cols), :]
                    tap = kw_ref[row_tap, pl.ds(col_tap, 1), :].astype(jnp.float32)
                    extra = extra + tap * window
            acc_ref[pl.ds(rows - 3, 3)] = acc_ref[pl.ds(rows - 3, 3)] + extra
            step = 8 if rows % 8 == 0 else rows

            def finish(i, carry):
                at = pl.ds(i * step, step)
                total = t_ref[at].astype(jnp.float32) + acc_ref[at]
                o_ref[at] = (m_ref[at].astype(jnp.float32) * total).astype(o_ref.dtype)
                return carry

            lax.fori_loop(0, rows // step, finish, 0)

    if fold_back:
        cotangent, keep = tail
        operands = (block, kernel, cotangent, keep)
    else:
        operands = (block, kernel, bias.reshape(1, chans))
    return pl.pallas_call(
        run,
        out_shape=jax.ShapeDtypeStruct(
            (rows, cols, chans), jnp.bfloat16 if fold_back else jnp.float32
        ),
        in_specs=[pl.BlockSpec(memory_space=pltpu.VMEM)] * len(operands),
        out_specs=pl.BlockSpec(memory_space=pltpu.VMEM),
        scratch_shapes=[
            pltpu.VMEM((rows + 6, cols + 6, chans), jnp.float32),
            pltpu.VMEM((9, cols + 6, chans), jnp.float32),
            pltpu.VMEM((49, 1, chans), jnp.float32),
            pltpu.VMEM((rows, cols, chans) if fold_back else (8, 128), jnp.float32),
            pltpu.VMEM((3, cols + 6, chans), jnp.float32),
            pltpu.SemaphoreType.DMA((11,)),
            pltpu.SemaphoreType.DMA((11,)),
            pltpu.SemaphoreType.DMA,
            pltpu.SemaphoreType.DMA((2,)),
        ],
        compiler_params=pltpu.CompilerParams(collective_id=collective, has_side_effects=True),
    )(*operands)


def gelu_value(values):
    return 0.5 * values * (1.0 + lax.erf(values * 0.7071067811865476))


def gelu_slope(values):
    cumulative = 0.5 * (1.0 + lax.erf(values * 0.7071067811865476))
    return cumulative + values * jnp.exp(-0.5 * values * values) * 0.3989422804014327


def pointwise(
    conv_out,
    ocean_state,
    keep_mask,
    cotangent,
    norm_gain,
    norm_bias,
    w_expand,
    b_expand,
    w_reduce,
    b_reduce,
    layer_scale,
    tile=80,
):
    band_rows, band_cols, chans = conv_out.shape
    cells = tile * band_cols
    hidden_size = w_expand.shape[1]
    tile = tile if band_rows % tile == 0 else band_rows
    cells = tile * band_cols
    contract_last = (((1,), (1,)), ((), ()))

    def run(c_ref, s_ref, m_ref, t_ref, g_ref, nb_ref, we_ref, be_ref, wr_ref, br_ref, ls_ref, r_ref, o_ref):
        flat = lambda ref: ref[...].reshape(cells, chans)
        conv = flat(c_ref)
        keep = flat(m_ref).astype(jnp.float32)
        gain = g_ref[...]
        scale = ls_ref[...]
        row_mean = jnp.mean(conv, axis=-1, keepdims=True)
        centered = conv - row_mean
        inv_std = lax.rsqrt(jnp.mean(centered * centered, axis=-1, keepdims=True) + 1e-06)
        normal_hat = centered * inv_std
        normed = (normal_hat * gain + nb_ref[...]).astype(jnp.bfloat16)
        hidden = jnp.dot(normed, we_ref[...], preferred_element_type=jnp.float32) + be_ref[...]
        erf_term = lax.erf(hidden * 0.7071067811865476)
        activated = (0.5 * hidden * (1.0 + erf_term)).astype(jnp.bfloat16)
        projected = jnp.dot(activated, wr_ref[...], preferred_element_type=jnp.float32) + br_ref[...]
        result = keep * (flat(s_ref).astype(jnp.float32) + scale * projected)
        r_ref[...] = result.astype(r_ref.dtype).reshape(tile, band_cols, chans)
        grad_out = (keep * scale * flat(t_ref).astype(jnp.float32)).astype(jnp.bfloat16)
        grad_act = lax.dot_general(
            grad_out, wr_ref[...], contract_last, preferred_element_type=jnp.float32
        )
        slope = 0.5 * (1.0 + erf_term) + hidden * jnp.exp(-0.5 * hidden * hidden) * 0.3989422804014327
        grad_hidden = (grad_act * slope).astype(jnp.bfloat16)
        grad_normed = lax.dot_general(
            grad_hidden, we_ref[...], contract_last, preferred_element_type=jnp.float32
        )
        grad_scaled = grad_normed * gain
        conv_grad = inv_std * (
            grad_scaled
            - jnp.mean(grad_scaled, axis=-1, keepdims=True)
            - normal_hat * jnp.mean(grad_scaled * normal_hat, axis=-1, keepdims=True)
        )
        o_ref[...] = conv_grad.reshape(tile, band_cols, chans)

    rows = lambda width: pl.BlockSpec((tile, band_cols, width), lambda i: (i, 0, 0))
    whole = lambda shape: pl.BlockSpec(shape, lambda i: (0, 0))
    vec = lambda v: v.reshape(1, -1)
    return pl.pallas_call(
        run,
        grid=(band_rows // tile,),
        out_shape=(
            jax.ShapeDtypeStruct(conv_out.shape, jnp.bfloat16),
            jax.ShapeDtypeStruct(conv_out.shape, jnp.float32),
        ),
        in_specs=[
            rows(chans), rows(chans), rows(chans), rows(chans),
            whole((1, chans)), whole((1, chans)),
            whole((chans, hidden_size)), whole((1, hidden_size)),
            whole((hidden_size, chans)), whole((1, chans)), whole((1, chans)),
        ],
        out_specs=(rows(chans), rows(chans)),
    )(
        conv_out, ocean_state, keep_mask, cotangent, vec(norm_gain), vec(norm_bias),
        w_expand, vec(b_expand), w_reduce, vec(b_reduce), vec(layer_scale),
    )


def body(
    ocean_state,
    land_sea,
    kernel,
    conv_bias,
    norm_gain,
    norm_bias,
    w_expand,
    b_expand,
    w_reduce,
    b_reduce,
    layer_scale,
    cotangent,
):
    band_rows, band_cols, channels = ocean_state.shape
    keep_mask = land_sea.astype(jnp.float32)[:, :, None]
    masked32 = ocean_state.astype(jnp.float32) * keep_mask
    keep_wide = jnp.broadcast_to(keep_mask, ocean_state.shape).astype(jnp.bfloat16)
    conv_out = halo_correlate(masked32, kernel, conv_bias, True, 0)
    result, conv_grad = pointwise(
        conv_out,
        ocean_state,
        keep_wide,
        cotangent,
        norm_gain,
        norm_bias,
        w_expand,
        b_expand,
        w_reduce,
        b_reduce,
        layer_scale,
    )

    state_grad = halo_correlate(
        conv_grad, kernel, None, False, 1, (cotangent, keep_wide)
    )
    return (result, state_grad)


def solution(mesh):
    placed = (
        P("lat", "lon", None),
        P("lat", "lon"),
        P(),
        P(),
        P(),
        P(),
        P(),
        P(),
        P(),
        P(),
        P(),
        P("lat", "lon", None),
    )
    return jax.shard_map(
        body,
        mesh=mesh,
        in_specs=placed,
        out_specs=(P("lat", "lon", None), P("lat", "lon", None)),
        check_vma=False,
    )
```

```python
import jax
import jax.numpy as jnp
from jax import lax
from jax.sharding import PartitionSpec as P
from jax.experimental import pallas as pl
from jax.experimental.pallas import tpu as pltpu


MESH = pl.DeviceIdType.MESH


def correlate_into(src, taps, bias, o_ref, first_row, count, col_tiles, block=16,
                   col_taps=tuple(range(7)), accumulate=False):
    chans = o_ref.shape[-1]
    block = min(block, count)
    steps, left = divmod(count, block)

    def one(r0, size):
        for c0 in col_tiles:
            at = (pl.ds(r0, size), pl.ds(c0, 8), slice(None))
            acc = o_ref[at] if accumulate else jnp.broadcast_to(bias, (size, 8, chans))
            for col_tap in col_taps:
                window = src[pl.ds(r0, size + 6), pl.ds(c0 + col_tap, 8), :]
                for row_tap in range(7):
                    acc = acc + taps[row_tap * 7 + col_tap] * window[row_tap : row_tap + size]
            o_ref[at] = acc

    def step(i, carry):
        one(first_row + i * block, block)
        return carry

    lax.fori_loop(0, steps, step, 0)
    if left:
        one(first_row + steps * block, left)


def halo_correlate(block, kernel, bias, north_fold, collective, tail=None):
    rows, cols, chans = block.shape
    nlat, nlon = lax.axis_size("lat"), lax.axis_size("lon")
    fold_back = tail is not None

    def run(*refs):
        if fold_back:
            x_ref, kw_ref, t_ref, m_ref, o_ref, pad, gf, k_ref, acc_ref, stage, send, recv, local, folds = refs
        else:
            x_ref, kw_ref, b_ref, o_ref, pad, gf, k_ref, acc_ref, stage, send, recv, local, folds = refs
            acc_ref = o_ref
        band = lax.axis_index("lat")
        lon = lax.axis_index("lon")
        has_south = band > 0
        has_north = band < nlat - 1
        top = band == nlat - 1
        west = lax.rem(lon + nlon - 1, nlon)
        east = lax.rem(lon + 1, nlon)
        fold_dst = gf if fold_back else pad
        fold_row = 6 if fold_back else rows + 3
        hi = pl.ds(rows - 3, 3)
        lo = pl.ds(0, 3)
        allr = pl.ds(0, rows)
        c_lo, c_hi, c_all = pl.ds(0, 3), pl.ds(cols - 3, 3), pl.ds(0, cols)
        d_w, d_mid, d_e = pl.ds(0, 3), pl.ds(3, cols), pl.ds(cols + 3, 3)
        messages = [
            (x_ref.at[hi, c_all], pad.at[pl.ds(0, 3), d_mid], (lon, band + 1), has_north, has_south),
            (x_ref.at[hi, c_hi], pad.at[pl.ds(0, 3), d_w], (east, band + 1), has_north, has_south),
            (x_ref.at[hi, c_lo], pad.at[pl.ds(0, 3), d_e], (west, band + 1), has_north, has_south),
            (x_ref.at[lo, c_all], pad.at[pl.ds(rows + 3, 3), d_mid], (lon, band - 1), has_south, has_north),
            (x_ref.at[lo, c_hi], pad.at[pl.ds(rows + 3, 3), d_w], (east, band - 1), has_south, has_north),
            (x_ref.at[lo, c_lo], pad.at[pl.ds(rows + 3, 3), d_e], (west, band - 1), has_south, has_north),
            (x_ref.at[allr, c_hi], pad.at[pl.ds(3, rows), d_w], (east, band), None, None),
            (x_ref.at[allr, c_lo], pad.at[pl.ds(3, rows), d_e], (west, band), None, None),
            (x_ref.at[hi, c_all], stage.at[:, d_mid], (nlon - 1 - lon, band), top, top),
            (x_ref.at[hi, c_lo], stage.at[:, d_e], (lax.rem(2 * nlon - lon, nlon), band), top, top),
            (x_ref.at[hi, c_hi], stage.at[:, d_w], (lax.rem(2 * nlon - 2 - lon, nlon), band), top, top),
        ]
        sources = [
            (lon, band - 1), (west, band - 1), (east, band - 1),
            (lon, band + 1), (west, band + 1), (east, band + 1),
            (west, band), (east, band),
        ]
        for i in (9, 10):
            src, dst, target, _, _ = messages[i]
            apart = jnp.logical_and(top, target[0] != lon)
            messages[i] = (src, dst, target, apart, apart)
        sources += [messages[8][2], messages[9][2], messages[10][2]]
        own = [
            (pltpu.make_async_copy(messages[i][0], messages[i][1], folds.at[j]),
             jnp.logical_and(top, messages[i][2][0] == lon))
            for j, i in enumerate((9, 10))
        ]
        for copy, cond in own:
            pl.when(cond)(copy.start)

        interior = pltpu.make_async_copy(x_ref, pad.at[pl.ds(3, rows), pl.ds(3, cols)], local)
        interior.start()

        @pl.when(band == 0)
        def _():
            pad[pl.ds(0, 3)] = jnp.zeros((3, cols + 6, chans), jnp.float32)

        if not north_fold:
            @pl.when(top)
            def _():
                pad[pl.ds(rows + 3, 3)] = jnp.zeros((3, cols + 6, chans), jnp.float32)

        if fold_back:
            gf[pl.ds(0, 6)] = jnp.zeros((6, cols + 6, chans), jnp.float32)

            @pl.when(jnp.logical_not(top))
            def _():
                gf[pl.ds(6, 3)] = jnp.zeros((3, cols + 6, chans), jnp.float32)

        barrier = pltpu.get_barrier_semaphore()

        def when(cond, fn):
            if cond is None:
                fn()
            else:
                pl.when(cond)(fn)

        for (src, dst, target, s_cond, r_cond), source in zip(messages, sources):
            def greet_target(target=target):
                pl.semaphore_signal(barrier, 1, device_id=target, device_id_type=MESH)

            def greet_source(source=source):
                pl.semaphore_signal(barrier, 1, device_id=source, device_id_type=MESH)

            when(s_cond, greet_target)
            when(r_cond, greet_source)
        for row_tap in range(7):
            for col_tap in range(7):
                a, b = (6 - row_tap, 6 - col_tap) if fold_back else (row_tap, col_tap)
                k_ref[row_tap * 7 + col_tap] = kw_ref[a, pl.ds(b, 1), :].astype(jnp.float32)
        if fold_back:
            bias_row = jnp.zeros((1, chans), jnp.float32)
        else:
            bias_row = b_ref[...]

        interior.wait()
        inner_tiles = tuple(range(8, cols - 8, 8))
        correlate_into(pad, k_ref, bias_row, acc_ref, 3, rows - 6, inner_tiles)
        correlate_into(pad, k_ref, bias_row, acc_ref, 3, rows - 6, (0,), col_taps=(3, 4, 5, 6))
        correlate_into(pad, k_ref, bias_row, acc_ref, 3, rows - 6, (cols - 8,), col_taps=(0, 1, 2, 3))

        edge = has_north.astype(jnp.int32) + has_south.astype(jnp.int32)
        folded = top.astype(jnp.int32) + sum(messages[i][3].astype(jnp.int32) for i in (9, 10))
        expected = 2 * (3 * edge + 2 + folded)
        pl.semaphore_wait(barrier, expected)

        copies = []
        for i, (src, dst, target, s_cond, r_cond) in enumerate(messages):
            copy = pltpu.make_async_remote_copy(
                src_ref=src,
                dst_ref=dst,
                send_sem=send.at[i],
                recv_sem=recv.at[i],
                device_id=target,
                device_id_type=MESH,
            )
            copies.append(copy)
            when(s_cond, copy.start)
        for copy, (src, dst, target, s_cond, r_cond) in zip(copies, messages):
            when(s_cond, copy.wait_send)
            when(r_cond, copy.wait_recv)
        for copy, cond in own:
            pl.when(cond)(copy.wait)

        @pl.when(top)
        def _():
            for t in range(3):
                for j in range(cols + 6):
                    fold_dst[fold_row + t, pl.ds(j, 1), :] = stage[2 - t, pl.ds(cols + 5 - j, 1), :]

        all_tiles = tuple(range(0, cols, 8))
        correlate_into(pad, k_ref, bias_row, acc_ref, 3, rows - 6, (0,), col_taps=(0, 1, 2),
                       accumulate=True)
        correlate_into(pad, k_ref, bias_row, acc_ref, 3, rows - 6, (cols - 8,), col_taps=(4, 5, 6),
                       accumulate=True)
        correlate_into(pad, k_ref, bias_row, acc_ref, 0, 3, all_tiles)
        correlate_into(pad, k_ref, bias_row, acc_ref, rows - 3, 3, all_tiles)
        if fold_back:
            extra = jnp.zeros((3, cols, chans), jnp.float32)
            for row_tap in range(7):
                for col_tap in range(7):
                    window = gf[pl.ds(row_tap, 3), pl.ds(col_tap, cols), :]
                    tap = kw_ref[row_tap, pl.ds(col_tap, 1), :].astype(jnp.float32)
                    extra = extra + tap * window
            acc_ref[pl.ds(rows - 3, 3)] = acc_ref[pl.ds(rows - 3, 3)] + extra
            step = 8 if rows % 8 == 0 else rows

            def finish(i, carry):
                at = pl.ds(i * step, step)
                total = t_ref[at].astype(jnp.float32) + acc_ref[at]
                o_ref[at] = (m_ref[at].astype(jnp.float32) * total).astype(o_ref.dtype)
                return carry

            lax.fori_loop(0, rows // step, finish, 0)

    if fold_back:
        cotangent, keep = tail
        operands = (block, kernel, cotangent, keep)
    else:
        operands = (block, kernel, bias.reshape(1, chans))
    return pl.pallas_call(
        run,
        out_shape=jax.ShapeDtypeStruct(
            (rows, cols, chans), jnp.bfloat16 if fold_back else jnp.float32
        ),
        in_specs=[pl.BlockSpec(memory_space=pltpu.VMEM)] * len(operands),
        out_specs=pl.BlockSpec(memory_space=pltpu.VMEM),
        scratch_shapes=[
            pltpu.VMEM((rows + 6, cols + 6, chans), jnp.float32),
            pltpu.VMEM((9, cols + 6, chans), jnp.float32),
            pltpu.VMEM((49, 1, chans), jnp.float32),
            pltpu.VMEM((rows, cols, chans) if fold_back else (8, 128), jnp.float32),
            pltpu.VMEM((3, cols + 6, chans), jnp.float32),
            pltpu.SemaphoreType.DMA((11,)),
            pltpu.SemaphoreType.DMA((11,)),
            pltpu.SemaphoreType.DMA,
            pltpu.SemaphoreType.DMA((2,)),
        ],
        compiler_params=pltpu.CompilerParams(collective_id=collective, has_side_effects=True),
    )(*operands)


def gelu_value(values):
    return 0.5 * values * (1.0 + lax.erf(values * 0.7071067811865476))


def gelu_slope(values):
    cumulative = 0.5 * (1.0 + lax.erf(values * 0.7071067811865476))
    return cumulative + values * jnp.exp(-0.5 * values * values) * 0.3989422804014327


def pointwise(
    conv_out,
    ocean_state,
    keep_mask,
    cotangent,
    norm_gain,
    norm_bias,
    w_expand,
    b_expand,
    w_reduce,
    b_reduce,
    layer_scale,
    tile=40,
):
    band_rows, band_cols, chans = conv_out.shape
    cells = tile * band_cols
    hidden_size = w_expand.shape[1]
    tile = tile if band_rows % tile == 0 else band_rows
    cells = tile * band_cols
    contract_last = (((1,), (1,)), ((), ()))

    def run(c_ref, s_ref, m_ref, t_ref, g_ref, nb_ref, we_ref, be_ref, wr_ref, br_ref, ls_ref, r_ref, o_ref):
        flat = lambda ref: ref[...].reshape(cells, chans)
        conv = flat(c_ref)
        keep = flat(m_ref).astype(jnp.float32)
        gain = g_ref[...]
        scale = ls_ref[...]
        row_mean = jnp.mean(conv, axis=-1, keepdims=True)
        centered = conv - row_mean
        inv_std = lax.rsqrt(jnp.mean(centered * centered, axis=-1, keepdims=True) + 1e-06)
        normal_hat = centered * inv_std
        normed = (normal_hat * gain + nb_ref[...]).astype(jnp.bfloat16)
        hidden = jnp.dot(normed, we_ref[...], preferred_element_type=jnp.float32) + be_ref[...]
        erf_term = lax.erf(hidden * 0.7071067811865476)
        activated = (0.5 * hidden * (1.0 + erf_term)).astype(jnp.bfloat16)
        projected = jnp.dot(activated, wr_ref[...], preferred_element_type=jnp.float32) + br_ref[...]
        result = keep * (flat(s_ref).astype(jnp.float32) + scale * projected)
        r_ref[...] = result.astype(r_ref.dtype).reshape(tile, band_cols, chans)
        grad_out = (keep * scale * flat(t_ref).astype(jnp.float32)).astype(jnp.bfloat16)
        grad_act = lax.dot_general(
            grad_out, wr_ref[...], contract_last, preferred_element_type=jnp.float32
        )
        slope = 0.5 * (1.0 + erf_term) + hidden * jnp.exp(-0.5 * hidden * hidden) * 0.3989422804014327
        grad_hidden = (grad_act * slope).astype(jnp.bfloat16)
        grad_normed = lax.dot_general(
            grad_hidden, we_ref[...], contract_last, preferred_element_type=jnp.float32
        )
        grad_scaled = grad_normed * gain
        conv_grad = inv_std * (
            grad_scaled
            - jnp.mean(grad_scaled, axis=-1, keepdims=True)
            - normal_hat * jnp.mean(grad_scaled * normal_hat, axis=-1, keepdims=True)
        )
        o_ref[...] = conv_grad.reshape(tile, band_cols, chans)

    rows = lambda width: pl.BlockSpec((tile, band_cols, width), lambda i: (i, 0, 0))
    whole = lambda shape: pl.BlockSpec(shape, lambda i: (0, 0))
    vec = lambda v: v.reshape(1, -1)
    return pl.pallas_call(
        run,
        grid=(band_rows // tile,),
        out_shape=(
            jax.ShapeDtypeStruct(conv_out.shape, jnp.bfloat16),
            jax.ShapeDtypeStruct(conv_out.shape, jnp.float32),
        ),
        in_specs=[
            rows(chans), rows(chans), rows(chans), rows(chans),
            whole((1, chans)), whole((1, chans)),
            whole((chans, hidden_size)), whole((1, hidden_size)),
            whole((hidden_size, chans)), whole((1, chans)), whole((1, chans)),
        ],
        out_specs=(rows(chans), rows(chans)),
    )(
        conv_out, ocean_state, keep_mask, cotangent, vec(norm_gain), vec(norm_bias),
        w_expand, vec(b_expand), w_reduce, vec(b_reduce), vec(layer_scale),
    )


def body(
    ocean_state,
    land_sea,
    kernel,
    conv_bias,
    norm_gain,
    norm_bias,
    w_expand,
    b_expand,
    w_reduce,
    b_reduce,
    layer_scale,
    cotangent,
):
    band_rows, band_cols, channels = ocean_state.shape
    keep_mask = land_sea.astype(jnp.float32)[:, :, None]
    masked32 = ocean_state.astype(jnp.float32) * keep_mask
    keep_wide = jnp.broadcast_to(keep_mask, ocean_state.shape).astype(jnp.bfloat16)
    conv_out = halo_correlate(masked32, kernel, conv_bias, True, 0)
    result, conv_grad = pointwise(
        conv_out,
        ocean_state,
        keep_wide,
        cotangent,
        norm_gain,
        norm_bias,
        w_expand,
        b_expand,
        w_reduce,
        b_reduce,
        layer_scale,
    )

    state_grad = halo_correlate(
        conv_grad, kernel, None, False, 1, (cotangent, keep_wide)
    )
    return (result, state_grad)


def solution(mesh):
    placed = (
        P("lat", "lon", None),
        P("lat", "lon"),
        P(),
        P(),
        P(),
        P(),
        P(),
        P(),
        P(),
        P(),
        P(),
        P("lat", "lon", None),
    )
    return jax.shard_map(
        body,
        mesh=mesh,
        in_specs=placed,
        out_specs=(P("lat", "lon", None), P("lat", "lon", None)),
        check_vma=False,
    )
```

```python
import jax
import jax.numpy as jnp
from jax import lax
from jax.sharding import PartitionSpec as P
from jax.experimental import pallas as pl
from jax.experimental.pallas import tpu as pltpu


MESH = pl.DeviceIdType.MESH


def correlate_into(src, taps, bias, o_ref, first_row, count, col_tiles, block=16,
                   col_taps=tuple(range(7)), accumulate=False):
    chans = o_ref.shape[-1]
    block = min(block, count)
    steps, left = divmod(count, block)

    def one(r0, size):
        for c0 in col_tiles:
            at = (pl.ds(r0, size), pl.ds(c0, 8), slice(None))
            acc = o_ref[at] if accumulate else jnp.broadcast_to(bias, (size, 8, chans))
            for col_tap in col_taps:
                window = src[pl.ds(r0, size + 6), pl.ds(c0 + col_tap, 8), :]
                for row_tap in range(7):
                    acc = acc + taps[row_tap * 7 + col_tap] * window[row_tap : row_tap + size]
            o_ref[at] = acc

    def step(i, carry):
        one(first_row + i * block, block)
        return carry

    lax.fori_loop(0, steps, step, 0)
    if left:
        one(first_row + steps * block, left)


def halo_correlate(block, kernel, bias, north_fold, collective, tail=None, mask=None):
    rows, cols, chans = block.shape
    nlat, nlon = lax.axis_size("lat"), lax.axis_size("lon")
    fold_back = tail is not None

    def run(*refs):
        if fold_back:
            x_ref, kw_ref, t_ref, m_ref, o_ref, pad, gf, k_ref, acc_ref, stage, _, send, recv, local, folds = refs
        else:
            s_ref, w_ref, kw_ref, b_ref, o_ref, pad, gf, k_ref, acc_ref, stage, x_ref, send, recv, local, folds = refs
            acc_ref = o_ref
            def mask_rows(i, carry):
                at = pl.ds(i * 8, 8)
                x_ref[at] = s_ref[at].astype(jnp.float32) * w_ref[at].astype(jnp.float32)
                return carry

            lax.fori_loop(0, rows // 8, mask_rows, 0)
        band = lax.axis_index("lat")
        lon = lax.axis_index("lon")
        has_south = band > 0
        has_north = band < nlat - 1
        top = band == nlat - 1
        west = lax.rem(lon + nlon - 1, nlon)
        east = lax.rem(lon + 1, nlon)
        fold_dst = gf if fold_back else pad
        fold_row = 6 if fold_back else rows + 3
        hi = pl.ds(rows - 3, 3)
        lo = pl.ds(0, 3)
        allr = pl.ds(0, rows)
        c_lo, c_hi, c_all = pl.ds(0, 3), pl.ds(cols - 3, 3), pl.ds(0, cols)
        d_w, d_mid, d_e = pl.ds(0, 3), pl.ds(3, cols), pl.ds(cols + 3, 3)
        messages = [
            (x_ref.at[hi, c_all], pad.at[pl.ds(0, 3), d_mid], (lon, band + 1), has_north, has_south),
            (x_ref.at[hi, c_hi], pad.at[pl.ds(0, 3), d_w], (east, band + 1), has_north, has_south),
            (x_ref.at[hi, c_lo], pad.at[pl.ds(0, 3), d_e], (west, band + 1), has_north, has_south),
            (x_ref.at[lo, c_all], pad.at[pl.ds(rows + 3, 3), d_mid], (lon, band - 1), has_south, has_north),
            (x_ref.at[lo, c_hi], pad.at[pl.ds(rows + 3, 3), d_w], (east, band - 1), has_south, has_north),
            (x_ref.at[lo, c_lo], pad.at[pl.ds(rows + 3, 3), d_e], (west, band - 1), has_south, has_north),
            (x_ref.at[allr, c_hi], pad.at[pl.ds(3, rows), d_w], (east, band), None, None),
            (x_ref.at[allr, c_lo], pad.at[pl.ds(3, rows), d_e], (west, band), None, None),
            (x_ref.at[hi, c_all], stage.at[:, d_mid], (nlon - 1 - lon, band), top, top),
            (x_ref.at[hi, c_lo], stage.at[:, d_e], (lax.rem(2 * nlon - lon, nlon), band), top, top),
            (x_ref.at[hi, c_hi], stage.at[:, d_w], (lax.rem(2 * nlon - 2 - lon, nlon), band), top, top),
        ]
        sources = [
            (lon, band - 1), (west, band - 1), (east, band - 1),
            (lon, band + 1), (west, band + 1), (east, band + 1),
            (west, band), (east, band),
        ]
        for i in (9, 10):
            src, dst, target, _, _ = messages[i]
            apart = jnp.logical_and(top, target[0] != lon)
            messages[i] = (src, dst, target, apart, apart)
        sources += [messages[8][2], messages[9][2], messages[10][2]]
        own = [
            (pltpu.make_async_copy(messages[i][0], messages[i][1], folds.at[j]),
             jnp.logical_and(top, messages[i][2][0] == lon))
            for j, i in enumerate((9, 10))
        ]
        for copy, cond in own:
            pl.when(cond)(copy.start)

        interior = pltpu.make_async_copy(x_ref, pad.at[pl.ds(3, rows), pl.ds(3, cols)], local)
        interior.start()

        @pl.when(band == 0)
        def _():
            pad[pl.ds(0, 3)] = jnp.zeros((3, cols + 6, chans), jnp.float32)

        if not north_fold:
            @pl.when(top)
            def _():
                pad[pl.ds(rows + 3, 3)] = jnp.zeros((3, cols + 6, chans), jnp.float32)

        if fold_back:
            gf[pl.ds(0, 6)] = jnp.zeros((6, cols + 6, chans), jnp.float32)

            @pl.when(jnp.logical_not(top))
            def _():
                gf[pl.ds(6, 3)] = jnp.zeros((3, cols + 6, chans), jnp.float32)

        barrier = pltpu.get_barrier_semaphore()

        def when(cond, fn):
            if cond is None:
                fn()
            else:
                pl.when(cond)(fn)

        for (src, dst, target, s_cond, r_cond), source in zip(messages, sources):
            def greet_target(target=target):
                pl.semaphore_signal(barrier, 1, device_id=target, device_id_type=MESH)

            def greet_source(source=source):
                pl.semaphore_signal(barrier, 1, device_id=source, device_id_type=MESH)

            when(s_cond, greet_target)
            when(r_cond, greet_source)
        for row_tap in range(7):
            for col_tap in range(7):
                a, b = (6 - row_tap, 6 - col_tap) if fold_back else (row_tap, col_tap)
                k_ref[row_tap * 7 + col_tap] = kw_ref[a, pl.ds(b, 1), :].astype(jnp.float32)
        if fold_back:
            bias_row = jnp.zeros((1, chans), jnp.float32)
        else:
            bias_row = b_ref[...]

        interior.wait()
        inner_tiles = tuple(range(8, cols - 8, 8))
        correlate_into(pad, k_ref, bias_row, acc_ref, 3, rows - 6, inner_tiles)
        correlate_into(pad, k_ref, bias_row, acc_ref, 3, rows - 6, (0,), col_taps=(3, 4, 5, 6))
        correlate_into(pad, k_ref, bias_row, acc_ref, 3, rows - 6, (cols - 8,), col_taps=(0, 1, 2, 3))

        edge = has_north.astype(jnp.int32) + has_south.astype(jnp.int32)
        folded = top.astype(jnp.int32) + sum(messages[i][3].astype(jnp.int32) for i in (9, 10))
        expected = 2 * (3 * edge + 2 + folded)
        pl.semaphore_wait(barrier, expected)

        copies = []
        for i, (src, dst, target, s_cond, r_cond) in enumerate(messages):
            copy = pltpu.make_async_remote_copy(
                src_ref=src,
                dst_ref=dst,
                send_sem=send.at[i],
                recv_sem=recv.at[i],
                device_id=target,
                device_id_type=MESH,
            )
            copies.append(copy)
            when(s_cond, copy.start)
        for copy, (src, dst, target, s_cond, r_cond) in zip(copies, messages):
            when(s_cond, copy.wait_send)
            when(r_cond, copy.wait_recv)
        for copy, cond in own:
            pl.when(cond)(copy.wait)

        @pl.when(top)
        def _():
            for t in range(3):
                for j in range(cols + 6):
                    fold_dst[fold_row + t, pl.ds(j, 1), :] = stage[2 - t, pl.ds(cols + 5 - j, 1), :]

        all_tiles = tuple(range(0, cols, 8))
        correlate_into(pad, k_ref, bias_row, acc_ref, 3, rows - 6, (0,), col_taps=(0, 1, 2),
                       accumulate=True)
        correlate_into(pad, k_ref, bias_row, acc_ref, 3, rows - 6, (cols - 8,), col_taps=(4, 5, 6),
                       accumulate=True)
        correlate_into(pad, k_ref, bias_row, acc_ref, 0, 3, all_tiles)
        correlate_into(pad, k_ref, bias_row, acc_ref, rows - 3, 3, all_tiles)
        if fold_back:
            extra = jnp.zeros((3, cols, chans), jnp.float32)
            for row_tap in range(7):
                for col_tap in range(7):
                    window = gf[pl.ds(row_tap, 3), pl.ds(col_tap, cols), :]
                    tap = kw_ref[row_tap, pl.ds(col_tap, 1), :].astype(jnp.float32)
                    extra = extra + tap * window
            acc_ref[pl.ds(rows - 3, 3)] = acc_ref[pl.ds(rows - 3, 3)] + extra
            step = 8 if rows % 8 == 0 else rows

            def finish(i, carry):
                at = pl.ds(i * step, step)
                total = t_ref[at].astype(jnp.float32) + acc_ref[at]
                o_ref[at] = (m_ref[at].astype(jnp.float32) * total).astype(o_ref.dtype)
                return carry

            lax.fori_loop(0, rows // step, finish, 0)

    if fold_back:
        cotangent, keep = tail
        operands = (block, kernel, cotangent, keep)
    else:
        operands = (block, mask, kernel, bias.reshape(1, chans))
    return pl.pallas_call(
        run,
        out_shape=jax.ShapeDtypeStruct(
            (rows, cols, chans), jnp.bfloat16 if fold_back else jnp.float32
        ),
        in_specs=[pl.BlockSpec(memory_space=pltpu.VMEM)] * len(operands),
        out_specs=pl.BlockSpec(memory_space=pltpu.VMEM),
        scratch_shapes=[
            pltpu.VMEM((rows + 6, cols + 6, chans), jnp.float32),
            pltpu.VMEM((9, cols + 6, chans), jnp.float32),
            pltpu.VMEM((49, 1, chans), jnp.float32),
            pltpu.VMEM((rows, cols, chans) if fold_back else (8, 128), jnp.float32),
            pltpu.VMEM((3, cols + 6, chans), jnp.float32),
            pltpu.VMEM((8, 128) if fold_back else (rows, cols, chans), jnp.float32),
            pltpu.SemaphoreType.DMA((11,)),
            pltpu.SemaphoreType.DMA((11,)),
            pltpu.SemaphoreType.DMA,
            pltpu.SemaphoreType.DMA((2,)),
        ],
        compiler_params=pltpu.CompilerParams(collective_id=collective, has_side_effects=True),
    )(*operands)


def gelu_value(values):
    return 0.5 * values * (1.0 + lax.erf(values * 0.7071067811865476))


def gelu_slope(values):
    cumulative = 0.5 * (1.0 + lax.erf(values * 0.7071067811865476))
    return cumulative + values * jnp.exp(-0.5 * values * values) * 0.3989422804014327


def pointwise(
    conv_out,
    ocean_state,
    keep_mask,
    cotangent,
    norm_gain,
    norm_bias,
    w_expand,
    b_expand,
    w_reduce,
    b_reduce,
    layer_scale,
    tile=40,
):
    band_rows, band_cols, chans = conv_out.shape
    cells = tile * band_cols
    hidden_size = w_expand.shape[1]
    tile = tile if band_rows % tile == 0 else band_rows
    cells = tile * band_cols
    contract_last = (((1,), (1,)), ((), ()))

    def run(c_ref, s_ref, m_ref, t_ref, g_ref, nb_ref, we_ref, be_ref, wr_ref, br_ref, ls_ref, r_ref, o_ref):
        flat = lambda ref: ref[...].reshape(cells, chans)
        conv = flat(c_ref)
        keep = flat(m_ref).astype(jnp.float32)
        gain = g_ref[...]
        scale = ls_ref[...]
        row_mean = jnp.mean(conv, axis=-1, keepdims=True)
        centered = conv - row_mean
        inv_std = lax.rsqrt(jnp.mean(centered * centered, axis=-1, keepdims=True) + 1e-06)
        normal_hat = centered * inv_std
        normed = (normal_hat * gain + nb_ref[...]).astype(jnp.bfloat16)
        hidden = jnp.dot(normed, we_ref[...], preferred_element_type=jnp.float32) + be_ref[...]
        erf_term = lax.erf(hidden * 0.7071067811865476)
        activated = (0.5 * hidden * (1.0 + erf_term)).astype(jnp.bfloat16)
        projected = jnp.dot(activated, wr_ref[...], preferred_element_type=jnp.float32) + br_ref[...]
        result = keep * (flat(s_ref).astype(jnp.float32) + scale * projected)
        r_ref[...] = result.astype(r_ref.dtype).reshape(tile, band_cols, chans)
        grad_out = (keep * scale * flat(t_ref).astype(jnp.float32)).astype(jnp.bfloat16)
        grad_act = lax.dot_general(
            grad_out, wr_ref[...], contract_last, preferred_element_type=jnp.float32
        )
        slope = 0.5 * (1.0 + erf_term) + hidden * jnp.exp(-0.5 * hidden * hidden) * 0.3989422804014327
        grad_hidden = (grad_act * slope).astype(jnp.bfloat16)
        grad_normed = lax.dot_general(
            grad_hidden, we_ref[...], contract_last, preferred_element_type=jnp.float32
        )
        grad_scaled = grad_normed * gain
        conv_grad = inv_std * (
            grad_scaled
            - jnp.mean(grad_scaled, axis=-1, keepdims=True)
            - normal_hat * jnp.mean(grad_scaled * normal_hat, axis=-1, keepdims=True)
        )
        o_ref[...] = conv_grad.reshape(tile, band_cols, chans)

    rows = lambda width: pl.BlockSpec((tile, band_cols, width), lambda i: (i, 0, 0))
    whole = lambda shape: pl.BlockSpec(shape, lambda i: (0, 0))
    vec = lambda v: v.reshape(1, -1)
    return pl.pallas_call(
        run,
        grid=(band_rows // tile,),
        out_shape=(
            jax.ShapeDtypeStruct(conv_out.shape, jnp.bfloat16),
            jax.ShapeDtypeStruct(conv_out.shape, jnp.float32),
        ),
        in_specs=[
            rows(chans), rows(chans), rows(chans), rows(chans),
            whole((1, chans)), whole((1, chans)),
            whole((chans, hidden_size)), whole((1, hidden_size)),
            whole((hidden_size, chans)), whole((1, chans)), whole((1, chans)),
        ],
        out_specs=(rows(chans), rows(chans)),
    )(
        conv_out, ocean_state, keep_mask, cotangent, vec(norm_gain), vec(norm_bias),
        w_expand, vec(b_expand), w_reduce, vec(b_reduce), vec(layer_scale),
    )


def body(
    ocean_state,
    land_sea,
    kernel,
    conv_bias,
    norm_gain,
    norm_bias,
    w_expand,
    b_expand,
    w_reduce,
    b_reduce,
    layer_scale,
    cotangent,
):
    band_rows, band_cols, channels = ocean_state.shape
    keep_mask = land_sea.astype(jnp.float32)[:, :, None]
    keep_wide = jnp.broadcast_to(keep_mask, ocean_state.shape).astype(jnp.bfloat16)
    conv_out = halo_correlate(ocean_state, kernel, conv_bias, True, 0, mask=keep_wide)
    result, conv_grad = pointwise(
        conv_out,
        ocean_state,
        keep_wide,
        cotangent,
        norm_gain,
        norm_bias,
        w_expand,
        b_expand,
        w_reduce,
        b_reduce,
        layer_scale,
    )

    state_grad = halo_correlate(
        conv_grad, kernel, None, False, 1, (cotangent, keep_wide)
    )
    return (result, state_grad)


def solution(mesh):
    placed = (
        P("lat", "lon", None),
        P("lat", "lon"),
        P(),
        P(),
        P(),
        P(),
        P(),
        P(),
        P(),
        P(),
        P(),
        P("lat", "lon", None),
    )
    return jax.shard_map(
        body,
        mesh=mesh,
        in_specs=placed,
        out_specs=(P("lat", "lon", None), P("lat", "lon", None)),
        check_vma=False,
    )
```

```python
import jax
import jax.numpy as jnp
from jax import lax
from jax.sharding import PartitionSpec as P
from jax.experimental import pallas as pl
from jax.experimental.pallas import tpu as pltpu


MESH = pl.DeviceIdType.MESH


def correlate_into(src, taps, bias, o_ref, first_row, count, col_tiles, block=16,
                   col_taps=tuple(range(7)), accumulate=False):
    chans = o_ref.shape[-1]
    block = min(block, count)
    steps, left = divmod(count, block)

    def one(r0, size):
        for c0 in col_tiles:
            at = (pl.ds(r0, size), pl.ds(c0, 8), slice(None))
            acc = o_ref[at] if accumulate else jnp.broadcast_to(bias, (size, 8, chans))
            for col_tap in col_taps:
                window = src[pl.ds(r0, size + 6), pl.ds(c0 + col_tap, 8), :]
                for row_tap in range(7):
                    acc = acc + taps[row_tap * 7 + col_tap] * window[row_tap : row_tap + size]
            o_ref[at] = acc

    def step(i, carry):
        one(first_row + i * block, block)
        return carry

    lax.fori_loop(0, steps, step, 0)
    if left:
        one(first_row + steps * block, left)


def halo_correlate(block, kernel, bias, north_fold, collective, tail=None, mask=None):
    rows, cols, chans = block.shape
    nlat, nlon = lax.axis_size("lat"), lax.axis_size("lon")
    fold_back = tail is not None

    def run(*refs):
        if fold_back:
            x_ref, kw_ref, t_ref, m_ref, o_ref, pad, gf, k_ref, acc_ref, stage, _, send, recv, local, folds = refs
        else:
            s_ref, w_ref, kw_ref, b_ref, o_ref, pad, gf, k_ref, acc_ref, stage, x_ref, send, recv, local, folds = refs
            acc_ref = o_ref
            def mask_rows(i, carry):
                at = pl.ds(i * 8, 8)
                x_ref[at] = s_ref[at].astype(jnp.float32) * w_ref[at].astype(jnp.float32)
                return carry

            lax.fori_loop(0, rows // 8, mask_rows, 0)
        band = lax.axis_index("lat")
        lon = lax.axis_index("lon")
        has_south = band > 0
        has_north = band < nlat - 1
        top = band == nlat - 1
        west = lax.rem(lon + nlon - 1, nlon)
        east = lax.rem(lon + 1, nlon)
        fold_dst = gf if fold_back else pad
        fold_row = 6 if fold_back else rows + 3
        hi = pl.ds(rows - 3, 3)
        lo = pl.ds(0, 3)
        allr = pl.ds(0, rows)
        c_lo, c_hi, c_all = pl.ds(0, 3), pl.ds(cols - 3, 3), pl.ds(0, cols)
        d_w, d_mid, d_e = pl.ds(0, 3), pl.ds(3, cols), pl.ds(cols + 3, 3)
        messages = [
            (x_ref.at[hi, c_all], pad.at[pl.ds(0, 3), d_mid], (lon, band + 1), has_north, has_south),
            (x_ref.at[hi, c_hi], pad.at[pl.ds(0, 3), d_w], (east, band + 1), has_north, has_south),
            (x_ref.at[hi, c_lo], pad.at[pl.ds(0, 3), d_e], (west, band + 1), has_north, has_south),
            (x_ref.at[lo, c_all], pad.at[pl.ds(rows + 3, 3), d_mid], (lon, band - 1), has_south, has_north),
            (x_ref.at[lo, c_hi], pad.at[pl.ds(rows + 3, 3), d_w], (east, band - 1), has_south, has_north),
            (x_ref.at[lo, c_lo], pad.at[pl.ds(rows + 3, 3), d_e], (west, band - 1), has_south, has_north),
            (x_ref.at[allr, c_hi], pad.at[pl.ds(3, rows), d_w], (east, band), None, None),
            (x_ref.at[allr, c_lo], pad.at[pl.ds(3, rows), d_e], (west, band), None, None),
            (x_ref.at[hi, c_all], stage.at[:, d_mid], (nlon - 1 - lon, band), top, top),
            (x_ref.at[hi, c_lo], stage.at[:, d_e], (lax.rem(2 * nlon - lon, nlon), band), top, top),
            (x_ref.at[hi, c_hi], stage.at[:, d_w], (lax.rem(2 * nlon - 2 - lon, nlon), band), top, top),
        ]
        sources = [
            (lon, band - 1), (west, band - 1), (east, band - 1),
            (lon, band + 1), (west, band + 1), (east, band + 1),
            (west, band), (east, band),
        ]
        for i in (9, 10):
            src, dst, target, _, _ = messages[i]
            apart = jnp.logical_and(top, target[0] != lon)
            messages[i] = (src, dst, target, apart, apart)
        sources += [messages[8][2], messages[9][2], messages[10][2]]
        own = [
            (pltpu.make_async_copy(messages[i][0], messages[i][1], folds.at[j]),
             jnp.logical_and(top, messages[i][2][0] == lon))
            for j, i in enumerate((9, 10))
        ]
        for copy, cond in own:
            pl.when(cond)(copy.start)

        interior = pltpu.make_async_copy(x_ref, pad.at[pl.ds(3, rows), pl.ds(3, cols)], local)
        interior.start()

        @pl.when(band == 0)
        def _():
            pad[pl.ds(0, 3)] = jnp.zeros((3, cols + 6, chans), jnp.float32)

        if not north_fold:
            @pl.when(top)
            def _():
                pad[pl.ds(rows + 3, 3)] = jnp.zeros((3, cols + 6, chans), jnp.float32)

        if fold_back:
            gf[pl.ds(0, 6)] = jnp.zeros((6, cols + 6, chans), jnp.float32)

            @pl.when(jnp.logical_not(top))
            def _():
                gf[pl.ds(6, 3)] = jnp.zeros((3, cols + 6, chans), jnp.float32)

        barrier = pltpu.get_barrier_semaphore()

        def when(cond, fn):
            if cond is None:
                fn()
            else:
                pl.when(cond)(fn)

        for (src, dst, target, s_cond, r_cond), source in zip(messages, sources):
            def greet_target(target=target):
                pl.semaphore_signal(barrier, 1, device_id=target, device_id_type=MESH)

            def greet_source(source=source):
                pl.semaphore_signal(barrier, 1, device_id=source, device_id_type=MESH)

            when(s_cond, greet_target)
            when(r_cond, greet_source)
        for row_tap in range(7):
            for col_tap in range(7):
                a, b = (6 - row_tap, 6 - col_tap) if fold_back else (row_tap, col_tap)
                k_ref[row_tap * 7 + col_tap] = kw_ref[a, pl.ds(b, 1), :].astype(jnp.float32)
        if fold_back:
            bias_row = jnp.zeros((1, chans), jnp.float32)
        else:
            bias_row = b_ref[...]

        interior.wait()
        inner_tiles = tuple(range(8, cols - 8, 8))
        correlate_into(pad, k_ref, bias_row, acc_ref, 3, rows - 6, inner_tiles)
        correlate_into(pad, k_ref, bias_row, acc_ref, 3, rows - 6, (0,), col_taps=(3, 4, 5, 6))
        correlate_into(pad, k_ref, bias_row, acc_ref, 3, rows - 6, (cols - 8,), col_taps=(0, 1, 2, 3))

        edge = has_north.astype(jnp.int32) + has_south.astype(jnp.int32)
        folded = top.astype(jnp.int32) + sum(messages[i][3].astype(jnp.int32) for i in (9, 10))
        expected = 2 * (3 * edge + 2 + folded)
        pl.semaphore_wait(barrier, expected)

        copies = []
        for i, (src, dst, target, s_cond, r_cond) in enumerate(messages):
            copy = pltpu.make_async_remote_copy(
                src_ref=src,
                dst_ref=dst,
                send_sem=send.at[i],
                recv_sem=recv.at[i],
                device_id=target,
                device_id_type=MESH,
            )
            copies.append(copy)
            when(s_cond, copy.start)
        for copy, (src, dst, target, s_cond, r_cond) in zip(copies, messages):
            when(s_cond, copy.wait_send)
            when(r_cond, copy.wait_recv)
        for copy, cond in own:
            pl.when(cond)(copy.wait)

        @pl.when(top)
        def _():
            for t in range(3):
                for j in range(cols + 6):
                    fold_dst[fold_row + t, pl.ds(j, 1), :] = stage[2 - t, pl.ds(cols + 5 - j, 1), :]

        all_tiles = tuple(range(0, cols, 8))
        correlate_into(pad, k_ref, bias_row, acc_ref, 3, rows - 6, (0,), col_taps=(0, 1, 2),
                       accumulate=True)
        correlate_into(pad, k_ref, bias_row, acc_ref, 3, rows - 6, (cols - 8,), col_taps=(4, 5, 6),
                       accumulate=True)
        correlate_into(pad, k_ref, bias_row, acc_ref, 0, 3, all_tiles)
        correlate_into(pad, k_ref, bias_row, acc_ref, rows - 3, 3, all_tiles)
        if fold_back:
            extra = jnp.zeros((3, cols, chans), jnp.float32)
            for row_tap in range(7):
                for col_tap in range(7):
                    window = gf[pl.ds(row_tap, 3), pl.ds(col_tap, cols), :]
                    tap = kw_ref[row_tap, pl.ds(col_tap, 1), :].astype(jnp.float32)
                    extra = extra + tap * window
            acc_ref[pl.ds(rows - 3, 3)] = acc_ref[pl.ds(rows - 3, 3)] + extra
            step = 8 if rows % 8 == 0 else rows

            def finish(i, carry):
                at = pl.ds(i * step, step)
                total = t_ref[at].astype(jnp.float32) + acc_ref[at]
                o_ref[at] = (m_ref[at].astype(jnp.float32) * total).astype(o_ref.dtype)
                return carry

            lax.fori_loop(0, rows // step, finish, 0)

    if fold_back:
        cotangent, keep = tail
        operands = (block, kernel, cotangent, keep)
    else:
        operands = (block, mask, kernel, bias.reshape(1, chans))
    return pl.pallas_call(
        run,
        out_shape=jax.ShapeDtypeStruct(
            (rows, cols, chans), jnp.bfloat16 if fold_back else jnp.float32
        ),
        in_specs=[pl.BlockSpec(memory_space=pltpu.VMEM)] * len(operands),
        out_specs=pl.BlockSpec(memory_space=pltpu.VMEM),
        scratch_shapes=[
            pltpu.VMEM((rows + 6, cols + 6, chans), jnp.float32),
            pltpu.VMEM((9, cols + 6, chans), jnp.float32),
            pltpu.VMEM((49, 1, chans), jnp.float32),
            pltpu.VMEM((rows, cols, chans) if fold_back else (8, 128), jnp.float32),
            pltpu.VMEM((3, cols + 6, chans), jnp.float32),
            pltpu.VMEM((8, 128) if fold_back else (rows, cols, chans), jnp.float32),
            pltpu.SemaphoreType.DMA((11,)),
            pltpu.SemaphoreType.DMA((11,)),
            pltpu.SemaphoreType.DMA,
            pltpu.SemaphoreType.DMA((2,)),
        ],
        compiler_params=pltpu.CompilerParams(collective_id=collective, has_side_effects=True),
    )(*operands)


def gelu_value(values):
    return 0.5 * values * (1.0 + lax.erf(values * 0.7071067811865476))


def gelu_slope(values):
    cumulative = 0.5 * (1.0 + lax.erf(values * 0.7071067811865476))
    return cumulative + values * jnp.exp(-0.5 * values * values) * 0.3989422804014327


def pointwise(
    conv_out,
    ocean_state,
    keep_mask,
    cotangent,
    norm_gain,
    norm_bias,
    w_expand,
    b_expand,
    w_reduce,
    b_reduce,
    layer_scale,
    tile=20,
):
    band_rows, band_cols, chans = conv_out.shape
    cells = tile * band_cols
    hidden_size = w_expand.shape[1]
    tile = tile if band_rows % tile == 0 else band_rows
    cells = tile * band_cols
    contract_last = (((1,), (1,)), ((), ()))

    def run(c_ref, s_ref, m_ref, t_ref, g_ref, nb_ref, we_ref, be_ref, wr_ref, br_ref, ls_ref, r_ref, o_ref):
        flat = lambda ref: ref[...].reshape(cells, chans)
        conv = flat(c_ref)
        keep = flat(m_ref).astype(jnp.float32)
        gain = g_ref[...]
        scale = ls_ref[...]
        row_mean = jnp.mean(conv, axis=-1, keepdims=True)
        centered = conv - row_mean
        inv_std = lax.rsqrt(jnp.mean(centered * centered, axis=-1, keepdims=True) + 1e-06)
        normal_hat = centered * inv_std
        normed = (normal_hat * gain + nb_ref[...]).astype(jnp.bfloat16)
        hidden = jnp.dot(normed, we_ref[...], preferred_element_type=jnp.float32) + be_ref[...]
        erf_term = lax.erf(hidden * 0.7071067811865476)
        activated = (0.5 * hidden * (1.0 + erf_term)).astype(jnp.bfloat16)
        projected = jnp.dot(activated, wr_ref[...], preferred_element_type=jnp.float32) + br_ref[...]
        result = keep * (flat(s_ref).astype(jnp.float32) + scale * projected)
        r_ref[...] = result.astype(r_ref.dtype).reshape(tile, band_cols, chans)
        grad_out = (keep * scale * flat(t_ref).astype(jnp.float32)).astype(jnp.bfloat16)
        grad_act = lax.dot_general(
            grad_out, wr_ref[...], contract_last, preferred_element_type=jnp.float32
        )
        slope = 0.5 * (1.0 + erf_term) + hidden * jnp.exp(-0.5 * hidden * hidden) * 0.3989422804014327
        grad_hidden = (grad_act * slope).astype(jnp.bfloat16)
        grad_normed = lax.dot_general(
            grad_hidden, we_ref[...], contract_last, preferred_element_type=jnp.float32
        )
        grad_scaled = grad_normed * gain
        conv_grad = inv_std * (
            grad_scaled
            - jnp.mean(grad_scaled, axis=-1, keepdims=True)
            - normal_hat * jnp.mean(grad_scaled * normal_hat, axis=-1, keepdims=True)
        )
        o_ref[...] = conv_grad.reshape(tile, band_cols, chans)

    rows = lambda width: pl.BlockSpec((tile, band_cols, width), lambda i: (i, 0, 0))
    whole = lambda shape: pl.BlockSpec(shape, lambda i: (0, 0))
    vec = lambda v: v.reshape(1, -1)
    return pl.pallas_call(
        run,
        grid=(band_rows // tile,),
        out_shape=(
            jax.ShapeDtypeStruct(conv_out.shape, jnp.bfloat16),
            jax.ShapeDtypeStruct(conv_out.shape, jnp.float32),
        ),
        in_specs=[
            rows(chans), rows(chans), rows(chans), rows(chans),
            whole((1, chans)), whole((1, chans)),
            whole((chans, hidden_size)), whole((1, hidden_size)),
            whole((hidden_size, chans)), whole((1, chans)), whole((1, chans)),
        ],
        out_specs=(rows(chans), rows(chans)),
    )(
        conv_out, ocean_state, keep_mask, cotangent, vec(norm_gain), vec(norm_bias),
        w_expand, vec(b_expand), w_reduce, vec(b_reduce), vec(layer_scale),
    )


def body(
    ocean_state,
    land_sea,
    kernel,
    conv_bias,
    norm_gain,
    norm_bias,
    w_expand,
    b_expand,
    w_reduce,
    b_reduce,
    layer_scale,
    cotangent,
):
    band_rows, band_cols, channels = ocean_state.shape
    keep_mask = land_sea.astype(jnp.float32)[:, :, None]
    keep_wide = jnp.broadcast_to(keep_mask, ocean_state.shape).astype(jnp.bfloat16)
    conv_out = halo_correlate(ocean_state, kernel, conv_bias, True, 0, mask=keep_wide)
    result, conv_grad = pointwise(
        conv_out,
        ocean_state,
        keep_wide,
        cotangent,
        norm_gain,
        norm_bias,
        w_expand,
        b_expand,
        w_reduce,
        b_reduce,
        layer_scale,
    )

    state_grad = halo_correlate(
        conv_grad, kernel, None, False, 1, (cotangent, keep_wide)
    )
    return (result, state_grad)


def solution(mesh):
    placed = (
        P("lat", "lon", None),
        P("lat", "lon"),
        P(),
        P(),
        P(),
        P(),
        P(),
        P(),
        P(),
        P(),
        P(),
        P("lat", "lon", None),
    )
    return jax.shard_map(
        body,
        mesh=mesh,
        in_specs=placed,
        out_specs=(P("lat", "lon", None), P("lat", "lon", None)),
        check_vma=False,
    )
```

```python
import jax
import jax.numpy as jnp
from jax import lax
from jax.sharding import PartitionSpec as P
from jax.experimental import pallas as pl
from jax.experimental.pallas import tpu as pltpu


MESH = pl.DeviceIdType.MESH


def correlate_into(src, taps, bias, o_ref, first_row, count, col_tiles, block=24,
                   col_taps=tuple(range(7)), accumulate=False):
    chans = o_ref.shape[-1]
    block = min(block, count)
    steps, left = divmod(count, block)

    def one(r0, size):
        for c0 in col_tiles:
            at = (pl.ds(r0, size), pl.ds(c0, 8), slice(None))
            acc = o_ref[at] if accumulate else jnp.broadcast_to(bias, (size, 8, chans))
            for col_tap in col_taps:
                window = src[pl.ds(r0, size + 6), pl.ds(c0 + col_tap, 8), :]
                for row_tap in range(7):
                    acc = acc + taps[row_tap * 7 + col_tap] * window[row_tap : row_tap + size]
            o_ref[at] = acc

    def step(i, carry):
        one(first_row + i * block, block)
        return carry

    lax.fori_loop(0, steps, step, 0)
    if left:
        one(first_row + steps * block, left)


def halo_correlate(block, kernel, bias, north_fold, collective, tail=None, mask=None):
    rows, cols, chans = block.shape
    nlat, nlon = lax.axis_size("lat"), lax.axis_size("lon")
    fold_back = tail is not None

    def run(*refs):
        if fold_back:
            x_ref, kw_ref, t_ref, m_ref, o_ref, pad, gf, k_ref, acc_ref, stage, _, send, recv, local, folds = refs
        else:
            s_ref, w_ref, kw_ref, b_ref, o_ref, pad, gf, k_ref, acc_ref, stage, x_ref, send, recv, local, folds = refs
            acc_ref = o_ref
            def mask_rows(i, carry):
                at = pl.ds(i * 8, 8)
                x_ref[at] = s_ref[at].astype(jnp.float32) * w_ref[at].astype(jnp.float32)
                return carry

            lax.fori_loop(0, rows // 8, mask_rows, 0)
        band = lax.axis_index("lat")
        lon = lax.axis_index("lon")
        has_south = band > 0
        has_north = band < nlat - 1
        top = band == nlat - 1
        west = lax.rem(lon + nlon - 1, nlon)
        east = lax.rem(lon + 1, nlon)
        fold_dst = gf if fold_back else pad
        fold_row = 6 if fold_back else rows + 3
        hi = pl.ds(rows - 3, 3)
        lo = pl.ds(0, 3)
        allr = pl.ds(0, rows)
        c_lo, c_hi, c_all = pl.ds(0, 3), pl.ds(cols - 3, 3), pl.ds(0, cols)
        d_w, d_mid, d_e = pl.ds(0, 3), pl.ds(3, cols), pl.ds(cols + 3, 3)
        messages = [
            (x_ref.at[hi, c_all], pad.at[pl.ds(0, 3), d_mid], (lon, band + 1), has_north, has_south),
            (x_ref.at[hi, c_hi], pad.at[pl.ds(0, 3), d_w], (east, band + 1), has_north, has_south),
            (x_ref.at[hi, c_lo], pad.at[pl.ds(0, 3), d_e], (west, band + 1), has_north, has_south),
            (x_ref.at[lo, c_all], pad.at[pl.ds(rows + 3, 3), d_mid], (lon, band - 1), has_south, has_north),
            (x_ref.at[lo, c_hi], pad.at[pl.ds(rows + 3, 3), d_w], (east, band - 1), has_south, has_north),
            (x_ref.at[lo, c_lo], pad.at[pl.ds(rows + 3, 3), d_e], (west, band - 1), has_south, has_north),
            (x_ref.at[allr, c_hi], pad.at[pl.ds(3, rows), d_w], (east, band), None, None),
            (x_ref.at[allr, c_lo], pad.at[pl.ds(3, rows), d_e], (west, band), None, None),
            (x_ref.at[hi, c_all], stage.at[:, d_mid], (nlon - 1 - lon, band), top, top),
            (x_ref.at[hi, c_lo], stage.at[:, d_e], (lax.rem(2 * nlon - lon, nlon), band), top, top),
            (x_ref.at[hi, c_hi], stage.at[:, d_w], (lax.rem(2 * nlon - 2 - lon, nlon), band), top, top),
        ]
        sources = [
            (lon, band - 1), (west, band - 1), (east, band - 1),
            (lon, band + 1), (west, band + 1), (east, band + 1),
            (west, band), (east, band),
        ]
        for i in (9, 10):
            src, dst, target, _, _ = messages[i]
            apart = jnp.logical_and(top, target[0] != lon)
            messages[i] = (src, dst, target, apart, apart)
        sources += [messages[8][2], messages[9][2], messages[10][2]]
        own = [
            (pltpu.make_async_copy(messages[i][0], messages[i][1], folds.at[j]),
             jnp.logical_and(top, messages[i][2][0] == lon))
            for j, i in enumerate((9, 10))
        ]
        for copy, cond in own:
            pl.when(cond)(copy.start)

        interior = pltpu.make_async_copy(x_ref, pad.at[pl.ds(3, rows), pl.ds(3, cols)], local)
        interior.start()

        @pl.when(band == 0)
        def _():
            pad[pl.ds(0, 3)] = jnp.zeros((3, cols + 6, chans), jnp.float32)

        if not north_fold:
            @pl.when(top)
            def _():
                pad[pl.ds(rows + 3, 3)] = jnp.zeros((3, cols + 6, chans), jnp.float32)

        if fold_back:
            gf[pl.ds(0, 6)] = jnp.zeros((6, cols + 6, chans), jnp.float32)

            @pl.when(jnp.logical_not(top))
            def _():
                gf[pl.ds(6, 3)] = jnp.zeros((3, cols + 6, chans), jnp.float32)

        barrier = pltpu.get_barrier_semaphore()

        def when(cond, fn):
            if cond is None:
                fn()
            else:
                pl.when(cond)(fn)

        for (src, dst, target, s_cond, r_cond), source in zip(messages, sources):
            def greet_target(target=target):
                pl.semaphore_signal(barrier, 1, device_id=target, device_id_type=MESH)

            def greet_source(source=source):
                pl.semaphore_signal(barrier, 1, device_id=source, device_id_type=MESH)

            when(s_cond, greet_target)
            when(r_cond, greet_source)
        for row_tap in range(7):
            for col_tap in range(7):
                a, b = (6 - row_tap, 6 - col_tap) if fold_back else (row_tap, col_tap)
                k_ref[row_tap * 7 + col_tap] = kw_ref[a, pl.ds(b, 1), :].astype(jnp.float32)
        if fold_back:
            bias_row = jnp.zeros((1, chans), jnp.float32)
        else:
            bias_row = b_ref[...]

        interior.wait()
        inner_tiles = tuple(range(8, cols - 8, 8))
        correlate_into(pad, k_ref, bias_row, acc_ref, 3, rows - 6, inner_tiles)
        correlate_into(pad, k_ref, bias_row, acc_ref, 3, rows - 6, (0,), col_taps=(3, 4, 5, 6))
        correlate_into(pad, k_ref, bias_row, acc_ref, 3, rows - 6, (cols - 8,), col_taps=(0, 1, 2, 3))

        edge = has_north.astype(jnp.int32) + has_south.astype(jnp.int32)
        folded = top.astype(jnp.int32) + sum(messages[i][3].astype(jnp.int32) for i in (9, 10))
        expected = 2 * (3 * edge + 2 + folded)
        pl.semaphore_wait(barrier, expected)

        copies = []
        for i, (src, dst, target, s_cond, r_cond) in enumerate(messages):
            copy = pltpu.make_async_remote_copy(
                src_ref=src,
                dst_ref=dst,
                send_sem=send.at[i],
                recv_sem=recv.at[i],
                device_id=target,
                device_id_type=MESH,
            )
            copies.append(copy)
            when(s_cond, copy.start)
        for copy, (src, dst, target, s_cond, r_cond) in zip(copies, messages):
            when(s_cond, copy.wait_send)
            when(r_cond, copy.wait_recv)
        for copy, cond in own:
            pl.when(cond)(copy.wait)

        @pl.when(top)
        def _():
            for t in range(3):
                for j in range(cols + 6):
                    fold_dst[fold_row + t, pl.ds(j, 1), :] = stage[2 - t, pl.ds(cols + 5 - j, 1), :]

        all_tiles = tuple(range(0, cols, 8))
        correlate_into(pad, k_ref, bias_row, acc_ref, 3, rows - 6, (0,), col_taps=(0, 1, 2),
                       accumulate=True)
        correlate_into(pad, k_ref, bias_row, acc_ref, 3, rows - 6, (cols - 8,), col_taps=(4, 5, 6),
                       accumulate=True)
        correlate_into(pad, k_ref, bias_row, acc_ref, 0, 3, all_tiles)
        correlate_into(pad, k_ref, bias_row, acc_ref, rows - 3, 3, all_tiles)
        if fold_back:
            extra = jnp.zeros((3, cols, chans), jnp.float32)
            for row_tap in range(7):
                for col_tap in range(7):
                    window = gf[pl.ds(row_tap, 3), pl.ds(col_tap, cols), :]
                    tap = kw_ref[row_tap, pl.ds(col_tap, 1), :].astype(jnp.float32)
                    extra = extra + tap * window
            acc_ref[pl.ds(rows - 3, 3)] = acc_ref[pl.ds(rows - 3, 3)] + extra
            step = 8 if rows % 8 == 0 else rows

            def finish(i, carry):
                at = pl.ds(i * step, step)
                total = t_ref[at].astype(jnp.float32) + acc_ref[at]
                o_ref[at] = (m_ref[at].astype(jnp.float32) * total).astype(o_ref.dtype)
                return carry

            lax.fori_loop(0, rows // step, finish, 0)

    if fold_back:
        cotangent, keep = tail
        operands = (block, kernel, cotangent, keep)
    else:
        operands = (block, mask, kernel, bias.reshape(1, chans))
    return pl.pallas_call(
        run,
        out_shape=jax.ShapeDtypeStruct(
            (rows, cols, chans), jnp.bfloat16 if fold_back else jnp.float32
        ),
        in_specs=[pl.BlockSpec(memory_space=pltpu.VMEM)] * len(operands),
        out_specs=pl.BlockSpec(memory_space=pltpu.VMEM),
        scratch_shapes=[
            pltpu.VMEM((rows + 6, cols + 6, chans), jnp.float32),
            pltpu.VMEM((9, cols + 6, chans), jnp.float32),
            pltpu.VMEM((49, 1, chans), jnp.float32),
            pltpu.VMEM((rows, cols, chans) if fold_back else (8, 128), jnp.float32),
            pltpu.VMEM((3, cols + 6, chans), jnp.float32),
            pltpu.VMEM((8, 128) if fold_back else (rows, cols, chans), jnp.float32),
            pltpu.SemaphoreType.DMA((11,)),
            pltpu.SemaphoreType.DMA((11,)),
            pltpu.SemaphoreType.DMA,
            pltpu.SemaphoreType.DMA((2,)),
        ],
        compiler_params=pltpu.CompilerParams(collective_id=collective, has_side_effects=True),
    )(*operands)


def gelu_value(values):
    return 0.5 * values * (1.0 + lax.erf(values * 0.7071067811865476))


def gelu_slope(values):
    cumulative = 0.5 * (1.0 + lax.erf(values * 0.7071067811865476))
    return cumulative + values * jnp.exp(-0.5 * values * values) * 0.3989422804014327


def pointwise(
    conv_out,
    ocean_state,
    keep_mask,
    cotangent,
    norm_gain,
    norm_bias,
    w_expand,
    b_expand,
    w_reduce,
    b_reduce,
    layer_scale,
    tile=40,
):
    band_rows, band_cols, chans = conv_out.shape
    cells = tile * band_cols
    hidden_size = w_expand.shape[1]
    tile = tile if band_rows % tile == 0 else band_rows
    cells = tile * band_cols
    contract_last = (((1,), (1,)), ((), ()))

    def run(c_ref, s_ref, m_ref, t_ref, g_ref, nb_ref, we_ref, be_ref, wr_ref, br_ref, ls_ref, r_ref, o_ref):
        flat = lambda ref: ref[...].reshape(cells, chans)
        conv = flat(c_ref)
        keep = flat(m_ref).astype(jnp.float32)
        gain = g_ref[...]
        scale = ls_ref[...]
        row_mean = jnp.mean(conv, axis=-1, keepdims=True)
        centered = conv - row_mean
        inv_std = lax.rsqrt(jnp.mean(centered * centered, axis=-1, keepdims=True) + 1e-06)
        normal_hat = centered * inv_std
        normed = (normal_hat * gain + nb_ref[...]).astype(jnp.bfloat16)
        hidden = jnp.dot(normed, we_ref[...], preferred_element_type=jnp.float32) + be_ref[...]
        erf_term = lax.erf(hidden * 0.7071067811865476)
        activated = (0.5 * hidden * (1.0 + erf_term)).astype(jnp.bfloat16)
        projected = jnp.dot(activated, wr_ref[...], preferred_element_type=jnp.float32) + br_ref[...]
        result = keep * (flat(s_ref).astype(jnp.float32) + scale * projected)
        r_ref[...] = result.astype(r_ref.dtype).reshape(tile, band_cols, chans)
        grad_out = (keep * scale * flat(t_ref).astype(jnp.float32)).astype(jnp.bfloat16)
        grad_act = lax.dot_general(
            grad_out, wr_ref[...], contract_last, preferred_element_type=jnp.float32
        )
        slope = 0.5 * (1.0 + erf_term) + hidden * jnp.exp(-0.5 * hidden * hidden) * 0.3989422804014327
        grad_hidden = (grad_act * slope).astype(jnp.bfloat16)
        grad_normed = lax.dot_general(
            grad_hidden, we_ref[...], contract_last, preferred_element_type=jnp.float32
        )
        grad_scaled = grad_normed * gain
        conv_grad = inv_std * (
            grad_scaled
            - jnp.mean(grad_scaled, axis=-1, keepdims=True)
            - normal_hat * jnp.mean(grad_scaled * normal_hat, axis=-1, keepdims=True)
        )
        o_ref[...] = conv_grad.reshape(tile, band_cols, chans)

    rows = lambda width: pl.BlockSpec((tile, band_cols, width), lambda i: (i, 0, 0))
    whole = lambda shape: pl.BlockSpec(shape, lambda i: (0, 0))
    vec = lambda v: v.reshape(1, -1)
    return pl.pallas_call(
        run,
        grid=(band_rows // tile,),
        out_shape=(
            jax.ShapeDtypeStruct(conv_out.shape, jnp.bfloat16),
            jax.ShapeDtypeStruct(conv_out.shape, jnp.float32),
        ),
        in_specs=[
            rows(chans), rows(chans), rows(chans), rows(chans),
            whole((1, chans)), whole((1, chans)),
            whole((chans, hidden_size)), whole((1, hidden_size)),
            whole((hidden_size, chans)), whole((1, chans)), whole((1, chans)),
        ],
        out_specs=(rows(chans), rows(chans)),
    )(
        conv_out, ocean_state, keep_mask, cotangent, vec(norm_gain), vec(norm_bias),
        w_expand, vec(b_expand), w_reduce, vec(b_reduce), vec(layer_scale),
    )


def body(
    ocean_state,
    land_sea,
    kernel,
    conv_bias,
    norm_gain,
    norm_bias,
    w_expand,
    b_expand,
    w_reduce,
    b_reduce,
    layer_scale,
    cotangent,
):
    band_rows, band_cols, channels = ocean_state.shape
    keep_mask = land_sea.astype(jnp.float32)[:, :, None]
    keep_wide = jnp.broadcast_to(keep_mask, ocean_state.shape).astype(jnp.bfloat16)
    conv_out = halo_correlate(ocean_state, kernel, conv_bias, True, 0, mask=keep_wide)
    result, conv_grad = pointwise(
        conv_out,
        ocean_state,
        keep_wide,
        cotangent,
        norm_gain,
        norm_bias,
        w_expand,
        b_expand,
        w_reduce,
        b_reduce,
        layer_scale,
    )

    state_grad = halo_correlate(
        conv_grad, kernel, None, False, 1, (cotangent, keep_wide)
    )
    return (result, state_grad)


def solution(mesh):
    placed = (
        P("lat", "lon", None),
        P("lat", "lon"),
        P(),
        P(),
        P(),
        P(),
        P(),
        P(),
        P(),
        P(),
        P(),
        P("lat", "lon", None),
    )
    return jax.shard_map(
        body,
        mesh=mesh,
        in_specs=placed,
        out_specs=(P("lat", "lon", None), P("lat", "lon", None)),
        check_vma=False,
    )
```

```python
import jax
import jax.numpy as jnp
from jax import lax
from jax.sharding import PartitionSpec as P
from jax.experimental import pallas as pl
from jax.experimental.pallas import tpu as pltpu


MESH = pl.DeviceIdType.MESH


def correlate_into(src, taps, bias, o_ref, first_row, count, col_tiles, block=32,
                   col_taps=tuple(range(7)), accumulate=False):
    chans = o_ref.shape[-1]
    block = min(block, count)
    steps, left = divmod(count, block)

    def one(r0, size):
        for c0 in col_tiles:
            at = (pl.ds(r0, size), pl.ds(c0, 8), slice(None))
            acc = o_ref[at] if accumulate else jnp.broadcast_to(bias, (size, 8, chans))
            for col_tap in col_taps:
                window = src[pl.ds(r0, size + 6), pl.ds(c0 + col_tap, 8), :]
                for row_tap in range(7):
                    acc = acc + taps[row_tap * 7 + col_tap] * window[row_tap : row_tap + size]
            o_ref[at] = acc

    def step(i, carry):
        one(first_row + i * block, block)
        return carry

    lax.fori_loop(0, steps, step, 0)
    if left:
        one(first_row + steps * block, left)


def halo_correlate(block, kernel, bias, north_fold, collective, tail=None, mask=None):
    rows, cols, chans = block.shape
    nlat, nlon = lax.axis_size("lat"), lax.axis_size("lon")
    fold_back = tail is not None

    def run(*refs):
        if fold_back:
            x_ref, kw_ref, t_ref, m_ref, o_ref, pad, gf, k_ref, acc_ref, stage, _, send, recv, local, folds = refs
        else:
            s_ref, w_ref, kw_ref, b_ref, o_ref, pad, gf, k_ref, acc_ref, stage, x_ref, send, recv, local, folds = refs
            acc_ref = o_ref
            def mask_rows(i, carry):
                at = pl.ds(i * 8, 8)
                x_ref[at] = s_ref[at].astype(jnp.float32) * w_ref[at].astype(jnp.float32)
                return carry

            lax.fori_loop(0, rows // 8, mask_rows, 0)
        band = lax.axis_index("lat")
        lon = lax.axis_index("lon")
        has_south = band > 0
        has_north = band < nlat - 1
        top = band == nlat - 1
        west = lax.rem(lon + nlon - 1, nlon)
        east = lax.rem(lon + 1, nlon)
        fold_dst = gf if fold_back else pad
        fold_row = 6 if fold_back else rows + 3
        hi = pl.ds(rows - 3, 3)
        lo = pl.ds(0, 3)
        allr = pl.ds(0, rows)
        c_lo, c_hi, c_all = pl.ds(0, 3), pl.ds(cols - 3, 3), pl.ds(0, cols)
        d_w, d_mid, d_e = pl.ds(0, 3), pl.ds(3, cols), pl.ds(cols + 3, 3)
        messages = [
            (x_ref.at[hi, c_all], pad.at[pl.ds(0, 3), d_mid], (lon, band + 1), has_north, has_south),
            (x_ref.at[hi, c_hi], pad.at[pl.ds(0, 3), d_w], (east, band + 1), has_north, has_south),
            (x_ref.at[hi, c_lo], pad.at[pl.ds(0, 3), d_e], (west, band + 1), has_north, has_south),
            (x_ref.at[lo, c_all], pad.at[pl.ds(rows + 3, 3), d_mid], (lon, band - 1), has_south, has_north),
            (x_ref.at[lo, c_hi], pad.at[pl.ds(rows + 3, 3), d_w], (east, band - 1), has_south, has_north),
            (x_ref.at[lo, c_lo], pad.at[pl.ds(rows + 3, 3), d_e], (west, band - 1), has_south, has_north),
            (x_ref.at[allr, c_hi], pad.at[pl.ds(3, rows), d_w], (east, band), None, None),
            (x_ref.at[allr, c_lo], pad.at[pl.ds(3, rows), d_e], (west, band), None, None),
            (x_ref.at[hi, c_all], stage.at[:, d_mid], (nlon - 1 - lon, band), top, top),
            (x_ref.at[hi, c_lo], stage.at[:, d_e], (lax.rem(2 * nlon - lon, nlon), band), top, top),
            (x_ref.at[hi, c_hi], stage.at[:, d_w], (lax.rem(2 * nlon - 2 - lon, nlon), band), top, top),
        ]
        sources = [
            (lon, band - 1), (west, band - 1), (east, band - 1),
            (lon, band + 1), (west, band + 1), (east, band + 1),
            (west, band), (east, band),
        ]
        for i in (9, 10):
            src, dst, target, _, _ = messages[i]
            apart = jnp.logical_and(top, target[0] != lon)
            messages[i] = (src, dst, target, apart, apart)
        sources += [messages[8][2], messages[9][2], messages[10][2]]
        own = [
            (pltpu.make_async_copy(messages[i][0], messages[i][1], folds.at[j]),
             jnp.logical_and(top, messages[i][2][0] == lon))
            for j, i in enumerate((9, 10))
        ]
        for copy, cond in own:
            pl.when(cond)(copy.start)

        interior = pltpu.make_async_copy(x_ref, pad.at[pl.ds(3, rows), pl.ds(3, cols)], local)
        interior.start()

        @pl.when(band == 0)
        def _():
            pad[pl.ds(0, 3)] = jnp.zeros((3, cols + 6, chans), jnp.float32)

        if not north_fold:
            @pl.when(top)
            def _():
                pad[pl.ds(rows + 3, 3)] = jnp.zeros((3, cols + 6, chans), jnp.float32)

        if fold_back:
            gf[pl.ds(0, 6)] = jnp.zeros((6, cols + 6, chans), jnp.float32)

            @pl.when(jnp.logical_not(top))
            def _():
                gf[pl.ds(6, 3)] = jnp.zeros((3, cols + 6, chans), jnp.float32)

        barrier = pltpu.get_barrier_semaphore()

        def when(cond, fn):
            if cond is None:
                fn()
            else:
                pl.when(cond)(fn)

        for (src, dst, target, s_cond, r_cond), source in zip(messages, sources):
            def greet_target(target=target):
                pl.semaphore_signal(barrier, 1, device_id=target, device_id_type=MESH)

            def greet_source(source=source):
                pl.semaphore_signal(barrier, 1, device_id=source, device_id_type=MESH)

            when(s_cond, greet_target)
            when(r_cond, greet_source)
        for row_tap in range(7):
            for col_tap in range(7):
                a, b = (6 - row_tap, 6 - col_tap) if fold_back else (row_tap, col_tap)
                k_ref[row_tap * 7 + col_tap] = kw_ref[a, pl.ds(b, 1), :].astype(jnp.float32)
        if fold_back:
            bias_row = jnp.zeros((1, chans), jnp.float32)
        else:
            bias_row = b_ref[...]

        interior.wait()
        inner_tiles = tuple(range(8, cols - 8, 8))
        correlate_into(pad, k_ref, bias_row, acc_ref, 3, rows - 6, inner_tiles)
        correlate_into(pad, k_ref, bias_row, acc_ref, 3, rows - 6, (0,), col_taps=(3, 4, 5, 6))
        correlate_into(pad, k_ref, bias_row, acc_ref, 3, rows - 6, (cols - 8,), col_taps=(0, 1, 2, 3))

        edge = has_north.astype(jnp.int32) + has_south.astype(jnp.int32)
        folded = top.astype(jnp.int32) + sum(messages[i][3].astype(jnp.int32) for i in (9, 10))
        expected = 2 * (3 * edge + 2 + folded)
        pl.semaphore_wait(barrier, expected)

        copies = []
        for i, (src, dst, target, s_cond, r_cond) in enumerate(messages):
            copy = pltpu.make_async_remote_copy(
                src_ref=src,
                dst_ref=dst,
                send_sem=send.at[i],
                recv_sem=recv.at[i],
                device_id=target,
                device_id_type=MESH,
            )
            copies.append(copy)
            when(s_cond, copy.start)
        for copy, (src, dst, target, s_cond, r_cond) in zip(copies, messages):
            when(s_cond, copy.wait_send)
            when(r_cond, copy.wait_recv)
        for copy, cond in own:
            pl.when(cond)(copy.wait)

        @pl.when(top)
        def _():
            for t in range(3):
                for j in range(cols + 6):
                    fold_dst[fold_row + t, pl.ds(j, 1), :] = stage[2 - t, pl.ds(cols + 5 - j, 1), :]

        all_tiles = tuple(range(0, cols, 8))
        correlate_into(pad, k_ref, bias_row, acc_ref, 3, rows - 6, (0,), col_taps=(0, 1, 2),
                       accumulate=True)
        correlate_into(pad, k_ref, bias_row, acc_ref, 3, rows - 6, (cols - 8,), col_taps=(4, 5, 6),
                       accumulate=True)
        correlate_into(pad, k_ref, bias_row, acc_ref, 0, 3, all_tiles)
        correlate_into(pad, k_ref, bias_row, acc_ref, rows - 3, 3, all_tiles)
        if fold_back:
            extra = jnp.zeros((3, cols, chans), jnp.float32)
            for row_tap in range(7):
                for col_tap in range(7):
                    window = gf[pl.ds(row_tap, 3), pl.ds(col_tap, cols), :]
                    tap = kw_ref[row_tap, pl.ds(col_tap, 1), :].astype(jnp.float32)
                    extra = extra + tap * window
            acc_ref[pl.ds(rows - 3, 3)] = acc_ref[pl.ds(rows - 3, 3)] + extra
            step = 8 if rows % 8 == 0 else rows

            def finish(i, carry):
                at = pl.ds(i * step, step)
                total = t_ref[at].astype(jnp.float32) + acc_ref[at]
                o_ref[at] = (m_ref[at].astype(jnp.float32) * total).astype(o_ref.dtype)
                return carry

            lax.fori_loop(0, rows // step, finish, 0)

    if fold_back:
        cotangent, keep = tail
        operands = (block, kernel, cotangent, keep)
    else:
        operands = (block, mask, kernel, bias.reshape(1, chans))
    return pl.pallas_call(
        run,
        out_shape=jax.ShapeDtypeStruct(
            (rows, cols, chans), jnp.bfloat16 if fold_back else jnp.float32
        ),
        in_specs=[pl.BlockSpec(memory_space=pltpu.VMEM)] * len(operands),
        out_specs=pl.BlockSpec(memory_space=pltpu.VMEM),
        scratch_shapes=[
            pltpu.VMEM((rows + 6, cols + 6, chans), jnp.float32),
            pltpu.VMEM((9, cols + 6, chans), jnp.float32),
            pltpu.VMEM((49, 1, chans), jnp.float32),
            pltpu.VMEM((rows, cols, chans) if fold_back else (8, 128), jnp.float32),
            pltpu.VMEM((3, cols + 6, chans), jnp.float32),
            pltpu.VMEM((8, 128) if fold_back else (rows, cols, chans), jnp.float32),
            pltpu.SemaphoreType.DMA((11,)),
            pltpu.SemaphoreType.DMA((11,)),
            pltpu.SemaphoreType.DMA,
            pltpu.SemaphoreType.DMA((2,)),
        ],
        compiler_params=pltpu.CompilerParams(collective_id=collective, has_side_effects=True),
    )(*operands)


def gelu_value(values):
    return 0.5 * values * (1.0 + lax.erf(values * 0.7071067811865476))


def gelu_slope(values):
    cumulative = 0.5 * (1.0 + lax.erf(values * 0.7071067811865476))
    return cumulative + values * jnp.exp(-0.5 * values * values) * 0.3989422804014327


def pointwise(
    conv_out,
    ocean_state,
    keep_mask,
    cotangent,
    norm_gain,
    norm_bias,
    w_expand,
    b_expand,
    w_reduce,
    b_reduce,
    layer_scale,
    tile=40,
):
    band_rows, band_cols, chans = conv_out.shape
    cells = tile * band_cols
    hidden_size = w_expand.shape[1]
    tile = tile if band_rows % tile == 0 else band_rows
    cells = tile * band_cols
    contract_last = (((1,), (1,)), ((), ()))

    def run(c_ref, s_ref, m_ref, t_ref, g_ref, nb_ref, we_ref, be_ref, wr_ref, br_ref, ls_ref, r_ref, o_ref):
        flat = lambda ref: ref[...].reshape(cells, chans)
        conv = flat(c_ref)
        keep = flat(m_ref).astype(jnp.float32)
        gain = g_ref[...]
        scale = ls_ref[...]
        row_mean = jnp.mean(conv, axis=-1, keepdims=True)
        centered = conv - row_mean
        inv_std = lax.rsqrt(jnp.mean(centered * centered, axis=-1, keepdims=True) + 1e-06)
        normal_hat = centered * inv_std
        normed = (normal_hat * gain + nb_ref[...]).astype(jnp.bfloat16)
        hidden = jnp.dot(normed, we_ref[...], preferred_element_type=jnp.float32) + be_ref[...]
        erf_term = lax.erf(hidden * 0.7071067811865476)
        activated = (0.5 * hidden * (1.0 + erf_term)).astype(jnp.bfloat16)
        projected = jnp.dot(activated, wr_ref[...], preferred_element_type=jnp.float32) + br_ref[...]
        result = keep * (flat(s_ref).astype(jnp.float32) + scale * projected)
        r_ref[...] = result.astype(r_ref.dtype).reshape(tile, band_cols, chans)
        grad_out = (keep * scale * flat(t_ref).astype(jnp.float32)).astype(jnp.bfloat16)
        grad_act = lax.dot_general(
            grad_out, wr_ref[...], contract_last, preferred_element_type=jnp.float32
        )
        slope = 0.5 * (1.0 + erf_term) + hidden * jnp.exp(-0.5 * hidden * hidden) * 0.3989422804014327
        grad_hidden = (grad_act * slope).astype(jnp.bfloat16)
        grad_normed = lax.dot_general(
            grad_hidden, we_ref[...], contract_last, preferred_element_type=jnp.float32
        )
        grad_scaled = grad_normed * gain
        conv_grad = inv_std * (
            grad_scaled
            - jnp.mean(grad_scaled, axis=-1, keepdims=True)
            - normal_hat * jnp.mean(grad_scaled * normal_hat, axis=-1, keepdims=True)
        )
        o_ref[...] = conv_grad.reshape(tile, band_cols, chans)

    rows = lambda width: pl.BlockSpec((tile, band_cols, width), lambda i: (i, 0, 0))
    whole = lambda shape: pl.BlockSpec(shape, lambda i: (0, 0))
    vec = lambda v: v.reshape(1, -1)
    return pl.pallas_call(
        run,
        grid=(band_rows // tile,),
        out_shape=(
            jax.ShapeDtypeStruct(conv_out.shape, jnp.bfloat16),
            jax.ShapeDtypeStruct(conv_out.shape, jnp.float32),
        ),
        in_specs=[
            rows(chans), rows(chans), rows(chans), rows(chans),
            whole((1, chans)), whole((1, chans)),
            whole((chans, hidden_size)), whole((1, hidden_size)),
            whole((hidden_size, chans)), whole((1, chans)), whole((1, chans)),
        ],
        out_specs=(rows(chans), rows(chans)),
    )(
        conv_out, ocean_state, keep_mask, cotangent, vec(norm_gain), vec(norm_bias),
        w_expand, vec(b_expand), w_reduce, vec(b_reduce), vec(layer_scale),
    )


def body(
    ocean_state,
    land_sea,
    kernel,
    conv_bias,
    norm_gain,
    norm_bias,
    w_expand,
    b_expand,
    w_reduce,
    b_reduce,
    layer_scale,
    cotangent,
):
    band_rows, band_cols, channels = ocean_state.shape
    keep_mask = land_sea.astype(jnp.float32)[:, :, None]
    keep_wide = jnp.broadcast_to(keep_mask, ocean_state.shape).astype(jnp.bfloat16)
    conv_out = halo_correlate(ocean_state, kernel, conv_bias, True, 0, mask=keep_wide)
    result, conv_grad = pointwise(
        conv_out,
        ocean_state,
        keep_wide,
        cotangent,
        norm_gain,
        norm_bias,
        w_expand,
        b_expand,
        w_reduce,
        b_reduce,
        layer_scale,
    )

    state_grad = halo_correlate(
        conv_grad, kernel, None, False, 1, (cotangent, keep_wide)
    )
    return (result, state_grad)


def solution(mesh):
    placed = (
        P("lat", "lon", None),
        P("lat", "lon"),
        P(),
        P(),
        P(),
        P(),
        P(),
        P(),
        P(),
        P(),
        P(),
        P("lat", "lon", None),
    )
    return jax.shard_map(
        body,
        mesh=mesh,
        in_specs=placed,
        out_specs=(P("lat", "lon", None), P("lat", "lon", None)),
        check_vma=False,
    )
```
